32 devices in a mesh: dp: 4 (over x, core), group: 4 (over z), tensor: 2 (over y).
Axes of the slice: x: 2, y: 2, z: 4, core: 2. Of those that a mesh axis runs over, the one named last changes fastest.
Arguments:
- residual_in: bfloat16 [32, 1024, 767], P(('dp', 'group'), 'tensor'), may hold values from -6 to 6
- piece_ids: int32 [32, 1024], P(('dp', 'group')), may hold values from -1 to 3, as said below
- norm_gains: bfloat16 [2, 768], replicated, may hold values from 0.25 to 1.75
- qkv_weight: bfloat16 [3, 768, 768], P(None, None, 'tensor'), may hold values from -0.21875 to 0.21875
- qv_bias: bfloat16 [2, 768], P(None, 'tensor'), may hold values from -3 to 3
- out_weight: bfloat16 [768, 767], P('tensor'), may hold values from -0.875 to 0.875
- fc_weight: bfloat16 [768, 3072], P(None, 'tensor'), may hold values from -0.21875 to 0.21875
- fc_bias: bfloat16 [3072], P('tensor'), may hold values from -3 to 3
- proj_weight: bfloat16 [3072, 767], P('tensor'), may hold values from -0.109375 to 0.109375
- out_biases: bfloat16 [2, 767], replicated, may hold values from -2 to 2
- cotangent: bfloat16 [32, 1024, 767], P(('dp', 'group'), 'tensor'), may hold values from -6 to 6
Outputs:
- block_out: bfloat16 [32, 1024, 767], P(('dp', 'group'), 'tensor')
- grad_input: bfloat16 [32, 1024, 767], P(('dp', 'group'), 'tensor')
- grad_gains: float32 [2, 768], replicated
- grad_qkv: float32 [3, 768, 768], P(None, 'dp', 'tensor')
- grad_qv_bias: float32 [2, 768], P(None, ('tensor', 'dp'))
- grad_out_weight: float32 [768, 767], P(('tensor', 'dp'))
- grad_fc_weight: float32 [768, 3072], P('dp', 'tensor')
- grad_fc_bias: float32 [3072], P(('tensor', 'dp'))
- grad_proj_weight: float32 [3072, 767], P(('tensor', 'dp'))
- grad_out_biases: float32 [2, 767], replicated
The draws below stay inside these ranges and needn't reach their ends.
Inputs may be any that keep to these rules, and one draw needn't show every extreme that they name: `piece_ids`: each aligned block of 256 positions of a sequence carries one id: -1 (text) or the block's own number (a picture piece). The first block of every sequence is text and the last one a picture piece.
All inputs are finite; a program needn't handle non-finite values.
Results may differ from the reference program's by a relative error of at most 0.02.
Values may be sent and summed in bfloat16 or wider, within the bound.
No kernel may reach another device: no remote copies, remote signals or barrier semaphores. Data moves between devices by JAX's collectives and lax.ppermute only.
A program may use at most 192 MiB of HBM per device.

```python
import jax
import jax.numpy as jnp
from jax import lax

D = 768
HEADS = 12
HD = 64
FF = 3072
DC = 767
LEN = 1024
PIECE = 256
SEQS = 32


def draw_piece_ids(key, part):
    block_count = LEN // PIECE
    picked = jax.random.randint(key, (SEQS, block_count), 0, 2)
    column = jnp.arange(block_count, dtype=jnp.int32)[None, :]
    picked = jnp.where(column == 0, 0, jnp.where(column == block_count - 1, 1, picked))
    labels = jnp.where(picked == 1, column, -1).astype(jnp.int32)
    return jnp.repeat(labels, PIECE, axis=1)


def shard_levels(stream_key, extent, pieces, least, high):
    level = 1.0
    for axis_at, parts in pieces:
        draws = jax.random.uniform(jax.random.fold_in(jax.random.fold_in(stream_key, 6), axis_at), (parts,), jnp.float32, least / len(pieces), high / len(pieces))
        level = level * jnp.repeat(jnp.exp(draws), extent[axis_at] // parts).reshape((-1,) + (1,) * (len(extent) - 1 - axis_at))
    return level


def scatter_about(stream_key, dims, deviation, most, cuts=(), kind=jnp.bfloat16):
    loudness = shard_levels(stream_key, dims, cuts, -0.22, 0.18) if cuts else 1.0
    drawn = jax.random.normal(stream_key, dims, jnp.float32) * deviation * loudness
    return jnp.minimum(jnp.maximum(drawn, -most), most).astype(kind)


def setup_inputs(seed: int = 0) -> dict:
    seeds = jax.random.split(jax.random.key(seed), 12)
    return {
        "residual_in": scatter_about(seeds[0], (SEQS, LEN, DC), 1.0, 6.0, ((0, 16), (1, 2))),
        "piece_ids": draw_piece_ids(jax.random.fold_in(seeds[11], 71), 0),
        "norm_gains": jnp.clip(1.0 + 0.15 * jax.random.normal(seeds[2], (2, D), jnp.float32), 0.25, 1.75).astype(jnp.bfloat16),
        "qkv_weight": scatter_about(seeds[3], (3, D, D), D ** -0.5, 0.21875, ((2, 2),)),
        "qv_bias": scatter_about(seeds[4], (2, D), 0.5, 3.0, ((1, 2),)),
        "out_weight": scatter_about(seeds[5], (D, DC), (D // 16) ** -0.5, 0.875, ((0, 2),)),
        "fc_weight": scatter_about(seeds[6], (D, FF), D ** -0.5, 0.21875, ((1, 2),)),
        "fc_bias": scatter_about(seeds[7], (FF,), 0.5, 3.0, ((0, 2),)),
        "proj_weight": scatter_about(seeds[8], (FF, DC), FF ** -0.5, 0.109375, ((0, 2),)),
        "out_biases": scatter_about(seeds[9], (2, DC), 0.3, 2.0),
        "cotangent": scatter_about(seeds[10], (SEQS, LEN, DC), 1.0, 6.0, ((0, 16), (1, 2))),
    }


EPSILON = 1e-05
MASKED = -1e+30
PRECISE = lax.Precision.HIGHEST

@jax.custom_vjp
def low(v):
    return lax.optimization_barrier(v.astype(jnp.bfloat16)).astype(jnp.float32)

@jax.custom_vjp
def low_back(v):
    return v

def low_keep(v):
    return (low(v), None)

def low_pass(kept, grad):
    return (grad,)

def back_keep(v):
    return (v, None)

def back_low(kept, grad):
    return (low(grad),)
low.defvjp(low_keep, low_pass)
low_back.defvjp(back_keep, back_low)

def decompress(compact):
    return jnp.concatenate([compact, -lax.optimization_barrier(jnp.sum(compact, axis=-1, keepdims=True))], axis=-1)

def crms_gain(compact, gain):
    full_rows = decompress(compact)
    factor = lax.rsqrt(lax.optimization_barrier(jnp.mean(full_rows * full_rows, axis=-1, keepdims=True)) + EPSILON)
    return full_rows * factor * gain

def visible_mask(labels, row_start, row_count):
    query_pos = row_start + jnp.arange(row_count)
    key_pos = jnp.arange(labels.shape[0])
    row_labels = labels[row_start:row_start + row_count]
    causal = key_pos[None, :] <= query_pos[:, None]
    inside = (row_labels[:, None] == labels[None, :]) & (row_labels[:, None] >= 0)
    return causal | inside

def sequence_forward(params, compact, labels):
    gains, qkv_weight, qv_bias, out_weight, fc_weight, fc_bias, proj_weight, out_biases = params
    length = compact.shape[0]
    normed_one = low(crms_gain(compact, gains[0]))
    projected = jnp.einsum('td,cde->cte', normed_one, qkv_weight, precision=PRECISE)
    queries = low(low_back(projected[0] + qv_bias[0])).reshape(length, HEADS, HD)
    key_rows = low(low_back(projected[1])).reshape(length, HEADS, HD)
    value_rows = low(low_back(projected[2] + qv_bias[1])).reshape(length, HEADS, HD)
    scores = jnp.einsum('qhd,khd->hqk', queries, key_rows, precision=PRECISE) * HD ** (-0.5)
    scores = low_back(scores)
    scores = jnp.where(visible_mask(labels, 0, length)[None], scores, MASKED)
    probs = jax.nn.softmax(scores, axis=-1)
    attended = jnp.einsum('hqk,khd->qhd', low(probs), value_rows, precision=PRECISE).reshape(length, D)
    attended = low(low_back(attended))
    branch = low_back(jnp.dot(attended, out_weight, precision=PRECISE) + out_biases[0])
    middle = compact + branch
    normed_two = low(crms_gain(middle, gains[1]))
    hidden_pre = low_back(jnp.dot(normed_two, fc_weight, precision=PRECISE) + fc_bias)
    active = low(jax.nn.gelu(hidden_pre, approximate=True))
    mlp_branch = low_back(jnp.dot(active, proj_weight, precision=PRECISE) + out_biases[1])
    return middle + mlp_branch

def reference(residual_in, piece_ids, norm_gains, qkv_weight, qv_bias, out_weight, fc_weight, fc_bias, proj_weight, out_biases, cotangent):
    params = (norm_gains.astype(jnp.float32), qkv_weight.astype(jnp.float32), qv_bias.astype(jnp.float32), out_weight.astype(jnp.float32), fc_weight.astype(jnp.float32), fc_bias.astype(jnp.float32), proj_weight.astype(jnp.float32), out_biases.astype(jnp.float32))
    zeros = jax.tree.map(jnp.zeros_like, params)

    def one_sequence(totals, inputs):
        compact, labels, upstream = inputs
        result, pullback = jax.vjp(lambda weights, rows_in: sequence_forward(weights, rows_in, labels), params, compact.astype(jnp.float32))
        weight_grads, input_grad = pullback(upstream.astype(jnp.float32))
        totals = jax.tree.map(jnp.add, totals, weight_grads)
        return (totals, (result.astype(jnp.bfloat16), input_grad.astype(jnp.bfloat16)))
    totals, (outputs, input_grads) = lax.scan(one_sequence, zeros, (residual_in, piece_ids, cotangent))
    return (outputs, input_grads, totals[0], totals[1], totals[2], totals[3], totals[4], totals[5], totals[6], totals[7])
```

```python
import functools
import jax
import jax.numpy as jnp
from jax import lax
from jax.sharding import PartitionSpec as P
from jax.experimental import pallas as pl
from jax.experimental.pallas import tpu as pltpu

D = 768
HD = 64
EPSILON = 1e-05
MASKED = -1e30
VMEM_CAP = 60 * 1024 * 1024
F32 = jnp.float32
BF16 = jnp.bfloat16


def dot_nn(a, b):
    return lax.dot_general(a, b, (((1,), (0,)), ((), ())), preferred_element_type=F32)


def dot_nt(a, b):
    return lax.dot_general(a, b, (((1,), (1,)), ((), ())), preferred_element_type=F32)


def dot_tn(a, b):
    return lax.dot_general(a, b, (((0,), (0,)), ((), ())), preferred_element_type=F32)


def column_sum(values):
    return jnp.sum(values, axis=0, keepdims=True)


def lane_of(shape):
    return lax.broadcasted_iota(jnp.int32, shape, len(shape) - 1)


def attend_forward_kernel(flags_ref, q_ref, k_ref, v_ref, out_ref, log_ref, *, block):
    length = q_ref.shape[0]
    row = lax.broadcasted_iota(jnp.int32, (block, block), 0)
    col = lax.broadcasted_iota(jnp.int32, (block, block), 1)
    causal = col <= row
    head_lane = lane_of((block, 128)) // HD
    for at in range(length // block):
        rows = pl.ds(at * block, block)
        seen = causal | (flags_ref[at] > 0)
        q_rows = q_ref[rows, :]
        reach = at * block
        parts = []
        for head in range(2):
            q_head = jnp.where(head_lane == head, q_rows, jnp.zeros_like(q_rows))
            near = jnp.where(seen, dot_nt(q_head, k_ref[rows, :]), MASKED)
            top = jnp.max(near, axis=-1, keepdims=True)
            if reach:
                far = dot_nt(q_head, k_ref[pl.ds(0, reach), :])
                top = jnp.maximum(top, jnp.max(far, axis=-1, keepdims=True))
            near = jnp.exp(near - top)
            total = jnp.sum(near, axis=-1, keepdims=True)
            mixed = dot_nn(near.astype(BF16), v_ref[rows, :])
            if reach:
                far = jnp.exp(far - top)
                total = total + jnp.sum(far, axis=-1, keepdims=True)
                mixed = mixed + dot_nn(far.astype(BF16), v_ref[pl.ds(0, reach), :])
            parts.append(mixed / total)
            logs = top + jnp.log(total)
            log_ref[0, pl.ds(head, 1), rows] = jnp.transpose(
                jnp.broadcast_to(logs, (block, 128)))[0:1, :]
        out_ref[rows, :] = jnp.where(head_lane == 0, parts[0], parts[1]).astype(BF16)


def attend_forward(flags, queries, key_rows, value_rows):
    length, width = queries.shape
    pairs = width // 128
    block = length // 4
    tile = pl.BlockSpec((length, 128), lambda h, f: (0, h))
    return pl.pallas_call(
        functools.partial(attend_forward_kernel, block=block),
        grid_spec=pltpu.PrefetchScalarGridSpec(
            num_scalar_prefetch=1, grid=(pairs,),
            in_specs=[tile, tile, tile],
            out_specs=[tile, pl.BlockSpec((1, 8, length), lambda h, f: (h, 0, 0))]),
        out_shape=[jax.ShapeDtypeStruct((length, width), BF16),
                   jax.ShapeDtypeStruct((pairs, 8, length), F32)],
        compiler_params=pltpu.CompilerParams(vmem_limit_bytes=VMEM_CAP),
        name="attend_forward",
    )(flags, queries, key_rows, value_rows)


def attend_backward_kernel(flags_ref, q_ref, k_ref, v_ref, up_ref, log_ref,
                           dq_ref, dk_ref, dv_ref, sum_ref, dk_acc, dv_acc, *, block):
    length = q_ref.shape[0]
    count = length // block
    key_at = lax.broadcasted_iota(jnp.int32, (block, block), 0)
    query_at = lax.broadcasted_iota(jnp.int32, (block, block), 1)
    causal = key_at <= query_at
    head_lane = lane_of((block, 128)) // HD
    full_lane = lane_of((length, 128)) // HD
    dq_sum = jnp.zeros((1, 128), F32)
    for at in reversed(range(count)):
        rows = pl.ds(at * block, block)
        reach = (at + 1) * block
        keys = pl.ds(0, reach)
        seen = causal | (flags_ref[at] > 0)
        dq = None
        for head in range(2):
            q_head = jnp.where(head_lane == head, q_ref[rows, :], jnp.zeros((block, 128), BF16))
            up_head = jnp.where(head_lane == head, up_ref[rows, :], jnp.zeros((block, 128), BF16))
            logs = log_ref[0, pl.ds(head, 1), rows]
            scores = dot_nt(k_ref[keys, :], q_head)
            last = jnp.where(seen, scores[reach - block :], MASKED)
            scores = last if at == 0 else jnp.concatenate([scores[: reach - block], last], 0)
            probs = jnp.exp(scores - logs)
            along = dot_nt(v_ref[keys, :], up_head)
            inner = jnp.sum(probs * along, axis=0, keepdims=True)
            low_grad = (probs * (along - inner)).astype(BF16)
            dv = dot_nn(probs.astype(BF16), up_head)
            dk = dot_nn(low_grad, q_head)
            if at == count - 1 and head == 0:
                dv_acc[keys, :] = dv
                dk_acc[keys, :] = dk
            else:
                dv_acc[keys, :] += dv
                dk_acc[keys, :] += dk
            k_head = jnp.where(full_lane[:reach] == head, k_ref[keys, :], jnp.zeros((reach, 128), BF16))
            part = dot_tn(low_grad, k_head)
            dq = part if dq is None else dq + part
        low_dq = (dq * HD ** (-0.5)).astype(BF16)
        dq_ref[rows, :] = low_dq
        dq_sum = dq_sum + column_sum(low_dq.astype(F32))
    dk_ref[...] = dk_acc[...].astype(BF16)
    low_dv = dv_acc[...].astype(BF16)
    dv_ref[...] = low_dv
    sum_ref[0:1, :] = dq_sum
    sum_ref[1:2, :] = column_sum(low_dv.astype(F32))


def attend_backward(flags, queries, key_rows, value_rows, upstream, log_sums, first, pairs):
    length, width = queries.shape
    block = length // 4
    tile = pl.BlockSpec((length, 128), lambda h, f: (0, h + first))
    out_tile = pl.BlockSpec((length, 128), lambda h, f: (0, h))
    out = jax.ShapeDtypeStruct((length, pairs * 128), BF16)
    return pl.pallas_call(
        functools.partial(attend_backward_kernel, block=block),
        grid_spec=pltpu.PrefetchScalarGridSpec(
            num_scalar_prefetch=1, grid=(pairs,),
            in_specs=[tile, tile, tile, tile,
                      pl.BlockSpec((1, 8, length), lambda h, f: (h + first, 0, 0))],
            out_specs=[out_tile, out_tile, out_tile, pl.BlockSpec((8, 128), lambda h, f: (0, h))],
            scratch_shapes=[pltpu.VMEM((length, 128), F32), pltpu.VMEM((length, 128), F32)]),
        out_shape=[out, out, out, jax.ShapeDtypeStruct((8, pairs * 128), F32)],
        compiler_params=pltpu.CompilerParams(vmem_limit_bytes=VMEM_CAP),
        name="attend_backward",
    )(flags, queries, key_rows, value_rows, upstream, log_sums)


def decompress(compact):
    total = jnp.sum(compact, axis=-1, keepdims=True)
    return jnp.where(lane_of(compact.shape) == D - 1, -total, compact)


def crms_back(normal, factor, gain, grad):
    scaled = gain * grad
    du = factor * (scaled - normal * jnp.mean(scaled * normal, axis=-1, keepdims=True))
    lane = lane_of(du.shape)
    last = jnp.sum(jnp.where(lane == D - 1, du, 0.0), axis=-1, keepdims=True)
    return jnp.where(lane == D - 1, 0.0, du - last)


def crms_normal(compact):
    full = decompress(compact)
    factor = lax.rsqrt(jnp.mean(full * full, axis=-1, keepdims=True) + EPSILON)
    return full * factor, factor


def project_kernel(place_ref, own_ref, other_ref, gain_ref, bias_ref, w_own, w_quarter,
                   normed_ref, q_ref, k_ref, v_ref, weight, sems, *, steps):
    at = pl.program_id(0)
    quarter = D // 4
    half = w_own.shape[2]

    def copies():
        out = [pltpu.make_async_copy(w_own, weight.at[:, :, pl.ds(0, half)], sems.at[0])]
        for rel in range(4):
            place = pl.multiple_of((place_ref[1] ^ rel) * quarter, quarter)
            out.append(pltpu.make_async_copy(
                w_quarter[rel], weight.at[:, pl.ds(place, quarter), pl.ds(half, half)],
                sems.at[rel + 1]))
        return out

    @pl.when(at == 0)
    def _():
        for copy in copies():
            copy.start()

    compact = jnp.where(at < steps // 2, own_ref[...], other_ref[...]).astype(F32)
    normal, _ = crms_normal(compact)
    normed = (normal * gain_ref[...]).astype(BF16)
    normed_ref[...] = normed

    @pl.when(at == 0)
    def _():
        for copy in copies():
            copy.wait()

    q_ref[...] = ((dot_nn(normed, weight[0]) + bias_ref[0:1, :]).astype(BF16).astype(F32)
                  * HD ** (-0.5)).astype(BF16)
    k_ref[...] = dot_nn(normed, weight[1]).astype(BF16)
    v_ref[...] = (dot_nn(normed, weight[2]) + bias_ref[1:2, :]).astype(BF16)


def row_maps(steps):
    half = steps // 2
    own = lambda i, s: (jnp.minimum(i, half - 1), 0)
    other = lambda i, s: (jnp.maximum(i - half, 0), 0)
    whole = lambda i, s: (jnp.where(i < half, s[0] * half + i, (1 - s[0]) * half + i - half), 0)
    return own, other, whole


ANY = pl.BlockSpec(memory_space=pl.ANY)


def project(place, own, other, gain, bias, w_own, w_quarter, steps=4):
    length = own.shape[0] * 2
    block = length // steps
    own_map, other_map, whole_map = row_maps(steps)
    fixed = lambda i, s: (0, 0)
    wide = pl.BlockSpec((block, D), whole_map)
    out = jax.ShapeDtypeStruct((length, D), BF16)

    def body(place_ref, own_ref, other_ref, gain_ref, bias_ref, w_own, a, b, c, d, *rest):
        project_kernel(place_ref, own_ref, other_ref, gain_ref, bias_ref, w_own, (a, b, c, d),
                       *rest, steps=steps)

    return pl.pallas_call(
        body,
        grid_spec=pltpu.PrefetchScalarGridSpec(
            num_scalar_prefetch=1, grid=(steps,),
            in_specs=[pl.BlockSpec((block, D), own_map), pl.BlockSpec((block, D), other_map),
                      pl.BlockSpec((1, D), fixed), pl.BlockSpec((2, D), fixed)] + [ANY] * 5,
            out_specs=[wide] * 4,
            scratch_shapes=[pltpu.VMEM((3, D, D), BF16), pltpu.SemaphoreType.DMA((5,))]),
        out_shape=[out] * 4,
        compiler_params=pltpu.CompilerParams(vmem_limit_bytes=VMEM_CAP),
        name="norm_project",
    )(place, own, other, gain, bias, w_own, *w_quarter)


SQRT_2_PI = 0.7978845608028654


def gelu_pair(v):
    square = v * v
    inner = v * (SQRT_2_PI + (SQRT_2_PI * 0.044715) * square)
    tanh = jnp.tanh(inner)
    cdf = 0.5 + 0.5 * tanh
    slope = SQRT_2_PI + (3 * SQRT_2_PI * 0.044715) * square
    back = cdf + (0.5 * v) * (1.0 - tanh * tanh) * slope
    return v * cdf, back


def middle_kernel(place_ref, att_ref, res_own, res_other, cot_own, cot_other, gain_ref, end_ref,
                  fcb_ref, weights, two_ref, active_ref, hidden_ref, own_out, send_out,
                  mid_ref, branch_ref, upgrad_ref, sums_ref,
                  out_w, fc_w, proj_w, sems, *, steps, chunk):
    at = pl.program_id(0)
    hid = fc_w.shape[1]
    half = hid // 2
    o_own, o_q, f_own, f_q, p_own, p_q = weights

    def copies(which):
        out = []
        if which == 0:
            out.append(pltpu.make_async_copy(o_own, out_w.at[pl.ds(0, D // 2), :], sems.at[0]))
        elif which == 1:
            out.append(pltpu.make_async_copy(f_own, fc_w.at[:, pl.ds(0, half)], sems.at[1]))
        else:
            out.append(pltpu.make_async_copy(p_own, proj_w.at[pl.ds(0, half), :], sems.at[2]))
        for rel in range(4):
            to = place_ref[1] ^ rel
            sem = sems.at[3 + 4 * which + rel]
            if which == 0:
                rows = D // 8
                out.append(pltpu.make_async_copy(
                    o_q[rel], out_w.at[pl.ds(pl.multiple_of(D // 2 + to * rows, rows), rows), :], sem))
            elif which == 1:
                rows = D // 4
                out.append(pltpu.make_async_copy(
                    f_q[rel], fc_w.at[pl.ds(pl.multiple_of(to * rows, rows), rows), pl.ds(half, half)], sem))
            else:
                rows = half // 4
                out.append(pltpu.make_async_copy(
                    p_q[rel], proj_w.at[pl.ds(pl.multiple_of(half + to * rows, rows), rows), :], sem))
        return out

    @pl.when(at == 0)
    def _():
        for which in range(3):
            for copy in copies(which):
                copy.start()
        sums_ref[...] = jnp.zeros_like(sums_ref)
        for copy in copies(0):
            copy.wait()

    mine = at < steps // 2
    compact = jnp.where(mine, res_own[...], res_other[...]).astype(F32)
    cot_low = jnp.where(mine, cot_own[...], cot_other[...])
    middle = compact + dot_nn(att_ref[...], out_w[...]) + end_ref[0:1, :]
    normal, factor = crms_normal(middle)
    gain = gain_ref[...]
    two = (normal * gain).astype(BF16)
    two_ref[...] = two

    @pl.when(at == 0)
    def _():
        for which in (1, 2):
            for copy in copies(which):
                copy.wait()

    mlp = jnp.zeros((two.shape[0], D), F32)
    two_grad = jnp.zeros((two.shape[0], D), F32)
    for start in range(0, hid, chunk):
        cols = pl.ds(start, chunk)
        pre = dot_nn(two, fc_w[:, cols]) + fcb_ref[0:1, cols]
        act, slope = gelu_pair(pre)
        act = act.astype(BF16)
        active_ref[:, cols] = act
        mlp = mlp + dot_nn(act, proj_w[cols, :])
        hidden = (dot_nt(cot_low, proj_w[cols, :]) * slope).astype(BF16)
        hidden_ref[:, cols] = hidden
        sums_ref[3:4, cols] += column_sum(hidden.astype(F32))
        two_grad = two_grad + dot_nt(hidden, fc_w[:, cols])
    block_out = (middle + mlp + end_ref[1:2, :]).astype(BF16)

    @pl.when(mine)
    def _():
        own_out[...] = block_out

    @pl.when(jnp.logical_not(mine))
    def _():
        send_out[...] = block_out

    cot = cot_low.astype(F32)
    mid_grad = cot + crms_back(normal, factor, gain, two_grad)
    mid_ref[...] = mid_grad
    branch = mid_grad.astype(BF16)
    branch_ref[...] = branch
    upgrad_ref[...] = dot_nt(branch, out_w[...]).astype(BF16)
    sums_ref[0:1, 0:D] += column_sum(two_grad * normal)
    sums_ref[1:2, 0:D] += column_sum(branch.astype(F32))
    sums_ref[2:3, 0:D] += column_sum(cot)


def middle_stage(place, att, res_own, res_other, cot_own, cot_other, gain, end_bias, fc_bias, weights,
                 steps=4, chunk=768):
    length = att.shape[0]
    hid = fc_bias.shape[1]
    block = length // steps
    own_map, other_map, whole_map = row_maps(steps)
    fixed = lambda i, s: (0, 0)
    o_own, o_q, f_own, f_q, p_own, p_q = weights
    flat = [o_own, *o_q, f_own, *f_q, p_own, *p_q]
    spec = lambda w, m: pl.BlockSpec((block, w), m)

    def body(place_ref, *refs):
        ins, rest = refs[:8], refs[8:]
        w, rest = rest[:15], rest[15:]
        packed = (w[0], w[1:5], w[5], w[6:10], w[10], w[11:15])
        middle_kernel(place_ref, *ins, packed, *rest, steps=steps, chunk=chunk)

    sd = jax.ShapeDtypeStruct
    return pl.pallas_call(
        body,
        grid_spec=pltpu.PrefetchScalarGridSpec(
            num_scalar_prefetch=1, grid=(steps,),
            in_specs=[spec(D, whole_map), spec(D, own_map), spec(D, other_map), spec(D, own_map),
                      spec(D, other_map), pl.BlockSpec((1, D), fixed), pl.BlockSpec((2, D), fixed),
                      pl.BlockSpec((1, hid), fixed)] + [ANY] * 15,
            out_specs=[spec(D, whole_map), spec(hid, whole_map), spec(hid, whole_map),
                       spec(D, own_map), spec(D, other_map),
                       spec(D, whole_map), spec(D, whole_map), spec(D, whole_map),
                       pl.BlockSpec((8, hid), fixed)],
            scratch_shapes=[pltpu.VMEM((D, D), BF16), pltpu.VMEM((D, hid), BF16),
                            pltpu.VMEM((hid, D), BF16), pltpu.SemaphoreType.DMA((15,))]),
        out_shape=[sd((length, D), BF16), sd((length, hid), BF16), sd((length, hid), BF16),
                   sd((length // 2, D), BF16), sd((length // 2, D), BF16),
                   sd((length, D), F32), sd((length, D), BF16), sd((length, D), BF16),
                   sd((8, hid), F32)],
        compiler_params=pltpu.CompilerParams(vmem_limit_bytes=VMEM_CAP),
        name="middle_stage",
    )(place, att, res_own, res_other, cot_own, cot_other, gain, end_bias, fc_bias, *flat)


def weight_grad_kernel(place_ref, *refs, rows, rights):
    left_ref = refs[0]
    right_refs = refs[1:1 + rights]
    keep_ref, send_ref = refs[1 + rights:]
    flip = (place_ref[1] & 1) == 1
    left = left_ref[...]
    for n, right in enumerate(right_refs):
        both = dot_tn(left, right[...]).astype(BF16)
        low, high = both[:rows], both[rows:]
        if rights == 1:
            keep_ref[0] = jnp.where(flip, high, low)
            send_ref[0] = jnp.where(flip, low, high)
        else:
            keep_ref[0, n] = jnp.where(flip, high, low)
            send_ref[0, n] = jnp.where(flip, low, high)


def weight_grad(place, left, rights, columns, col_at=0, left_cols=None, left_at=0):
    length = left.shape[0]
    span = left_cols or left.shape[1]
    rows = span // 4
    first = left_at * 2
    many = len(rights)
    width = columns
    shape = (2, rows, width) if many == 1 else (2, many, rows, width)
    out_map = (lambda j, s: (j ^ (s[1] >> 1), 0, 0)) if many == 1 else (
        lambda j, s: (j ^ (s[1] >> 1), 0, 0, 0))
    out_spec = pl.BlockSpec((1,) + shape[1:], out_map)
    out = jax.ShapeDtypeStruct(shape, BF16)
    return pl.pallas_call(
        functools.partial(weight_grad_kernel, rows=rows, rights=many),
        grid_spec=pltpu.PrefetchScalarGridSpec(
            num_scalar_prefetch=1, grid=(2,),
            in_specs=[pl.BlockSpec((length, 2 * rows), lambda j, s: (0, first + j))]
            + [pl.BlockSpec((length, width), lambda j, s: (0, col_at)) for _ in rights],
            out_specs=[out_spec, out_spec]),
        out_shape=[out, out],
        compiler_params=pltpu.CompilerParams(vmem_limit_bytes=VMEM_CAP),
        name="weight_grad",
    )(place, left, *rights)


def out_grad_kernel(place_ref, left_ref, right_ref, keep_ref, send_ref, *, rows):
    flip = (place_ref[1] & 1) == 1
    both = dot_tn(left_ref[...], right_ref[...]).astype(BF16)
    for side in range(2):
        for pair in range(2):
            at = (side * 4 + pair * 2) * rows
            low, high = both[at : at + rows], both[at + rows : at + 2 * rows]
            to = pair ^ (place_ref[1] >> 1)
            keep_ref[to, side] = jnp.where(flip, high, low)
            send_ref[to, side] = jnp.where(flip, low, high)


def out_grad(place, left, right):
    length, width = left.shape
    rows = width // 8
    out = jax.ShapeDtypeStruct((2, 2, rows, right.shape[1]), BF16)
    return pl.pallas_call(
        functools.partial(out_grad_kernel, rows=rows),
        grid_spec=pltpu.PrefetchScalarGridSpec(
            num_scalar_prefetch=1, grid=(1,),
            in_specs=[pl.BlockSpec(value.shape, lambda i, s: (0, 0)) for value in (left, right)],
            out_specs=[pl.BlockSpec(out.shape, lambda i, s: (0, 0, 0, 0))] * 2),
        out_shape=[out, out],
        compiler_params=pltpu.CompilerParams(vmem_limit_bytes=VMEM_CAP),
        name="out_grad",
    )(place, left, right)


def input_grad_kernel(place_ref, dq_refs, res_own, res_other, mid_ref, gain_ref, w_own, w_quarter,
                      own_out, send_out, sums_ref, weight, sems, *, steps):
    at = pl.program_id(0)
    quarter = D // 4
    half = w_own.shape[2]

    def copies():
        out = [pltpu.make_async_copy(w_own, weight.at[:, :, pl.ds(0, half)], sems.at[0])]
        for rel in range(4):
            place = pl.multiple_of((place_ref[1] ^ rel) * quarter, quarter)
            out.append(pltpu.make_async_copy(
                w_quarter[rel], weight.at[:, pl.ds(place, quarter), pl.ds(half, half)],
                sems.at[rel + 1]))
        return out

    @pl.when(at == 0)
    def _():
        for copy in copies():
            copy.start()
        sums_ref[...] = jnp.zeros_like(sums_ref)

    mine = at < steps // 2
    compact = jnp.where(mine, res_own[...], res_other[...]).astype(F32)
    normal, factor = crms_normal(compact)
    gain = gain_ref[...]

    @pl.when(at == 0)
    def _():
        for copy in copies():
            copy.wait()

    grad = None
    for n in range(6):
        part = dot_nt(dq_refs[n][...], weight[n % 3, :, pl.ds((n // 3) * half, half)])
        grad = part if grad is None else grad + part
    sums_ref[0:1, :] += column_sum(grad * normal)
    result = (mid_ref[...] + crms_back(normal, factor, gain, grad)).astype(BF16)

    @pl.when(mine)
    def _():
        own_out[...] = result

    @pl.when(jnp.logical_not(mine))
    def _():
        send_out[...] = result


def input_grad(place, head_grads, res_own, res_other, mid, gain, w_own, w_quarter, steps=4):
    length = mid.shape[0]
    block = length // steps
    own_map, other_map, whole_map = row_maps(steps)
    fixed = lambda i, s: (0, 0)
    half = head_grads[0].shape[1]

    def body(place_ref, *refs):
        grads, rest = refs[:6], refs[6:]
        res_own, res_other, mid_ref, gain_ref, w_own, a, b, c, d = rest[:9]
        input_grad_kernel(place_ref, grads, res_own, res_other, mid_ref, gain_ref, w_own,
                          (a, b, c, d), *rest[9:], steps=steps)

    sd = jax.ShapeDtypeStruct
    return pl.pallas_call(
        body,
        grid_spec=pltpu.PrefetchScalarGridSpec(
            num_scalar_prefetch=1, grid=(steps,),
            in_specs=[pl.BlockSpec((block, half), whole_map)] * 6
            + [pl.BlockSpec((block, D), own_map), pl.BlockSpec((block, D), other_map),
               pl.BlockSpec((block, D), whole_map), pl.BlockSpec((1, D), fixed)] + [ANY] * 5,
            out_specs=[pl.BlockSpec((block, D), own_map), pl.BlockSpec((block, D), other_map),
                       pl.BlockSpec((8, D), fixed)],
            scratch_shapes=[pltpu.VMEM((3, D, D), BF16), pltpu.SemaphoreType.DMA((5,))]),
        out_shape=[sd((length // 2, D), BF16), sd((length // 2, D), BF16), sd((8, D), F32)],
        compiler_params=pltpu.CompilerParams(vmem_limit_bytes=VMEM_CAP),
        name="input_grad",
    )(place, *head_grads, res_own, res_other, mid, gain, w_own, *w_quarter)


def swap(value, axis, bit, size):
    return lax.ppermute(value, axis, [(n, n ^ bit) for n in range(size)])


def fetch_other(shard, dim, sizes, quarter_at):
    n_dp, n_tensor = sizes
    rows = shard.shape[dim] // 4
    piece = lax.dynamic_slice_in_dim(shard, quarter_at * rows, rows, dim)
    first = swap(piece, "tensor", 1, n_tensor)
    third = swap(first, "dp", 2, n_dp)
    second = swap(first, "dp", 1, n_dp)
    fourth = swap(third, "dp", 1, n_dp)
    return first, second, third, fourth


def add_low(*values):
    total = values[0].astype(F32)
    for value in values[1:]:
        total = total + value.astype(F32)
    return total.astype(BF16)


def chain_sum(value, size, index):
    if size != 4:
        return lax.psum(value, "group")
    low = value.dtype
    inward = lax.ppermute(value, "group", [(0, 1), (3, 2)])
    part = (value.astype(F32) + inward.astype(F32)).astype(low)
    across = lax.ppermute(part, "group", [(1, 2), (2, 1)])
    total = (part.astype(F32) + across.astype(F32)).astype(low)
    outward = lax.ppermute(total, "group", [(1, 0), (2, 3)])
    return jnp.where((index == 1) | (index == 2), total, outward)


def pick(pair, index):
    return jnp.where(index == 0, pair[0], pair[1])


def reduce_x_first(own, other, n_dp, n_tensor):
    results = []
    arrived = [swap(pair[1], "dp", 1, n_dp) for pair in (own, other)]
    away = [add_low(pair[0][1], got[1]) for pair, got in zip((own, other), arrived)]
    arrived_x = [swap(value, "dp", 2, n_dp) for value in away]
    for pair, got, far in zip((own, other), arrived, arrived_x):
        results.append(add_low(pair[0][0], got[0], far))
    return add_low(results[0], swap(results[1], "tensor", 1, n_tensor))


def reduce_y_first(own, other, n_dp, n_tensor):
    arrived = [swap(pair[1], "dp", 1, n_dp) for pair in (own, other)]
    away = add_low(other[0], arrived[1])
    got = swap(away, "tensor", 1, n_tensor)
    far = add_low(own[0][1], arrived[0][1], got[1])
    return add_low(own[0][0], arrived[0][0], got[0], swap(far, "dp", 2, n_dp))


def all_sum(value, sizes, group_at):
    n_dp, n_group, n_tensor = sizes
    bit = 1
    while bit < n_dp:
        value = value + swap(value, "dp", bit, n_dp)
        bit *= 2
    value = value + swap(value, "tensor", 1, n_tensor)
    return chain_sum(value, n_group, group_at)


def on_device(sizes, residual_in, piece_ids, norm_gains, qkv_weight, qv_bias, out_weight, fc_weight,
              fc_bias, proj_weight, out_biases, cotangent):
    n_dp, n_group, n_tensor = sizes
    dp_at = lax.axis_index("dp")
    group_at = lax.axis_index("group")
    tensor_at = lax.axis_index("tensor")
    quarter_at = dp_at & 3
    place = jnp.stack([tensor_at, quarter_at]).astype(jnp.int32)
    pad = ((0, 0), (0, 1))

    def half_rows(value, at):
        return jnp.pad(lax.dynamic_index_in_dim(value, at, 0, keepdims=False), pad)

    res_own = half_rows(residual_in, tensor_at)
    res_other = swap(half_rows(residual_in, 1 - tensor_at), "tensor", 1, n_tensor)
    small_bias = jnp.concatenate([qv_bias.reshape(1, -1), fc_bias.reshape(1, -1)], axis=1)
    other_bias = swap(small_bias, "tensor", 1, n_tensor)
    qkv_other = fetch_other(qkv_weight, 1, (n_dp, n_tensor), quarter_at)
    out_own = jnp.pad(out_weight, pad)
    proj_own = jnp.pad(proj_weight, pad)
    out_other = fetch_other(out_own, 0, (n_dp, n_tensor), quarter_at)
    fc_other = fetch_other(fc_weight, 0, (n_dp, n_tensor), quarter_at)
    proj_other = fetch_other(proj_own, 0, (n_dp, n_tensor), quarter_at)
    cot_own = half_rows(cotangent, tensor_at)
    cot_other = swap(half_rows(cotangent, 1 - tensor_at), "tensor", 1, n_tensor)

    gains = norm_gains.astype(F32)
    end_biases = jnp.pad(out_biases, pad).astype(F32)
    half = qv_bias.shape[1]
    qv_other = other_bias[:, : 2 * half].reshape(2, half)
    qv_full = jnp.concatenate([qv_bias, qv_other], axis=1).astype(F32)
    fc_full = jnp.concatenate([fc_bias.reshape(1, -1), other_bias[:, 2 * half :]], axis=1).astype(F32)

    length = piece_ids.shape[1]
    flags = (lax.dynamic_index_in_dim(piece_ids, tensor_at, 0, keepdims=False)[:: length // 4] >= 0)
    flags = flags.astype(jnp.int32)

    normed_one, queries, key_rows, value_rows = project(
        place, res_own, res_other, gains[0:1], qv_full, qkv_weight, qkv_other)
    attended, log_sums = attend_forward(flags, queries, key_rows, value_rows)
    (normed_two, active, hidden_grad, out_mine, out_send, middle_grad, branch_grad, attended_grad,
     middle_sums) = middle_stage(
        place, attended, res_own, res_other, cot_own, cot_other, gains[1:2], end_biases, fc_full,
        (out_own, out_other, fc_weight, fc_other, proj_own, proj_other))
    cot_rows = jnp.where(tensor_at == 0, jnp.concatenate([cot_own, cot_other]),
                         jnp.concatenate([cot_other, cot_own]))

    pairs = half // 128
    first = attend_backward(flags, queries, key_rows, value_rows, attended_grad, log_sums, pairs, pairs)
    second = attend_backward(flags, queries, key_rows, value_rows, attended_grad, log_sums, 0, pairs)
    head_grads = list(second[:3]) + list(first[:3])
    in_mine, in_send, in_sums = input_grad(
        place, head_grads, res_own, res_other, middle_grad, gains[0:1], qkv_weight, qkv_other)

    hid = fc_bias.shape[0]
    if n_dp == 4:
        proj_grads = [weight_grad(place, active, [cot_rows], D, left_cols=hid, left_at=n) for n in range(2)]
        fc_grads = [weight_grad(place, normed_two, [hidden_grad], hid, col_at=n) for n in range(2)]
        out_keep, out_push = out_grad(place, attended, branch_grad)
        qkv_grads = [weight_grad(place, normed_one, list(part[:3]), half) for part in (second, first)]
        proj_shard = reduce_x_first(*proj_grads, n_dp, n_tensor)
        fc_shard = reduce_y_first(*fc_grads, n_dp, n_tensor)
        got = swap(out_push, "dp", 1, n_dp)
        far = swap(add_low(out_keep[1], got[1]), "dp", 2, n_dp)
        near = add_low(out_keep[0], got[0], far)
        out_shard = add_low(near[0], swap(near[1], "tensor", 1, n_tensor))
        qkv_shard = reduce_x_first(*qkv_grads, n_dp, n_tensor)
    else:
        def scatter(own, other, dim):
            total = [lax.psum_scatter(value.astype(BF16), "dp", scatter_dimension=dim, tiled=True)
                     for value in (own, other)]
            return add_low(total[0], swap(total[1], "tensor", 1, n_tensor))

        proj_shard = scatter(dot_tn(active[:, :hid], cot_rows), dot_tn(active[:, hid:], cot_rows), 0)
        fc_shard = scatter(dot_tn(normed_two, hidden_grad[:, :hid]), dot_tn(normed_two, hidden_grad[:, hid:]), 0)
        out_shard = scatter(dot_tn(attended[:, :half], branch_grad), dot_tn(attended[:, half:], branch_grad), 0)
        qkv_shard = scatter(
            *[jnp.stack([dot_tn(normed_one, value) for value in part[:3]], 1) for part in (second, first)], 0)

    proj_shard = chain_sum(proj_shard, n_group, group_at)
    fc_shard = chain_sum(fc_shard, n_group, group_at)
    out_shard = chain_sum(out_shard, n_group, group_at)
    qkv_shard = chain_sum(qkv_shard, n_group, group_at)

    def natural(own, other):
        return jnp.where(tensor_at == 0, jnp.concatenate([own, other], -1), jnp.concatenate([other, own], -1))

    small = jnp.concatenate([
        in_sums[0], middle_sums[0, :D], middle_sums[1, :D], middle_sums[2, :D],
        natural(second[3][0], first[3][0]), natural(second[3][1], first[3][1]),
        natural(middle_sums[3, :hid], middle_sums[3, hid:])]).reshape(-1, 128)
    small = all_sum(small, sizes, group_at).reshape(-1)
    grad_gains = small[: 2 * D].reshape(2, D)
    grad_out_biases = small[2 * D : 4 * D].reshape(2, D)[:, : D - 1]
    part = half // n_dp
    grad_qv_bias = lax.dynamic_slice_in_dim(
        small[4 * D : 6 * D].reshape(2, D), tensor_at * half + dp_at * part, part, 1)
    part = hid // n_dp
    grad_fc_bias = lax.dynamic_slice_in_dim(small[6 * D :], tensor_at * hid + dp_at * part, part, 0)

    def restore(mine, send):
        got = swap(send, "tensor", 1, n_tensor)
        return jnp.where(tensor_at == 0, jnp.stack([mine, got]), jnp.stack([got, mine]))[:, :, : D - 1]

    return (
        restore(out_mine, out_send),
        restore(in_mine, in_send),
        grad_gains,
        jnp.swapaxes(qkv_shard, 0, 1).astype(F32) if n_dp != 4 else qkv_shard.astype(F32),
        grad_qv_bias,
        out_shard[:, : D - 1].astype(F32),
        fc_shard.astype(F32),
        grad_fc_bias,
        proj_shard[:, : D - 1].astype(F32),
        grad_out_biases,
    )


def solution(mesh):
    sizes = (mesh.shape["dp"], mesh.shape["group"], mesh.shape["tensor"])
    in_specs = (
        P(("dp", "group"), "tensor", None),
        P(("dp", "group"), None),
        P(),
        P(None, None, "tensor"),
        P(None, "tensor"),
        P("tensor", None),
        P(None, "tensor"),
        P("tensor"),
        P("tensor", None),
        P(),
        P(("dp", "group"), "tensor", None),
    )
    out_specs = (
        P(("dp", "group"), "tensor", None),
        P(("dp", "group"), "tensor", None),
        P(),
        P(None, "dp", "tensor"),
        P(None, ("tensor", "dp")),
        P(("tensor", "dp"), None),
        P("dp", "tensor"),
        P(("tensor", "dp")),
        P(("tensor", "dp"), None),
        P(),
    )
    return jax.shard_map(
        functools.partial(on_device, sizes), mesh=mesh, in_specs=in_specs, out_specs=out_specs,
        check_vma=False)
```

```python
import functools
import jax
import jax.numpy as jnp
from jax import lax
from jax.sharding import PartitionSpec as P
from jax.experimental import pallas as pl
from jax.experimental.pallas import tpu as pltpu

D = 768
HD = 64
EPSILON = 1e-05
MASKED = -1e30
VMEM_CAP = 60 * 1024 * 1024
F32 = jnp.float32
BF16 = jnp.bfloat16
COST_FLOPS = 0.4e9


def cost(micros):
    return pl.CostEstimate(flops=int(micros * COST_FLOPS), bytes_accessed=int(micros * 4e5), transcendentals=0)


def after(value, *others):
    return lax.optimization_barrier((value, *others))[0]


def dot_nn(a, b):
    return lax.dot_general(a, b, (((1,), (0,)), ((), ())), preferred_element_type=F32)


def dot_nt(a, b):
    return lax.dot_general(a, b, (((1,), (1,)), ((), ())), preferred_element_type=F32)


def dot_tn(a, b):
    return lax.dot_general(a, b, (((0,), (0,)), ((), ())), preferred_element_type=F32)


def dot_tn_halves(left, right):
    half = left.shape[0] // 2
    return (dot_tn(left[pl.ds(0, half), :], right[pl.ds(0, half), :])
            + dot_tn(left[pl.ds(half, half), :], right[pl.ds(half, half), :]))


def column_sum(values):
    return jnp.sum(values, axis=0, keepdims=True)


def lane_of(shape):
    return lax.broadcasted_iota(jnp.int32, shape, len(shape) - 1)


def attend_forward_kernel(flags_ref, q_ref, k_ref, v_ref, out_ref, log_ref, *, block):
    length = q_ref.shape[0]
    row = lax.broadcasted_iota(jnp.int32, (block, block), 0)
    col = lax.broadcasted_iota(jnp.int32, (block, block), 1)
    causal = col <= row
    head_lane = lane_of((block, 128)) // HD
    for at in range(length // block):
        rows = pl.ds(at * block, block)
        seen = causal | (flags_ref[at] > 0)
        q_rows = q_ref[rows, :]
        reach = at * block
        parts = []
        for head in range(2):
            q_head = jnp.where(head_lane == head, q_rows, jnp.zeros_like(q_rows))
            near = jnp.where(seen, dot_nt(q_head, k_ref[rows, :]), MASKED)
            top = jnp.max(near, axis=-1, keepdims=True)
            if reach:
                far = dot_nt(q_head, k_ref[pl.ds(0, reach), :])
                top = jnp.maximum(top, jnp.max(far, axis=-1, keepdims=True))
            near = jnp.exp(near - top)
            total = jnp.sum(near, axis=-1, keepdims=True)
            mixed = dot_nn(near.astype(BF16), v_ref[rows, :])
            if reach:
                far = jnp.exp(far - top)
                total = total + jnp.sum(far, axis=-1, keepdims=True)
                mixed = mixed + dot_nn(far.astype(BF16), v_ref[pl.ds(0, reach), :])
            parts.append(mixed / total)
            logs = top + jnp.log(total)
            log_ref[0, pl.ds(head, 1), rows] = jnp.transpose(
                jnp.broadcast_to(logs, (block, 128)))[0:1, :]
        out_ref[rows, :] = jnp.where(head_lane == 0, parts[0], parts[1]).astype(BF16)


def attend_forward(flags, queries, key_rows, value_rows, first, pairs, into=None):
    length, width = queries.shape
    block = length // 4
    tile = pl.BlockSpec((length, 128), lambda h, f: (0, h + first))
    more = [] if into is None else list(into)

    def body(flags_ref, q_ref, k_ref, v_ref, *rest):
        attend_forward_kernel(flags_ref, q_ref, k_ref, v_ref, *rest[len(more):], block=block)

    return pl.pallas_call(
        body,
        grid_spec=pltpu.PrefetchScalarGridSpec(
            num_scalar_prefetch=1, grid=(pairs,),
            in_specs=[tile, tile, tile] + [pl.BlockSpec(memory_space=pl.ANY)] * len(more),
            out_specs=[tile, pl.BlockSpec((1, 8, length), lambda h, f: (h + first, 0, 0))]),
        out_shape=[jax.ShapeDtypeStruct((length, width), BF16),
                   jax.ShapeDtypeStruct((width // 128, 8, length), F32)],
        input_output_aliases={4 + n: n for n in range(len(more))},
        compiler_params=pltpu.CompilerParams(vmem_limit_bytes=VMEM_CAP),
        cost_estimate=cost(3.8 * pairs),
        name="attend_forward",
    )(flags, queries, key_rows, value_rows, *more)


def attend_backward_kernel(flags_ref, q_ref, k_ref, v_ref, up_ref, log_ref,
                           grad_ref, sum_ref, dk_acc, dv_acc, *, block):
    length = q_ref.shape[0]
    count = length // block
    key_at = lax.broadcasted_iota(jnp.int32, (block, block), 0)
    query_at = lax.broadcasted_iota(jnp.int32, (block, block), 1)
    causal = key_at <= query_at
    head_lane = lane_of((block, 128)) // HD
    full_lane = lane_of((length, 128)) // HD
    dq_sum = jnp.zeros((1, 128), F32)
    for at in reversed(range(count)):
        rows = pl.ds(at * block, block)
        reach = (at + 1) * block
        keys = pl.ds(0, reach)
        seen = causal | (flags_ref[at] > 0)
        dq = None
        for head in range(2):
            q_head = jnp.where(head_lane == head, q_ref[rows, :], jnp.zeros((block, 128), BF16))
            up_head = jnp.where(head_lane == head, up_ref[rows, :], jnp.zeros((block, 128), BF16))
            logs = log_ref[0, pl.ds(head, 1), rows]
            scores = dot_nt(k_ref[keys, :], q_head)
            last = jnp.where(seen, scores[reach - block :], MASKED)
            scores = last if at == 0 else jnp.concatenate([scores[: reach - block], last], 0)
            probs = jnp.exp(scores - logs)
            along = dot_nt(v_ref[keys, :], up_head)
            inner = jnp.sum(probs * along, axis=0, keepdims=True)
            low_grad = (probs * (along - inner)).astype(BF16)
            dv = dot_nn(probs.astype(BF16), up_head)
            dk = dot_nn(low_grad, q_head)
            if at == count - 1 and head == 0:
                dv_acc[keys, :] = dv
                dk_acc[keys, :] = dk
            else:
                dv_acc[keys, :] += dv
                dk_acc[keys, :] += dk
            k_head = jnp.where(full_lane[:reach] == head, k_ref[keys, :], jnp.zeros((reach, 128), BF16))
            part = dot_tn(low_grad, k_head)
            dq = part if dq is None else dq + part
        low_dq = (dq * HD ** (-0.5)).astype(BF16)
        grad_ref[0, rows, :] = low_dq
        dq_sum = dq_sum + column_sum(low_dq.astype(F32))
    grad_ref[1] = dk_acc[...].astype(BF16)
    low_dv = dv_acc[...].astype(BF16)
    grad_ref[2] = low_dv
    sum_ref[...] = jnp.zeros_like(sum_ref)
    sum_ref[0:1, :] = dq_sum
    sum_ref[1:2, :] = column_sum(low_dv.astype(F32))


def attend_backward(flags, queries, key_rows, value_rows, upstream, log_sums, first, pairs):
    length = queries.shape[0]
    width = pairs * 128
    tile = pl.BlockSpec((length, 128), lambda h, f: (0, h + first))
    return pl.pallas_call(
        functools.partial(attend_backward_kernel, block=length // 4),
        grid_spec=pltpu.PrefetchScalarGridSpec(
            num_scalar_prefetch=1, grid=(pairs,),
            in_specs=[tile, tile, tile, tile,
                      pl.BlockSpec((1, 8, length), lambda h, f: (h + first, 0, 0))],
            out_specs=[pl.BlockSpec((3, length, 128), lambda h, f: (0, 0, h)),
                       pl.BlockSpec((8, 128), lambda h, f: (0, h))],
            scratch_shapes=[pltpu.VMEM((length, 128), F32), pltpu.VMEM((length, 128), F32)]),
        out_shape=[jax.ShapeDtypeStruct((3, length, width), BF16), jax.ShapeDtypeStruct((8, width), F32)],
        compiler_params=pltpu.CompilerParams(vmem_limit_bytes=VMEM_CAP),
        cost_estimate=cost(6.1 * pairs),
        name="attend_backward",
    )(flags, queries, key_rows, value_rows, upstream, log_sums)


def unpack_kernel(place_ref, rows_ref, own_ref, send_ref):
    packed = rows_ref[...]
    packed = packed.reshape(packed.shape[0] * 2, packed.shape[2])
    shape = (packed.shape[0], D)
    row = lax.broadcasted_iota(jnp.int32, shape, 0)
    column = lax.broadcasted_iota(jnp.int32, shape, 1)
    for seq, out_ref in ((1 - place_ref[0], send_ref), (place_ref[0], own_ref)):
        choose = jnp.where(row == 2 * column + seq, 1.0, 0.0).astype(BF16)
        out_ref[...] = dot_tn(packed, choose).astype(BF16)


def unpack_rows(place, rows):
    packed = rows.transpose(2, 0, 1)
    out = jax.ShapeDtypeStruct((rows.shape[1], D), BF16)
    return pl.pallas_call(
        unpack_kernel,
        grid_spec=pltpu.PrefetchScalarGridSpec(
            num_scalar_prefetch=1, grid=(1,),
            in_specs=[pl.BlockSpec(packed.shape, lambda i, s: (0, 0, 0))],
            out_specs=[pl.BlockSpec(out.shape, lambda i, s: (0, 0))] * 2),
        out_shape=[out, out],
        compiler_params=pltpu.CompilerParams(vmem_limit_bytes=VMEM_CAP),
        cost_estimate=cost(5),
        name="unpack_rows",
    )(place, packed)


def decompress(compact):
    total = jnp.sum(compact, axis=-1, keepdims=True)
    return jnp.where(lane_of(compact.shape) == D - 1, -total, compact)


def crms_back(normal, factor, gain, grad):
    scaled = gain * grad
    du = factor * (scaled - normal * jnp.mean(scaled * normal, axis=-1, keepdims=True))
    lane = lane_of(du.shape)
    last = jnp.sum(jnp.where(lane == D - 1, du, 0.0), axis=-1, keepdims=True)
    return jnp.where(lane == D - 1, 0.0, du - last)


def crms_normal(compact):
    full = decompress(compact)
    factor = lax.rsqrt(jnp.mean(full * full, axis=-1, keepdims=True) + EPSILON)
    return full * factor, factor


def project_kernel(place_ref, own_ref, other_ref, gain_ref, bias_ref, w_own, w_quarter,
                   normed_ref, q_ref, k_ref, v_ref, weight, sems, *, steps):
    at = pl.program_id(0)
    quarter = D // 4
    half = w_own.shape[2]

    def copies():
        out = [pltpu.make_async_copy(w_own, weight.at[:, :, pl.ds(0, half)], sems.at[0])]
        for rel in range(4):
            place = pl.multiple_of((place_ref[1] ^ rel) * quarter, quarter)
            out.append(pltpu.make_async_copy(
                w_quarter[rel], weight.at[:, pl.ds(place, quarter), pl.ds(half, half)],
                sems.at[rel + 1]))
        return out

    @pl.when(at == 0)
    def _():
        for copy in copies():
            copy.start()

    compact = jnp.where(at < steps // 2, own_ref[...], other_ref[...]).astype(F32)
    normal, _ = crms_normal(compact)
    normed = (normal * gain_ref[...]).astype(BF16)
    normed_ref[...] = normed

    @pl.when(at == 0)
    def _():
        for copy in copies():
            copy.wait()

    q_ref[...] = ((dot_nn(normed, weight[0]) + bias_ref[0:1, :]).astype(BF16).astype(F32)
                  * HD ** (-0.5)).astype(BF16)
    k_ref[...] = dot_nn(normed, weight[1]).astype(BF16)
    v_ref[...] = (dot_nn(normed, weight[2]) + bias_ref[1:2, :]).astype(BF16)


def row_maps(steps):
    half = steps // 2
    own = lambda i, s: (jnp.minimum(i, half - 1), 0)
    other = lambda i, s: (jnp.maximum(i - half, 0), 0)
    whole = lambda i, s: (jnp.where(i < half, s[0] * half + i, (1 - s[0]) * half + i - half), 0)
    return own, other, whole


ANY = pl.BlockSpec(memory_space=pl.ANY)


def project(place, own, other, gain, bias, w_own, w_quarter, steps=4):
    length = own.shape[0] * 2
    block = length // steps
    own_map, other_map, whole_map = row_maps(steps)
    fixed = lambda i, s: (0, 0)
    wide = pl.BlockSpec((block, D), whole_map)
    out = jax.ShapeDtypeStruct((length, D), BF16)

    def body(place_ref, own_ref, other_ref, gain_ref, bias_ref, w_own, a, b, c, d, *rest):
        project_kernel(place_ref, own_ref, other_ref, gain_ref, bias_ref, w_own, (a, b, c, d),
                       *rest, steps=steps)

    return pl.pallas_call(
        body,
        grid_spec=pltpu.PrefetchScalarGridSpec(
            num_scalar_prefetch=1, grid=(steps,),
            in_specs=[pl.BlockSpec((block, D), own_map), pl.BlockSpec((block, D), other_map),
                      pl.BlockSpec((1, D), fixed), pl.BlockSpec((2, D), fixed)] + [ANY] * 5,
            out_specs=[wide] * 4,
            scratch_shapes=[pltpu.VMEM((3, D, D), BF16), pltpu.SemaphoreType.DMA((5,))]),
        out_shape=[out] * 4,
        compiler_params=pltpu.CompilerParams(vmem_limit_bytes=VMEM_CAP),
        cost_estimate=cost(10),
        name="norm_project",
    )(place, own, other, gain, bias, w_own, *w_quarter)


SQRT_2_PI = 0.7978845608028654


def gelu_pair(v):
    square = v * v
    inner = v * (SQRT_2_PI + (SQRT_2_PI * 0.044715) * square)
    tanh = jnp.tanh(inner)
    cdf = 0.5 + 0.5 * tanh
    slope = SQRT_2_PI + (3 * SQRT_2_PI * 0.044715) * square
    back = cdf + (0.5 * v) * (1.0 - tanh * tanh) * slope
    return v * cdf, back


def middle_kernel(place_ref, att_ref, res_own, res_other, cot_own, cot_other, gain_ref, end_ref,
                  fcb_ref, weights, two_ref, active_ref, hidden_ref, own_out, send_out,
                  mid_ref, branch_ref, upgrad_ref, sums_ref, own_sums, other_sums,
                  out_w, fc_w, proj_w, sems, *, steps, chunk):
    at = pl.program_id(0)
    hid = fc_w.shape[1]
    half = hid // 2
    o_own, f_own, p_own, quarters, proj_quarters = weights

    def copies(which):
        if which == 0:
            own, target = o_own, out_w.at[pl.ds(0, D // 2), :]
        elif which == 1:
            own, target = f_own, fc_w.at[:, pl.ds(0, half)]
        else:
            own, target = p_own, proj_w.at[pl.ds(0, half), :]
        out = [pltpu.make_async_copy(own, target, sems.at[which, 0])]
        for rel in range(4):
            source = proj_quarters[rel] if which == 2 else quarters[rel]
            to = place_ref[2 if which == 2 else 1] ^ rel
            if which == 0:
                moves = [(0, D // 8, out_w, D // 2 + to * (D // 8), None)]
            elif which == 1:
                moves = [(D // 8 + n * (D // 4), D // 4, fc_w, to * (D // 4), half + n * D)
                         for n in range(half // D)]
            else:
                moves = [(0, half // 4, proj_w, half + to * (half // 4), None)]
            for n, (start, rows, into, row, col) in enumerate(moves):
                spot = pl.ds(pl.multiple_of(row, rows), rows)
                out.append(pltpu.make_async_copy(
                    source.at[pl.ds(start, rows), :],
                    into.at[spot, :] if col is None else into.at[spot, pl.ds(col, D)],
                    sems.at[which, 1 + 2 * rel + n]))
        return out

    @pl.when(at == 0)
    def _():
        for which in range(3):
            for copy in copies(which):
                copy.start()
        for ref in (sums_ref, own_sums, other_sums):
            ref[...] = jnp.zeros_like(ref)
        for copy in copies(0):
            copy.wait()

    mine = at < steps // 2
    compact = jnp.where(mine, res_own[...], res_other[...]).astype(F32)
    cot_low = jnp.where(mine, cot_own[...], cot_other[...])
    middle = compact + dot_nn(att_ref[...], out_w[...]) + end_ref[0:1, :]
    normal, factor = crms_normal(middle)
    gain = gain_ref[...]
    two = (normal * gain).astype(BF16)
    two_ref[...] = two

    @pl.when(at == 0)
    def _():
        for which in (1, 2):
            for copy in copies(which):
                copy.wait()

    mlp = jnp.zeros((two.shape[0], D), F32)
    two_grad = jnp.zeros((two.shape[0], D), F32)
    for start in range(0, hid, chunk):
        cols = pl.ds(start, chunk)
        pre = dot_nn(two, fc_w[:, cols]) + fcb_ref[0:1, cols]
        act, slope = gelu_pair(pre)
        act = act.astype(BF16)
        active_ref[:, cols] = act
        mlp = mlp + dot_nn(act, proj_w[cols, :])
        hidden = (dot_nt(cot_low, proj_w[cols, :]) * slope).astype(BF16)
        hidden_ref[:, cols] = hidden
        to = own_sums if start < half else other_sums
        to[0:1, pl.ds(start % half, chunk)] += column_sum(hidden.astype(F32))
        two_grad = two_grad + dot_nt(hidden, fc_w[:, cols])
    block_out = (middle + mlp + end_ref[1:2, :]).astype(BF16)

    @pl.when(mine)
    def _():
        own_out[...] = block_out

    @pl.when(jnp.logical_not(mine))
    def _():
        send_out[...] = block_out

    cot = cot_low.astype(F32)
    mid_grad = cot + crms_back(normal, factor, gain, two_grad)
    mid_ref[...] = mid_grad
    branch = mid_grad.astype(BF16)
    branch_ref[...] = branch
    upgrad_ref[...] = dot_nt(branch, out_w[...]).astype(BF16)
    sums_ref[0:1, :] += column_sum(two_grad * normal)
    sums_ref[1:2, :] += column_sum(branch.astype(F32))
    sums_ref[2:3, :] += column_sum(cot)


def middle_stage(place, att, res_own, res_other, cot_own, cot_other, gain, end_bias, fc_bias, weights,
                 steps=4, chunk=768):
    length = att.shape[0]
    hid = fc_bias.shape[1]
    block = length // steps
    own_map, other_map, whole_map = row_maps(steps)
    fixed = lambda i, s: (0, 0)
    flat = [*weights[:3], *weights[3], *weights[4]]
    spec = lambda w, m: pl.BlockSpec((block, w), m)

    def body(place_ref, *refs):
        ins, rest = refs[:8], refs[8:]
        w, rest = rest[:11], rest[11:]
        packed = (*w[:3], w[3:7], w[7:])
        middle_kernel(place_ref, *ins, packed, *rest, steps=steps, chunk=chunk)

    sd = jax.ShapeDtypeStruct
    return pl.pallas_call(
        body,
        grid_spec=pltpu.PrefetchScalarGridSpec(
            num_scalar_prefetch=1, grid=(steps,),
            in_specs=[spec(D, whole_map), spec(D, own_map), spec(D, other_map), spec(D, own_map),
                      spec(D, other_map), pl.BlockSpec((1, D), fixed), pl.BlockSpec((2, D), fixed),
                      pl.BlockSpec((1, hid), fixed)] + [ANY] * 11,
            out_specs=[spec(D, whole_map), spec(hid, whole_map), spec(hid, whole_map),
                       spec(D, own_map), spec(D, other_map),
                       spec(D, whole_map), spec(D, whole_map), spec(D, whole_map),
                       pl.BlockSpec((8, D), fixed), pl.BlockSpec((8, hid // 2), fixed),
                       pl.BlockSpec((8, hid // 2), fixed)],
            scratch_shapes=[pltpu.VMEM((D, D), BF16), pltpu.VMEM((D, hid), BF16),
                            pltpu.VMEM((hid, D), BF16), pltpu.SemaphoreType.DMA((3, 9))]),
        out_shape=[sd((length, D), BF16), sd((length, hid), BF16), sd((length, hid), BF16),
                   sd((length // 2, D), BF16), sd((length // 2, D), BF16),
                   sd((length, D), F32), sd((length, D), BF16), sd((length, D), BF16),
                   sd((8, D), F32), sd((8, hid // 2), F32), sd((8, hid // 2), F32)],
        compiler_params=pltpu.CompilerParams(vmem_limit_bytes=VMEM_CAP),
        cost_estimate=cost(38),
        name="middle_stage",
    )(place, att, res_own, res_other, cot_own, cot_other, gain, end_bias, fc_bias, *flat)


def fc_grad_kernel(place_ref, left_ref, right_ref, keep_ref, send_ref, *, rows):
    flip = (place_ref[1] & 1) == 1
    both = dot_tn_halves(left_ref, right_ref).astype(BF16)
    for pair in range(2):
        low, high = both[2 * pair * rows : (2 * pair + 1) * rows], both[(2 * pair + 1) * rows : (2 * pair + 2) * rows]
        to = pair ^ (place_ref[1] >> 1)
        keep_ref[to, 0] = jnp.where(flip, high, low)
        send_ref[to, 0] = jnp.where(flip, low, high)


def fc_grad(place, left, right, chunk=768):
    length, width = left.shape
    rows = width // 4
    half = right.shape[1] // 2
    parts = half // chunk
    out = jax.ShapeDtypeStruct((2, 2, rows, half), BF16)
    out_spec = pl.BlockSpec((2, 1, rows, chunk), lambda n, s: (0, n // parts, 0, n % parts))
    return pl.pallas_call(
        functools.partial(fc_grad_kernel, rows=rows),
        grid_spec=pltpu.PrefetchScalarGridSpec(
            num_scalar_prefetch=1, grid=(2 * parts,),
            in_specs=[pl.BlockSpec((length, width), lambda n, s: (0, 0)),
                      pl.BlockSpec((length, chunk), lambda n, s: (0, n))],
            out_specs=[out_spec, out_spec]),
        out_shape=[out, out],
        compiler_params=pltpu.CompilerParams(vmem_limit_bytes=VMEM_CAP),
        cost_estimate=cost(10),
        name="fc_grad",
    )(place, left, right)


def qkv_grad_kernel(place_ref, left_ref, right_ref, keep_ref, send_ref, *, rows):
    flip = (place_ref[1] & 1) == 1
    half = left_ref.shape[0] // 2
    width = right_ref.shape[2]
    both = None
    for n in range(2):
        part = pl.ds(n * half, half)
        right = jnp.concatenate([right_ref[c, part, :] for c in range(3)], axis=1)
        here = dot_tn(left_ref[part, :], right)
        both = here if both is None else both + here
    both = both.astype(BF16)
    for c in range(3):
        low = both[:rows, c * width : (c + 1) * width]
        high = both[rows:, c * width : (c + 1) * width]
        keep_ref[0, c] = jnp.where(flip, high, low)
        send_ref[0, c] = jnp.where(flip, low, high)


def qkv_grad(place, left, rights):
    length, width = left.shape
    rows = width // 4
    cols = rights.shape[2]
    out = jax.ShapeDtypeStruct((2, 3, rows, cols), BF16)
    out_spec = pl.BlockSpec((1, 3, rows, cols), lambda j, s: (j ^ (s[1] >> 1), 0, 0, 0))
    return pl.pallas_call(
        functools.partial(qkv_grad_kernel, rows=rows),
        grid_spec=pltpu.PrefetchScalarGridSpec(
            num_scalar_prefetch=1, grid=(2,),
            in_specs=[pl.BlockSpec((length, 2 * rows), lambda j, s: (0, j)),
                      pl.BlockSpec((3, length, cols), lambda j, s: (0, 0, 0))],
            out_specs=[out_spec, out_spec]),
        out_shape=[out, out],
        compiler_params=pltpu.CompilerParams(vmem_limit_bytes=VMEM_CAP),
        cost_estimate=cost(5),
        name="qkv_grad",
    )(place, left, rights)


def proj_grad_kernel(place_ref, own_act, other_act, own_cot, other_cot, keep_ref, send_ref, *, rows):
    flip = (place_ref[1] & 1) == 1
    both = (dot_tn(own_act[...], own_cot[...]) + dot_tn(other_act[...], other_cot[...])).astype(BF16)
    low, high = both[:rows], both[rows:]
    keep_ref[0, 0] = jnp.where(flip, high, low)
    send_ref[0, 0] = jnp.where(flip, low, high)


def proj_grad(place, active, cot_own, cot_other):
    length, width = active.shape
    rows = width // 8
    out = jax.ShapeDtypeStruct((2, 2, rows, D), BF16)
    out_spec = pl.BlockSpec((1, 1, rows, D), lambda n, j, s: (j ^ (s[1] >> 1), n, 0, 0))
    cot_spec = pl.BlockSpec((length // 2, D), lambda n, j, s: (0, 0))
    return pl.pallas_call(
        functools.partial(proj_grad_kernel, rows=rows),
        grid_spec=pltpu.PrefetchScalarGridSpec(
            num_scalar_prefetch=1, grid=(2, 2),
            in_specs=[pl.BlockSpec((length // 2, 2 * rows), lambda n, j, s: (s[0], n * 2 + j)),
                      pl.BlockSpec((length // 2, 2 * rows), lambda n, j, s: (1 - s[0], n * 2 + j)),
                      cot_spec, cot_spec],
            out_specs=[out_spec, out_spec]),
        out_shape=[out, out],
        compiler_params=pltpu.CompilerParams(vmem_limit_bytes=VMEM_CAP),
        cost_estimate=cost(13),
        name="proj_grad",
    )(place, active, active, cot_own, cot_other)


def out_grad_kernel(place_ref, left_ref, right_ref, keep_ref, send_ref, *, rows):
    flip = (place_ref[1] & 1) == 1
    both = dot_tn_halves(left_ref, right_ref).astype(BF16)
    for side in range(2):
        for pair in range(2):
            at = (side * 4 + pair * 2) * rows
            low, high = both[at : at + rows], both[at + rows : at + 2 * rows]
            to = pair ^ (place_ref[1] >> 1)
            keep_ref[to, side] = jnp.where(flip, high, low)
            send_ref[to, side] = jnp.where(flip, low, high)


def out_grad(place, left, right):
    length, width = left.shape
    rows = width // 8
    out = jax.ShapeDtypeStruct((2, 2, rows, right.shape[1]), BF16)
    return pl.pallas_call(
        functools.partial(out_grad_kernel, rows=rows),
        grid_spec=pltpu.PrefetchScalarGridSpec(
            num_scalar_prefetch=1, grid=(1,),
            in_specs=[pl.BlockSpec(value.shape, lambda i, s: (0, 0)) for value in (left, right)],
            out_specs=[pl.BlockSpec(out.shape, lambda i, s: (0, 0, 0, 0))] * 2),
        out_shape=[out, out],
        compiler_params=pltpu.CompilerParams(vmem_limit_bytes=VMEM_CAP),
        cost_estimate=cost(5),
        name="out_grad",
    )(place, left, right)


def input_grad_kernel(place_ref, own_grad, other_grad, res_own, res_other, mid_ref, gain_ref, w_own, w_quarter,
                      own_out, send_out, sums_ref, weight, sems, *, steps):
    at = pl.program_id(0)
    quarter = D // 4
    half = w_own.shape[2]

    def copies():
        out = []
        for c in range(3):
            out.append(pltpu.make_async_copy(
                w_own.at[c], weight.at[:, pl.ds(c * half, half)], sems.at[c, 0]))
            for rel in range(4):
                place = pl.multiple_of((place_ref[1] ^ rel) * quarter, quarter)
                out.append(pltpu.make_async_copy(
                    w_quarter[rel].at[c], weight.at[pl.ds(place, quarter), pl.ds((3 + c) * half, half)],
                    sems.at[c, rel + 1]))
        return out

    @pl.when(at == 0)
    def _():
        for copy in copies():
            copy.start()
        sums_ref[...] = jnp.zeros_like(sums_ref)

    mine = at < steps // 2
    compact = jnp.where(mine, res_own[...], res_other[...]).astype(F32)
    normal, factor = crms_normal(compact)

    @pl.when(at == 0)
    def _():
        for copy in copies():
            copy.wait()

    left = jnp.concatenate([own_grad[c] for c in range(3)] + [other_grad[c] for c in range(3)], axis=1)
    grad = dot_nt(left, weight[...])
    sums_ref[0:1, :] += column_sum(grad * normal)
    result = (mid_ref[...] + crms_back(normal, factor, gain_ref[...], grad)).astype(BF16)

    @pl.when(mine)
    def _():
        own_out[...] = result

    @pl.when(jnp.logical_not(mine))
    def _():
        send_out[...] = result


def input_grad(place, own_grad, other_grad, res_own, res_other, mid, gain, w_own, w_quarter, steps=4):
    length = mid.shape[0]
    block = length // steps
    own_map, other_map, whole_map = row_maps(steps)
    fixed = lambda i, s: (0, 0)
    half = own_grad.shape[2]
    grad_spec = pl.BlockSpec((3, block, half), lambda i, s: (0, whole_map(i, s)[0], 0))

    def body(place_ref, *refs):
        input_grad_kernel(place_ref, *refs[:7], refs[7:11], *refs[11:], steps=steps)

    sd = jax.ShapeDtypeStruct
    return pl.pallas_call(
        body,
        grid_spec=pltpu.PrefetchScalarGridSpec(
            num_scalar_prefetch=1, grid=(steps,),
            in_specs=[grad_spec, grad_spec, pl.BlockSpec((block, D), own_map), pl.BlockSpec((block, D), other_map),
                      pl.BlockSpec((block, D), whole_map), pl.BlockSpec((1, D), fixed)] + [ANY] * 5,
            out_specs=[pl.BlockSpec((block, D), own_map), pl.BlockSpec((block, D), other_map),
                       pl.BlockSpec((8, D), fixed)],
            scratch_shapes=[pltpu.VMEM((D, 3 * D), BF16), pltpu.SemaphoreType.DMA((3, 5))]),
        out_shape=[sd((length // 2, D), BF16), sd((length // 2, D), BF16), sd((8, D), F32)],
        compiler_params=pltpu.CompilerParams(vmem_limit_bytes=VMEM_CAP),
        cost_estimate=cost(9),
        name="input_grad",
    )(place, own_grad, other_grad, res_own, res_other, mid, gain, w_own, *w_quarter)


FORWARD_SPLIT = ((0, 2), (2, 3), (5, 1))


def swap(value, axis, bit, size):
    return lax.ppermute(value, axis, [(n, n ^ bit) for n in range(size)])


def meet(*values):
    return lax.optimization_barrier(values)


def add_low(*values):
    total = values[0].astype(F32)
    for value in values[1:]:
        total = total + value.astype(F32)
    return total.astype(BF16)


def fours(value, axis, size):
    return [swap(value, axis, rel, size) for rel in (1, 2, 3)]


def sum_fours(value, others):
    return (value + others[0]) + (others[1] + others[2])


def quarter_of(value, index):
    rows = value.shape[0] // 4
    return lax.dynamic_slice_in_dim(value, index * rows, rows, 0)


def in_order(parts, index):
    odd, high = (index & 1) == 1, (index & 2) == 2
    flip = lambda flag, a, b: (jnp.where(flag, b, a), jnp.where(flag, a, b))
    parts = [*flip(odd, parts[0], parts[1]), *flip(odd, parts[2], parts[3])]
    first, third = flip(high, parts[0], parts[2])
    second, fourth = flip(high, parts[1], parts[3])
    return jnp.concatenate([first, second, third, fourth], 0)


def on_device(sizes, residual_in, piece_ids, norm_gains, qkv_weight, qv_bias, out_weight, fc_weight,
              fc_bias, proj_weight, out_biases, cotangent):
    n_dp, n_group, n_tensor = sizes["dp"], sizes["group"], sizes["tensor"]
    dp_at = lax.axis_index("dp")
    group_at = lax.axis_index("group")
    tensor_at = lax.axis_index("tensor")
    quarter_at = dp_at & 3
    proj_at = (dp_at & 1) | ((group_at & 1) << 1)
    place = jnp.stack([tensor_at, quarter_at, proj_at]).astype(jnp.int32)
    pad = ((0, 0), (0, 1))
    half = qv_bias.shape[1]
    hid = fc_bias.shape[0]
    pairs = half // 128
    y_swap = lambda value: swap(value, "tensor", 1, n_tensor)
    x_swap = lambda value: swap(value, "dp", 2, n_dp)
    c_swap = lambda value: swap(value, "dp", 1, n_dp)
    z_swap = lambda value: swap(value, "group", 1, n_group)

    def piece_of(shard, dim, at):
        rows = shard.shape[dim] // 4
        return lax.dynamic_slice_in_dim(shard, at * rows, rows, dim)

    qkv_piece = piece_of(qkv_weight, 1, quarter_at)
    qkv_y = y_swap(qkv_piece)
    res_own, res_send = unpack_rows(after(place, qkv_piece), residual_in)
    small_bias = jnp.concatenate([qv_bias.reshape(1, -1), fc_bias.reshape(1, -1)], axis=1)
    qkv_y, res_own, res_send, small_bias, out_gated, fc_gated, proj_gated = meet(
        qkv_y, res_own, res_send, small_bias, out_weight, fc_weight, proj_weight)
    res_other = y_swap(res_send)
    other_bias = y_swap(small_bias)
    qkv_x = x_swap(qkv_y)
    qkv_c = c_swap(qkv_y)
    fc_piece = piece_of(fc_gated, 0, quarter_at)
    mix = jnp.concatenate([jnp.pad(piece_of(out_gated, 0, quarter_at), pad)]
                          + [fc_piece[:, n : n + D] for n in range(0, hid, D)], 0)
    proj_piece = jnp.pad(piece_of(proj_gated, 0, proj_at), pad)
    cot_own, cot_send = unpack_rows(after(place, mix, proj_piece), cotangent)
    out_own = jnp.pad(out_gated, pad)
    proj_own = jnp.pad(proj_gated, pad)
    qkv_x, qkv_c, res_other, other_bias, mix, proj_piece, cot_send, out_own, proj_own = meet(
        qkv_x, qkv_c, res_other, other_bias, mix, proj_piece, cot_send, out_own, proj_own)
    mix_y = y_swap(mix)
    qkv_cx = c_swap(qkv_x)
    qkv_others = (qkv_y, qkv_c, qkv_x, qkv_cx)

    gains = norm_gains.astype(F32)
    end_biases = jnp.pad(out_biases, pad).astype(F32)
    qv_other = other_bias[:, : 2 * half].reshape(2, half)
    qv_full = jnp.concatenate([qv_bias, qv_other], axis=1).astype(F32)
    fc_full = jnp.concatenate([fc_bias.reshape(1, -1), other_bias[:, 2 * half :]], axis=1).astype(F32)
    length = piece_ids.shape[1]
    flags = (lax.dynamic_index_in_dim(piece_ids, tensor_at, 0, keepdims=False)[:: length // 4] >= 0)
    flags = flags.astype(jnp.int32)

    normed_one, queries, key_rows, value_rows = project(
        place, res_own, res_other, gains[0:1], qv_full, qkv_weight, qkv_others)
    queries, proj_piece = meet(queries, proj_piece)
    attended = None
    proj_y = y_swap(proj_piece)
    for n, (start, count) in enumerate(FORWARD_SPLIT):
        if n == 1:
            attended[0], attended[1], queries, mix_y, cot_send = meet(*attended, queries, mix_y, cot_send)
            mix_x, mix_c = x_swap(mix_y), c_swap(mix_y)
            cot_other = y_swap(cot_send)
        elif n == 2:
            attended[0], attended[1], queries, proj_y = meet(*attended, queries, proj_y)
            proj_x, proj_c = z_swap(proj_y), c_swap(proj_y)
        attended = list(attend_forward(flags, queries, key_rows, value_rows, start, count, attended))
    attended, log_sums, mix_x, proj_x = meet(*attended, mix_x, proj_x)
    mix_others = (mix_y, mix_c, mix_x, c_swap(mix_x))
    proj_others = (proj_y, proj_c, proj_x, c_swap(proj_x))

    (normed_two, active, hidden_grad, out_mine, out_send, middle_grad, branch_grad, attended_grad,
     middle_sums, own_sums, other_sums) = middle_stage(
        place, attended, res_own, res_other, cot_own, cot_other, gains[1:2], end_biases, fc_full,
        (out_own, fc_weight, proj_own, mix_others, proj_others))
    backward = functools.partial(attend_backward, flags, queries, key_rows, value_rows)
    restore = lambda mine, got: jnp.where(
        tensor_at == 0, jnp.stack([mine, got]), jnp.stack([got, mine]))[:, :, : D - 1]

    if n_dp == 4 and n_group == 4:
        out_got = y_swap(out_send)
        proj_k, proj_s = proj_grad(after(place, middle_sums), active, cot_own, cot_other)
        proj_c = c_swap(proj_s)
        fc_k, fc_s = fc_grad(after(place, proj_k), normed_two, hidden_grad)
        fc_k, fc_s, proj_k, proj_c, out_got = meet(fc_k, fc_s, proj_k, proj_c, out_got)
        fc_c = c_swap(fc_s)
        proj_f = add_low(proj_k[1], proj_c[1])
        proj_x = x_swap(proj_f)
        out_k, out_s = out_grad(after(place, proj_f), attended, branch_grad)
        out_k, out_s, fc_k, fc_c = meet(out_k, out_s, fc_k, fc_c)
        out_c = c_swap(out_s)
        fc_away = add_low(fc_k[:, 1], fc_c[:, 1])
        fc_y = y_swap(fc_away)
        first, first_sums = backward(after(attended_grad, fc_away), log_sums, pairs, pairs)
        first, first_sums, proj_k, proj_c, proj_x, out_k, out_c = meet(
            first, first_sums, proj_k, proj_c, proj_x, out_k, out_c)
        proj_r = [add_low(proj_k[0, n], proj_c[0, n], proj_x[n]) for n in range(2)]
        proj_y = y_swap(proj_r[1])
        out_f = add_low(out_k[1], out_c[1])
        out_x = x_swap(out_f)
        qo_k, qo_s = qkv_grad(after(place, proj_r[1], out_f), normed_one, first)
        qo_k, qo_s, fc_k, fc_c, fc_y, out_k, out_c, out_x = meet(qo_k, qo_s, fc_k, fc_c, fc_y, out_k, out_c, out_x)
        qo_c = c_swap(qo_s)
        fc_far = add_low(fc_k[1, 0], fc_c[1, 0], fc_y[1])
        fc_x = x_swap(fc_far)
        out_r = [add_low(out_k[0, n], out_c[0, n], out_x[n]) for n in range(2)]
        out_y = y_swap(out_r[1])
        second, second_sums = backward(after(attended_grad, fc_far, out_r[1]), log_sums, 0, pairs)
        second, second_sums, proj_y, fc_x, out_y, qo_k, qo_c = meet(
            second, second_sums, proj_y, fc_x, out_y, qo_k, qo_c)
        proj_shard = add_low(proj_r[0], proj_y)
        fc_shard = add_low(fc_k[0, 0], fc_c[0, 0], fc_y[0], fc_x)
        proj_shard, fc_shard = lax.psum((proj_shard, fc_shard), "group")
        qo_f = add_low(qo_k[1], qo_c[1])
        qo_x = x_swap(qo_f)
        qm_k, qm_s = qkv_grad(after(place, qo_f), normed_one, second)
        qm_k, qm_s, qo_k, qo_c, qo_x = meet(qm_k, qm_s, qo_k, qo_c, qo_x)
        qm_c = c_swap(qm_s)
        qo_r = add_low(qo_k[0], qo_c[0], qo_x)
        qo_y = y_swap(qo_r)
        small_y = [y_swap(value) for value in meet(middle_sums, other_sums, first_sums, qo_r)[:3]]
        block_out = restore(after(out_mine, qo_r), out_got)
        qm_k, qm_c, block_out = meet(qm_k, qm_c, block_out)
        qm_f = add_low(qm_k[1], qm_c[1])
        qm_x = x_swap(qm_f)
        in_mine, in_send, in_sums = input_grad(
            after(place, qm_f), second, first, res_own, res_other, middle_grad, gains[0:1], qkv_weight, qkv_others)
        in_mine, in_send, in_sums, qm_x, qo_y, *small_y = meet(in_mine, in_send, in_sums, qm_x, qo_y, *small_y)
        in_y = y_swap(in_sums)
        in_got = y_swap(in_send)
        small = jnp.concatenate(
            [middle_sums + small_y[0], own_sums + small_y[1], second_sums + small_y[2]], 1)
        small_dp = fours(small, "dp", n_dp)
        last = jnp.concatenate([add_low(qm_k[0], qm_c[0], qm_x, qo_y).reshape(-1, D), add_low(out_r[0], out_y)], 0)
        last_z = [swap(quarter_of(last, group_at ^ rel), "group", rel, n_group) for rel in (1, 2, 3)]
        small, in_sums, in_y, *small_dp = meet(small, in_sums, in_y, *small_dp)
        in_sums = in_sums + in_y
        in_dp = fours(in_sums, "dp", n_dp)
        small = sum_fours(small, small_dp)
        last, in_sums, *others = meet(last, in_sums, *last_z, *in_dp)
        total = add_low(quarter_of(last, group_at), *others[:3])
        total_z = fours(total, "group", n_group)
        in_sums = sum_fours(in_sums, others[3:])
        in_z = fours(in_sums, "group", n_group)
        small_z = fours(small, "group", n_group)
        small = sum_fours(small, small_z)
        in_sums = sum_fours(in_sums, in_z)
        total, small, in_sums, proj_shard, fc_shard = meet(total, small, in_sums, proj_shard, fc_shard)
        last = in_order([total] + total_z, group_at).astype(F32)
        qkv_shard = last[: 3 * D // 8].reshape(3, D // 4, half)
        out_shard = last[3 * D // 8 :]
    else:
        first, first_sums = backward(attended_grad, log_sums, pairs, pairs)
        second, second_sums = backward(attended_grad, log_sums, 0, pairs)
        in_mine, in_send, in_sums = input_grad(
            place, second, first, res_own, res_other, middle_grad, gains[0:1], qkv_weight, qkv_others)
        in_got = y_swap(in_send)
        block_out = restore(out_mine, y_swap(out_send))

        def scatter(own, other):
            total = [lax.psum_scatter(value.astype(BF16), "dp", scatter_dimension=0, tiled=True)
                     for value in (own, other)]
            return lax.psum(add_low(total[0], y_swap(total[1])), "group")

        cot_rows = jnp.where(tensor_at == 0, jnp.concatenate([cot_own, cot_other]),
                             jnp.concatenate([cot_other, cot_own]))
        proj_shard = scatter(dot_tn(active[:, :hid], cot_rows), dot_tn(active[:, hid:], cot_rows))
        fc_shard = scatter(dot_tn(normed_two, hidden_grad[:, :hid]), dot_tn(normed_two, hidden_grad[:, hid:]))
        out_shard = scatter(dot_tn(attended[:, :half], branch_grad), dot_tn(attended[:, half:], branch_grad))
        qkv_shard = jnp.swapaxes(scatter(
            *[jnp.stack([dot_tn(normed_one, part[c]) for c in range(3)], 1) for part in (second, first)]), 0, 1)
        small = jnp.concatenate([
            middle_sums + y_swap(middle_sums), own_sums + y_swap(other_sums), second_sums + y_swap(first_sums)], 1)
        small = lax.psum(small, ("dp", "group"))
        in_sums = lax.psum(in_sums, ("dp", "group", "tensor"))

    grad_gains = jnp.concatenate([in_sums[0:1], small[0:1, :D]], 0)
    grad_out_biases = small[1:3, : D - 1]
    part = hid // n_dp
    grad_fc_bias = lax.dynamic_slice(small, (0, D + dp_at * part), (1, part)).reshape(part)
    part = half // n_dp
    grad_qv_bias = lax.dynamic_slice(small, (0, D + hid + dp_at * part), (2, part))

    return (
        block_out,
        restore(in_mine, in_got),
        grad_gains,
        qkv_shard.astype(F32),
        grad_qv_bias,
        out_shard[:, : D - 1].astype(F32),
        fc_shard.astype(F32),
        grad_fc_bias,
        proj_shard[:, : D - 1].astype(F32),
        grad_out_biases,
    )


def solution(mesh):
    sizes = dict(mesh.shape)
    in_specs = (
        P(("dp", "group"), "tensor", None),
        P(("dp", "group"), None),
        P(),
        P(None, None, "tensor"),
        P(None, "tensor"),
        P("tensor", None),
        P(None, "tensor"),
        P("tensor"),
        P("tensor", None),
        P(),
        P(("dp", "group"), "tensor", None),
    )
    out_specs = (
        P(("dp", "group"), "tensor", None),
        P(("dp", "group"), "tensor", None),
        P(),
        P(None, "dp", "tensor"),
        P(None, ("tensor", "dp")),
        P(("tensor", "dp"), None),
        P("dp", "tensor"),
        P(("tensor", "dp")),
        P(("tensor", "dp"), None),
        P(),
    )
    return jax.shard_map(
        functools.partial(on_device, sizes), mesh=mesh, in_specs=in_specs, out_specs=out_specs,
        check_vma=False)
```

```python
import functools
import jax
import jax.numpy as jnp
from jax import lax
from jax.sharding import PartitionSpec as P
from jax.experimental import pallas as pl
from jax.experimental.pallas import tpu as pltpu

D = 768
HD = 64
EPSILON = 1e-05
MASKED = -1e30
VMEM_CAP = 60 * 1024 * 1024
F32 = jnp.float32
BF16 = jnp.bfloat16
COST_FLOPS = 0.4e9


def cost(micros):
    return pl.CostEstimate(flops=int(micros * COST_FLOPS), bytes_accessed=int(micros * 4e5), transcendentals=0)


def after(value, *others):
    return lax.optimization_barrier((value, *others))[0]


def dot_nn(a, b):
    return lax.dot_general(a, b, (((1,), (0,)), ((), ())), preferred_element_type=F32)


def dot_nt(a, b):
    return lax.dot_general(a, b, (((1,), (1,)), ((), ())), preferred_element_type=F32)


def dot_tn(a, b):
    return lax.dot_general(a, b, (((0,), (0,)), ((), ())), preferred_element_type=F32)


def dot_tn_halves(left, right):
    half = left.shape[0] // 2
    return (dot_tn(left[pl.ds(0, half), :], right[pl.ds(0, half), :])
            + dot_tn(left[pl.ds(half, half), :], right[pl.ds(half, half), :]))


def column_sum(values):
    return jnp.sum(values, axis=0, keepdims=True)


def lane_of(shape):
    return lax.broadcasted_iota(jnp.int32, shape, len(shape) - 1)


def attend_forward_kernel(flags_ref, q_ref, k_ref, v_ref, out_ref, log_ref, *, block):
    length = q_ref.shape[0]
    row = lax.broadcasted_iota(jnp.int32, (block, block), 0)
    col = lax.broadcasted_iota(jnp.int32, (block, block), 1)
    causal = col <= row
    head_lane = lane_of((block, 128)) // HD
    for at in range(length // block):
        rows = pl.ds(at * block, block)
        seen = causal | (flags_ref[at] > 0)
        q_rows = q_ref[rows, :]
        reach = at * block
        parts = []
        for head in range(2):
            q_head = jnp.where(head_lane == head, q_rows, jnp.zeros_like(q_rows))
            near = jnp.where(seen, dot_nt(q_head, k_ref[rows, :]), MASKED)
            top = jnp.max(near, axis=-1, keepdims=True)
            if reach:
                far = dot_nt(q_head, k_ref[pl.ds(0, reach), :])
                top = jnp.maximum(top, jnp.max(far, axis=-1, keepdims=True))
            near = jnp.exp(near - top)
            total = jnp.sum(near, axis=-1, keepdims=True)
            mixed = dot_nn(near.astype(BF16), v_ref[rows, :])
            if reach:
                far = jnp.exp(far - top)
                total = total + jnp.sum(far, axis=-1, keepdims=True)
                mixed = mixed + dot_nn(far.astype(BF16), v_ref[pl.ds(0, reach), :])
            parts.append(mixed / total)
            logs = top + jnp.log(total)
            log_ref[0, pl.ds(head, 1), rows] = jnp.transpose(
                jnp.broadcast_to(logs, (block, 128)))[0:1, :]
        out_ref[rows, :] = jnp.where(head_lane == 0, parts[0], parts[1]).astype(BF16)


def attend_forward(flags, queries, key_rows, value_rows, first, pairs, into=None):
    length, width = queries.shape
    block = length // 4
    tile = pl.BlockSpec((length, 128), lambda h, f: (0, h + first))
    more = [] if into is None else list(into)

    def body(flags_ref, q_ref, k_ref, v_ref, *rest):
        attend_forward_kernel(flags_ref, q_ref, k_ref, v_ref, *rest[len(more):], block=block)

    return pl.pallas_call(
        body,
        grid_spec=pltpu.PrefetchScalarGridSpec(
            num_scalar_prefetch=1, grid=(pairs,),
            in_specs=[tile, tile, tile] + [pl.BlockSpec(memory_space=pl.ANY)] * len(more),
            out_specs=[tile, pl.BlockSpec((1, 8, length), lambda h, f: (h + first, 0, 0))]),
        out_shape=[jax.ShapeDtypeStruct((length, width), BF16),
                   jax.ShapeDtypeStruct((width // 128, 8, length), F32)],
        input_output_aliases={4 + n: n for n in range(len(more))},
        compiler_params=pltpu.CompilerParams(vmem_limit_bytes=VMEM_CAP),
        cost_estimate=cost(3.8 * pairs),
        name="attend_forward",
    )(flags, queries, key_rows, value_rows, *more)


def attend_backward_kernel(flags_ref, q_ref, k_ref, v_ref, up_ref, log_ref,
                           grad_ref, sum_ref, dk_acc, dv_acc, *, block):
    length = q_ref.shape[0]
    count = length // block
    key_at = lax.broadcasted_iota(jnp.int32, (block, block), 0)
    query_at = lax.broadcasted_iota(jnp.int32, (block, block), 1)
    causal = key_at <= query_at
    head_lane = lane_of((block, 128)) // HD
    full_lane = lane_of((length, 128)) // HD
    dq_sum = jnp.zeros((1, 128), F32)
    for at in reversed(range(count)):
        rows = pl.ds(at * block, block)
        reach = (at + 1) * block
        keys = pl.ds(0, reach)
        seen = causal | (flags_ref[at] > 0)
        dq = None
        for head in range(2):
            q_head = jnp.where(head_lane == head, q_ref[rows, :], jnp.zeros((block, 128), BF16))
            up_head = jnp.where(head_lane == head, up_ref[rows, :], jnp.zeros((block, 128), BF16))
            logs = log_ref[0, pl.ds(head, 1), rows]
            scores = dot_nt(k_ref[keys, :], q_head)
            last = jnp.where(seen, scores[reach - block :], MASKED)
            scores = last if at == 0 else jnp.concatenate([scores[: reach - block], last], 0)
            probs = jnp.exp(scores - logs)
            along = dot_nt(v_ref[keys, :], up_head)
            inner = jnp.sum(probs * along, axis=0, keepdims=True)
            low_grad = (probs * (along - inner)).astype(BF16)
            dv = dot_nn(probs.astype(BF16), up_head)
            dk = dot_nn(low_grad, q_head)
            if at == count - 1 and head == 0:
                dv_acc[keys, :] = dv
                dk_acc[keys, :] = dk
            else:
                dv_acc[keys, :] += dv
                dk_acc[keys, :] += dk
            k_head = jnp.where(full_lane[:reach] == head, k_ref[keys, :], jnp.zeros((reach, 128), BF16))
            part = dot_tn(low_grad, k_head)
            dq = part if dq is None else dq + part
        low_dq = (dq * HD ** (-0.5)).astype(BF16)
        grad_ref[0, rows, :] = low_dq
        dq_sum = dq_sum + column_sum(low_dq.astype(F32))
    grad_ref[1] = dk_acc[...].astype(BF16)
    low_dv = dv_acc[...].astype(BF16)
    grad_ref[2] = low_dv
    sum_ref[...] = jnp.zeros_like(sum_ref)
    sum_ref[0:1, :] = dq_sum
    sum_ref[1:2, :] = column_sum(low_dv.astype(F32))


def attend_backward(flags, queries, key_rows, value_rows, upstream, log_sums, first, pairs):
    length = queries.shape[0]
    tile = pl.BlockSpec((length, 128), lambda h, f: (0, h + first))
    return pl.pallas_call(
        functools.partial(attend_backward_kernel, block=length // 4),
        grid_spec=pltpu.PrefetchScalarGridSpec(
            num_scalar_prefetch=1, grid=(pairs,),
            in_specs=[tile, tile, tile, tile,
                      pl.BlockSpec((1, 8, length), lambda h, f: (h + first, 0, 0))],
            out_specs=[pl.BlockSpec((3, length, 128), lambda h, f: (0, 0, h)),
                       pl.BlockSpec((8, 128), lambda h, f: (0, h))],
            scratch_shapes=[pltpu.VMEM((length, 128), F32), pltpu.VMEM((length, 128), F32)]),
        out_shape=[jax.ShapeDtypeStruct((3, length, pairs * 128), BF16),
                   jax.ShapeDtypeStruct((8, pairs * 128), F32)],
        compiler_params=pltpu.CompilerParams(vmem_limit_bytes=VMEM_CAP),
        cost_estimate=cost(1 + 6 * pairs),
        name="attend_backward",
    )(flags, queries, key_rows, value_rows, upstream, log_sums)


def unpack_kernel(place_ref, rows_ref, *refs):
    own_ref, send_ref = refs[-2:]
    packed = rows_ref[...]
    packed = packed.reshape(packed.shape[0] * 2, packed.shape[2])
    shape = (packed.shape[0], D)
    row = lax.broadcasted_iota(jnp.int32, shape, 0)
    column = lax.broadcasted_iota(jnp.int32, shape, 1)
    pick = lambda seq: dot_tn(packed, jnp.where(row == 2 * column + seq, 1.0, 0.0).astype(BF16)).astype(BF16)
    count = own_ref.shape[0]
    send_ref[pl.ds(0, count), :] = pick(1 - place_ref[0])
    if len(refs) > 2:
        send_ref[pl.ds(count, refs[0].shape[0]), :] = refs[0][...]
    own_ref[...] = pick(place_ref[0])


def unpack_rows(place, rows, *extra):
    packed = rows.transpose(2, 0, 1)
    count = rows.shape[1]
    counts = [count, count + sum(value.shape[0] for value in extra)]
    fixed = lambda value: pl.BlockSpec(value.shape, lambda i, s: (0,) * len(value.shape))
    return pl.pallas_call(
        unpack_kernel,
        grid_spec=pltpu.PrefetchScalarGridSpec(
            num_scalar_prefetch=1, grid=(1,),
            in_specs=[fixed(packed)] + [fixed(value) for value in extra],
            out_specs=[pl.BlockSpec((n, D), lambda i, s: (0, 0)) for n in counts]),
        out_shape=[jax.ShapeDtypeStruct((n, D), BF16) for n in counts],
        compiler_params=pltpu.CompilerParams(vmem_limit_bytes=VMEM_CAP),
        cost_estimate=cost(5),
        name="unpack_rows",
    )(place, packed, *extra)


def decompress(compact):
    total = jnp.sum(compact, axis=-1, keepdims=True)
    return jnp.where(lane_of(compact.shape) == D - 1, -total, compact)


def crms_back(normal, factor, gain, grad):
    scaled = gain * grad
    du = factor * (scaled - normal * jnp.mean(scaled * normal, axis=-1, keepdims=True))
    lane = lane_of(du.shape)
    last = jnp.sum(jnp.where(lane == D - 1, du, 0.0), axis=-1, keepdims=True)
    return jnp.where(lane == D - 1, 0.0, du - last)


def crms_normal(compact):
    full = decompress(compact)
    factor = lax.rsqrt(jnp.mean(full * full, axis=-1, keepdims=True) + EPSILON)
    return full * factor, factor


def project_kernel(place_ref, own_ref, other_ref, gain_ref, bias_ref, w_own, w_quarter,
                   normed_ref, q_ref, k_ref, v_ref, weight, sems, *, steps):
    at = pl.program_id(0)
    quarter = D // 4
    half = w_own.shape[2]

    def copies():
        out = [pltpu.make_async_copy(w_own, weight.at[:, :, pl.ds(0, half)], sems.at[0])]
        for rel in range(4):
            place = pl.multiple_of((place_ref[1] ^ rel) * quarter, quarter)
            out.append(pltpu.make_async_copy(
                w_quarter[rel], weight.at[:, pl.ds(place, quarter), pl.ds(half, half)],
                sems.at[rel + 1]))
        return out

    @pl.when(at == 0)
    def _():
        for copy in copies():
            copy.start()

    compact = jnp.where(at < steps // 2, own_ref[...], other_ref[...]).astype(F32)
    normal, _ = crms_normal(compact)
    normed = (normal * gain_ref[...]).astype(BF16)
    normed_ref[...] = normed

    @pl.when(at == 0)
    def _():
        for copy in copies():
            copy.wait()

    q_ref[...] = ((dot_nn(normed, weight[0]) + bias_ref[0:1, :]).astype(BF16).astype(F32)
                  * HD ** (-0.5)).astype(BF16)
    k_ref[...] = dot_nn(normed, weight[1]).astype(BF16)
    v_ref[...] = (dot_nn(normed, weight[2]) + bias_ref[1:2, :]).astype(BF16)


def row_maps(steps):
    half = steps // 2
    own = lambda i, s: (jnp.minimum(i, half - 1), 0)
    other = lambda i, s: (jnp.maximum(i - half, 0), 0)
    whole = lambda i, s: (jnp.where(i < half, s[0] * half + i, (1 - s[0]) * half + i - half), 0)
    return own, other, whole


ANY = pl.BlockSpec(memory_space=pl.ANY)


def project(place, own, other, gain, bias, w_own, w_quarter, steps=4):
    length = own.shape[0] * 2
    block = length // steps
    own_map, other_map, whole_map = row_maps(steps)
    fixed = lambda i, s: (0, 0)
    wide = pl.BlockSpec((block, D), whole_map)
    out = jax.ShapeDtypeStruct((length, D), BF16)

    def body(place_ref, own_ref, other_ref, gain_ref, bias_ref, w_own, a, b, c, d, *rest):
        project_kernel(place_ref, own_ref, other_ref, gain_ref, bias_ref, w_own, (a, b, c, d),
                       *rest, steps=steps)

    return pl.pallas_call(
        body,
        grid_spec=pltpu.PrefetchScalarGridSpec(
            num_scalar_prefetch=1, grid=(steps,),
            in_specs=[pl.BlockSpec((block, D), own_map), pl.BlockSpec((block, D), other_map),
                      pl.BlockSpec((1, D), fixed), pl.BlockSpec((2, D), fixed)] + [ANY] * 5,
            out_specs=[wide] * 4,
            scratch_shapes=[pltpu.VMEM((3, D, D), BF16), pltpu.SemaphoreType.DMA((5,))]),
        out_shape=[out] * 4,
        compiler_params=pltpu.CompilerParams(vmem_limit_bytes=VMEM_CAP),
        cost_estimate=cost(10),
        name="norm_project",
    )(place, own, other, gain, bias, w_own, *w_quarter)


SQRT_2_PI = 0.7978845608028654


def gelu_pair(v):
    square = v * v
    inner = v * (SQRT_2_PI + (SQRT_2_PI * 0.044715) * square)
    tanh = jnp.tanh(inner)
    cdf = 0.5 + 0.5 * tanh
    slope = SQRT_2_PI + (3 * SQRT_2_PI * 0.044715) * square
    back = cdf + (0.5 * v) * (1.0 - tanh * tanh) * slope
    return v * cdf, back


def middle_kernel(place_ref, att_ref, res_own, res_other, cot_own, cot_other, gain_ref, end_ref,
                  fcb_ref, weights, two_ref, active_ref, hidden_ref, own_out, send_first, send_second,
                  mid_ref, branch_ref, upgrad_ref, sums_ref, own_sums, other_sums,
                  out_w, fc_w, proj_w, sems, *, steps, chunk):
    at = pl.program_id(0)
    hid = fc_w.shape[1]
    half = hid // 2
    o_own, f_own, p_own, quarters, proj_quarters = weights

    def copies(which):
        if which == 0:
            own, target = o_own, out_w.at[pl.ds(0, D // 2), :]
        elif which == 1:
            own, target = f_own, fc_w.at[:, pl.ds(0, half)]
        else:
            own, target = p_own, proj_w.at[pl.ds(0, half), :]
        out = [pltpu.make_async_copy(own, target, sems.at[which, 0])]
        for rel in range(4):
            source = proj_quarters[rel] if which == 2 else quarters[rel]
            to = place_ref[2 if which == 2 else 1] ^ rel
            if which == 0:
                moves = [(0, D // 8, out_w, D // 2 + to * (D // 8), None)]
            elif which == 1:
                moves = [(D // 8 + n * (D // 4), D // 4, fc_w, to * (D // 4), half + n * D)
                         for n in range(half // D)]
            else:
                moves = [(0, half // 4, proj_w, half + to * (half // 4), None)]
            for n, (start, rows, into, row, col) in enumerate(moves):
                spot = pl.ds(pl.multiple_of(row, rows), rows)
                out.append(pltpu.make_async_copy(
                    source.at[pl.ds(start, rows), :],
                    into.at[spot, :] if col is None else into.at[spot, pl.ds(col, D)],
                    sems.at[which, 1 + 2 * rel + n]))
        return out

    @pl.when(at == 0)
    def _():
        for which in range(3):
            for copy in copies(which):
                copy.start()
        for ref in (sums_ref, own_sums, other_sums):
            ref[...] = jnp.zeros_like(ref)
        for copy in copies(0):
            copy.wait()

    mine = at < steps // 2
    compact = jnp.where(mine, res_own[...], res_other[...]).astype(F32)
    cot_low = jnp.where(mine, cot_own[...], cot_other[...])
    middle = compact + dot_nn(att_ref[...], out_w[...]) + end_ref[0:1, :]
    normal, factor = crms_normal(middle)
    gain = gain_ref[...]
    two = (normal * gain).astype(BF16)
    two_ref[...] = two

    @pl.when(at == 0)
    def _():
        for which in (1, 2):
            for copy in copies(which):
                copy.wait()

    mlp = jnp.zeros((two.shape[0], D), F32)
    two_grad = jnp.zeros((two.shape[0], D), F32)
    for start in range(0, hid, chunk):
        cols = pl.ds(start, chunk)
        pre = dot_nn(two, fc_w[:, cols]) + fcb_ref[0:1, cols]
        act, slope = gelu_pair(pre)
        act = act.astype(BF16)
        active_ref[:, cols] = act
        mlp = mlp + dot_nn(act, proj_w[cols, :])
        hidden = (dot_nt(cot_low, proj_w[cols, :]) * slope).astype(BF16)
        hidden_ref[:, cols] = hidden
        to = own_sums if start < half else other_sums
        to[0:1, pl.ds(start % half, chunk)] += column_sum(hidden.astype(F32))
        two_grad = two_grad + dot_nt(hidden, fc_w[:, cols])
    block_out = (middle + mlp + end_ref[1:2, :]).astype(BF16)

    @pl.when(mine)
    def _():
        own_out[...] = block_out

    @pl.when(at == steps // 2)
    def _():
        send_first[...] = block_out

    @pl.when(at == steps // 2 + 1)
    def _():
        send_second[...] = block_out

    cot = cot_low.astype(F32)
    mid_grad = cot + crms_back(normal, factor, gain, two_grad)
    mid_ref[...] = mid_grad
    branch = mid_grad.astype(BF16)
    branch_ref[...] = branch
    upgrad_ref[...] = dot_nt(branch, out_w[...]).astype(BF16)
    sums_ref[0:1, :] += column_sum(two_grad * normal)
    sums_ref[1:2, :] += column_sum(branch.astype(F32))
    sums_ref[2:3, :] += column_sum(cot)


def middle_stage(place, att, res_own, res_other, cot_own, cot_other, gain, end_bias, fc_bias, weights,
                 steps=4, chunk=768):
    length = att.shape[0]
    hid = fc_bias.shape[1]
    block = length // steps
    own_map, other_map, whole_map = row_maps(steps)
    fixed = lambda i, s: (0, 0)
    flat = [*weights[:3], *weights[3], *weights[4]]
    spec = lambda w, m: pl.BlockSpec((block, w), m)

    def body(place_ref, *refs):
        ins, rest = refs[:8], refs[8:]
        w, rest = rest[:11], rest[11:]
        packed = (*w[:3], w[3:7], w[7:])
        middle_kernel(place_ref, *ins, packed, *rest, steps=steps, chunk=chunk)

    sd = jax.ShapeDtypeStruct
    return pl.pallas_call(
        body,
        grid_spec=pltpu.PrefetchScalarGridSpec(
            num_scalar_prefetch=1, grid=(steps,),
            in_specs=[spec(D, whole_map), spec(D, own_map), spec(D, other_map), spec(D, own_map),
                      spec(D, other_map), pl.BlockSpec((1, D), fixed), pl.BlockSpec((2, D), fixed),
                      pl.BlockSpec((1, hid), fixed)] + [ANY] * 11,
            out_specs=[spec(D, whole_map), spec(hid, whole_map), spec(hid, whole_map),
                       spec(D, own_map), spec(D, fixed), spec(D, fixed),
                       spec(D, whole_map), spec(D, whole_map), spec(D, whole_map),
                       pl.BlockSpec((8, D), fixed), pl.BlockSpec((8, hid // 2), fixed),
                       pl.BlockSpec((8, hid // 2), fixed)],
            scratch_shapes=[pltpu.VMEM((D, D), BF16), pltpu.VMEM((D, hid), BF16),
                            pltpu.VMEM((hid, D), BF16), pltpu.SemaphoreType.DMA((3, 9))]),
        out_shape=[sd((length, D), BF16), sd((length, hid), BF16), sd((length, hid), BF16),
                   sd((length // 2, D), BF16), sd((block, D), BF16), sd((block, D), BF16),
                   sd((length, D), F32), sd((length, D), BF16), sd((length, D), BF16),
                   sd((8, D), F32), sd((8, hid // 2), F32), sd((8, hid // 2), F32)],
        compiler_params=pltpu.CompilerParams(vmem_limit_bytes=VMEM_CAP),
        cost_estimate=cost(38),
        name="middle_stage",
    )(place, att, res_own, res_other, cot_own, cot_other, gain, end_bias, fc_bias, *flat)


def fc_out_grad_kernel(place_ref, left_ref, right_ref, att_ref, branch_ref, keep_ref, send_ref, rest, *, rows, parts):
    at = pl.program_id(0)
    flip = (place_ref[1] & 1) == 1
    out_rows = att_ref.shape[1] // 4

    @pl.when(at == 0)
    def _():
        rest[...] = dot_tn_halves(att_ref, branch_ref).astype(BF16)

    both = dot_tn_halves(left_ref, right_ref).astype(BF16)
    strip = out_rows // parts
    for pair in range(2):
        to = pair ^ (place_ref[1] >> 1)
        low, high = both[2 * pair * rows : (2 * pair + 1) * rows], both[(2 * pair + 1) * rows : (2 * pair + 2) * rows]
        keep_ref[to, pl.ds(0, rows), :] = jnp.where(flip, high, low)
        send_ref[to, pl.ds(0, rows), :] = jnp.where(flip, low, high)
        base = 2 * pair * out_rows + at * strip
        low = rest[pl.ds(pl.multiple_of(base, strip), strip), :]
        high = rest[pl.ds(pl.multiple_of(base + out_rows, strip), strip), :]
        keep_ref[to, pl.ds(rows, strip), :] = jnp.where(flip, high, low)
        send_ref[to, pl.ds(rows, strip), :] = jnp.where(flip, low, high)


def fc_out_grad(place, left, right, attended, branch, side, chunk=768):
    length, width = left.shape
    rows = width // 4
    half = right.shape[1] // 2
    parts = half // chunk
    att = attended.shape[1] // 2
    strip = att // 4 // parts
    out = jax.ShapeDtypeStruct((2, rows + strip, half), BF16)
    out_spec = pl.BlockSpec((2, rows + strip, chunk), lambda n, s: (0, 0, n))
    fixed = lambda value: pl.BlockSpec(value.shape, lambda n, s: (0, 0))
    return pl.pallas_call(
        functools.partial(fc_out_grad_kernel, rows=rows, parts=parts),
        grid_spec=pltpu.PrefetchScalarGridSpec(
            num_scalar_prefetch=1, grid=(parts,),
            in_specs=[fixed(left), pl.BlockSpec((length, chunk), lambda n, s: (0, n + side * parts)),
                      pl.BlockSpec((length, att), lambda n, s: (0, side)), fixed(branch)],
            out_specs=[out_spec, out_spec],
            scratch_shapes=[pltpu.VMEM((att, branch.shape[1]), BF16)]),
        out_shape=[out, out],
        compiler_params=pltpu.CompilerParams(vmem_limit_bytes=VMEM_CAP),
        cost_estimate=cost(7),
        name="fc_out_grad",
    )(place, left, right, attended, branch)


def qkv_grad_kernel(place_ref, left_ref, *refs, rows, parts, pieces):
    right_refs, weight_refs = refs[:parts], refs[parts : parts + pieces]
    keep_ref, send_ref, sum_ref, total = refs[parts + pieces :]
    flip = (place_ref[1] & 1) == 1
    half = left_ref.shape[0] // 2
    width = sum(ref.shape[2] for ref in right_refs)
    both = None
    for n in range(2):
        part = pl.ds(n * half, half)
        right = jnp.concatenate([ref[c, part, :] for c in range(3) for ref in right_refs], axis=1)
        here = dot_tn(left_ref[part, :], right)
        both = here if both is None else both + here
    low_both = both.astype(BF16)
    for pair in range(2):
        to = pair ^ (place_ref[1] >> 1)
        for c in range(3):
            cols = slice(c * width, (c + 1) * width)
            low = low_both[2 * pair * rows : (2 * pair + 1) * rows, cols]
            high = low_both[(2 * pair + 1) * rows : (2 * pair + 2) * rows, cols]
            keep_ref[to, c] = jnp.where(flip, high, low)
            send_ref[to, c] = jnp.where(flip, low, high)
    sum_ref[...] = jnp.zeros_like(sum_ref)
    if pieces > 1:
        total[...] = both
    span = both.shape[0] // pieces
    for n in range(pieces):
        at = pl.multiple_of((place_ref[1] ^ n) * span, span) if pieces > 1 else 0
        folded = jnp.zeros((span, 128), F32)
        for c in range(3):
            here = total[pl.ds(at, span), pl.ds(c * width, width)] if pieces > 1 else both[:, c * width : (c + 1) * width]
            product = here * weight_refs[n][c].astype(F32)
            for k in range(0, width, 128):
                folded = folded + product[:, k : k + 128]
        total[pl.ds(at, span), pl.ds(0, 128)] = folded
    sum_ref[0:1, :] = column_sum(jnp.transpose(total[:, 0:128]))


def qkv_grad(place, left, rights, weights, col_at=0):
    length, width = left.shape
    rows = width // 4
    cols = sum(value.shape[2] for value in rights)
    out = jax.ShapeDtypeStruct((2, 3, rows, cols), BF16)
    whole = lambda value: pl.BlockSpec(value.shape, lambda i, s: (0,) * len(value.shape))
    sums = jax.ShapeDtypeStruct((8, width), F32)
    return pl.pallas_call(
        functools.partial(qkv_grad_kernel, rows=rows, parts=len(rights), pieces=len(weights)),
        grid_spec=pltpu.PrefetchScalarGridSpec(
            num_scalar_prefetch=1, grid=(1,),
            in_specs=[whole(value) for value in (left, *rights)]
            + [pl.BlockSpec((3, value.shape[1], cols), lambda i, s: (0, 0, col_at)) for value in weights],
            out_specs=[whole(out), whole(out), whole(sums)],
            scratch_shapes=[pltpu.VMEM((width, 3 * cols), F32)]),
        out_shape=[out, out, sums],
        compiler_params=pltpu.CompilerParams(vmem_limit_bytes=VMEM_CAP),
        cost_estimate=cost(6.5),
        name="qkv_grad",
    )(place, left, *rights, *weights)


def proj_grad_kernel(place_ref, own_act, other_act, own_cot, other_cot, keep_ref, send_ref, *, rows):
    flip = (place_ref[1] & 1) == 1
    both = (dot_tn(own_act[...], own_cot[...]) + dot_tn(other_act[...], other_cot[...])).astype(BF16)
    low, high = both[:rows], both[rows:]
    keep_ref[0, 0] = jnp.where(flip, high, low)
    send_ref[0, 0] = jnp.where(flip, low, high)


def proj_grad(place, active, cot_own, cot_other):
    length, width = active.shape
    rows = width // 8
    out = jax.ShapeDtypeStruct((2, 2, rows, D), BF16)
    out_spec = pl.BlockSpec((1, 1, rows, D), lambda n, j, s: (j ^ (s[1] >> 1), n, 0, 0))
    cot_spec = pl.BlockSpec((length // 2, D), lambda n, j, s: (0, 0))
    return pl.pallas_call(
        functools.partial(proj_grad_kernel, rows=rows),
        grid_spec=pltpu.PrefetchScalarGridSpec(
            num_scalar_prefetch=1, grid=(2, 2),
            in_specs=[pl.BlockSpec((length // 2, 2 * rows), lambda n, j, s: (s[0], n * 2 + j)),
                      pl.BlockSpec((length // 2, 2 * rows), lambda n, j, s: (1 - s[0], n * 2 + j)),
                      cot_spec, cot_spec],
            out_specs=[out_spec, out_spec]),
        out_shape=[out, out],
        compiler_params=pltpu.CompilerParams(vmem_limit_bytes=VMEM_CAP),
        cost_estimate=cost(13),
        name="proj_grad",
    )(place, active, active, cot_own, cot_other)


def input_grad_kernel(place_ref, own_grads, other_grads, res_own, res_other, mid_ref, gain_ref, w_own, w_quarter,
                      own_out, send_out, weight, sems, *, steps):
    at = pl.program_id(0)
    quarter = D // 4
    half = w_own.shape[2]

    def copies():
        out = []
        for c in range(3):
            out.append(pltpu.make_async_copy(
                w_own.at[c], weight.at[:, pl.ds(c * half, half)], sems.at[c, 0]))
            for rel in range(4):
                place = pl.multiple_of((place_ref[1] ^ rel) * quarter, quarter)
                out.append(pltpu.make_async_copy(
                    w_quarter[rel].at[c], weight.at[pl.ds(place, quarter), pl.ds((3 + c) * half, half)],
                    sems.at[c, rel + 1]))
        return out

    @pl.when(at == 0)
    def _():
        for copy in copies():
            copy.start()

    mine = at < steps // 2
    compact = jnp.where(mine, res_own[...], res_other[...]).astype(F32)
    normal, factor = crms_normal(compact)

    @pl.when(at == 0)
    def _():
        for copy in copies():
            copy.wait()

    left = jnp.concatenate([ref[c] for part in (own_grads, other_grads) for c in range(3) for ref in part], axis=1)
    grad = dot_nt(left, weight[...])
    result = (mid_ref[...] + crms_back(normal, factor, gain_ref[...], grad)).astype(BF16)

    @pl.when(mine)
    def _():
        own_out[...] = result

    @pl.when(jnp.logical_not(mine))
    def _():
        send_out[...] = result


def input_grad(place, own_grads, other_grads, res_own, res_other, mid, gain, w_own, w_quarter, steps=4):
    length = mid.shape[0]
    block = length // steps
    own_map, other_map, whole_map = row_maps(steps)
    fixed = lambda i, s: (0, 0)
    mine, many = len(own_grads), len(own_grads) + len(other_grads)
    grad_spec = lambda value: pl.BlockSpec((3, block, value.shape[2]), lambda i, s: (0, whole_map(i, s)[0], 0))

    def body(place_ref, *refs):
        rest = refs[many:]
        input_grad_kernel(place_ref, refs[:mine], refs[mine:many], *rest[:5], rest[5:9], *rest[9:], steps=steps)

    sd = jax.ShapeDtypeStruct
    return pl.pallas_call(
        body,
        grid_spec=pltpu.PrefetchScalarGridSpec(
            num_scalar_prefetch=1, grid=(steps,),
            in_specs=[grad_spec(value) for value in (*own_grads, *other_grads)] + [pl.BlockSpec((block, D), own_map), pl.BlockSpec((block, D), other_map),
                      pl.BlockSpec((block, D), whole_map), pl.BlockSpec((1, D), fixed)] + [ANY] * 5,
            out_specs=[pl.BlockSpec((block, D), own_map), pl.BlockSpec((block, D), other_map)],
            scratch_shapes=[pltpu.VMEM((D, 3 * D), BF16), pltpu.SemaphoreType.DMA((3, 5))]),
        out_shape=[sd((length // 2, D), BF16), sd((length // 2, D), BF16)],
        compiler_params=pltpu.CompilerParams(vmem_limit_bytes=VMEM_CAP),
        cost_estimate=cost(9),
        name="input_grad",
    )(place, *own_grads, *other_grads, res_own, res_other, mid, gain, w_own, *w_quarter)


def swap(value, axis, bit, size):
    return lax.ppermute(value, axis, [(n, n ^ bit) for n in range(size)])


def meet(*values):
    return lax.optimization_barrier(values)


def add_low(*values):
    total = values[0].astype(F32)
    for value in values[1:]:
        total = total + value.astype(F32)
    return total.astype(BF16)


def chain_in(value):
    return lax.ppermute(value, "group", [(0, 1), (3, 2)])


def chain_across(value):
    return lax.ppermute(value, "group", [(1, 2), (2, 1)])


def chain_out(value):
    return lax.ppermute(value, "group", [(1, 0), (2, 3)])


def on_device(sizes, residual_in, piece_ids, norm_gains, qkv_weight, qv_bias, out_weight, fc_weight,
              fc_bias, proj_weight, out_biases, cotangent):
    n_dp, n_group, n_tensor = sizes["dp"], sizes["group"], sizes["tensor"]
    dp_at = lax.axis_index("dp")
    group_at = lax.axis_index("group")
    tensor_at = lax.axis_index("tensor")
    quarter_at = dp_at & 3
    proj_at = (dp_at & 1) | ((group_at & 1) << 1)
    place = jnp.stack([tensor_at, quarter_at, proj_at]).astype(jnp.int32)
    pad = ((0, 0), (0, 1))
    half = qv_bias.shape[1]
    hid = fc_bias.shape[0]
    pairs = half // 128
    y_swap = lambda value: swap(value, "tensor", 1, n_tensor)
    x_swap = lambda value: swap(value, "dp", 2, n_dp)
    c_swap = lambda value: swap(value, "dp", 1, n_dp)
    z_swap = lambda value: swap(value, "group", 1, n_group)

    def piece_of(shard, dim, at):
        rows = shard.shape[dim] // 4
        return lax.dynamic_slice_in_dim(shard, at * rows, rows, dim)

    qkv_piece = piece_of(qkv_weight, 1, quarter_at)
    qkv_y = y_swap(qkv_piece)
    bias_rows = jnp.concatenate([fc_bias.reshape(-1, D), qv_bias.reshape(1, D), jnp.zeros((13, D), BF16)], 0)
    res_own, res_send = unpack_rows(after(place, qkv_piece), residual_in, bias_rows)
    qkv_y, res_own, res_send, out_gated, fc_gated, proj_gated = meet(
        qkv_y, res_own, res_send, out_weight, fc_weight, proj_weight)
    res_other = y_swap(res_send)
    qkv_x = x_swap(qkv_y)
    qkv_c = c_swap(qkv_y)
    fc_piece = piece_of(fc_gated, 0, quarter_at)
    mix = jnp.concatenate([jnp.pad(piece_of(out_gated, 0, quarter_at), pad)]
                          + [fc_piece[:, n : n + D] for n in range(0, hid, D)], 0)
    proj_piece = jnp.pad(piece_of(proj_gated, 0, proj_at), pad)
    qkv_c, mix, proj_piece = meet(qkv_c, mix, proj_piece)
    mix_y, proj_y = y_swap(mix), y_swap(proj_piece)
    cot_own, cot_send = unpack_rows(after(place, mix, proj_piece), cotangent)
    out_own = jnp.pad(out_gated, pad)
    proj_own = jnp.pad(proj_gated, pad)
    qkv_x, res_other, out_own, proj_own, cot_send = meet(qkv_x, res_other, out_own, proj_own, cot_send)
    qkv_cx = c_swap(qkv_x)
    qkv_others = (qkv_y, qkv_c, qkv_x, qkv_cx)

    gains = norm_gains.astype(F32)
    end_biases = jnp.pad(out_biases, pad).astype(F32)
    count = residual_in.shape[1]
    bias_other = res_other[count : count + 8].astype(F32)
    fc_rows = hid // D
    qv_full = jnp.concatenate([qv_bias.astype(F32), bias_other[fc_rows].reshape(2, half)], axis=1)
    fc_full = jnp.concatenate([fc_bias.astype(F32).reshape(1, -1), bias_other[:fc_rows].reshape(1, -1)], axis=1)
    length = piece_ids.shape[1]
    flags = (lax.dynamic_index_in_dim(piece_ids, tensor_at, 0, keepdims=False)[:: length // 4] >= 0)
    flags = flags.astype(jnp.int32)

    normed_one, queries, key_rows, value_rows = project(
        place, res_own, res_other, gains[0:1], qv_full, qkv_weight, qkv_others)
    queries, cot_send = meet(queries, cot_send)
    cot_other = y_swap(cot_send)
    attended = attend_forward(flags, queries, key_rows, value_rows, 0, pairs)
    *attended, queries, mix_y, proj_y = meet(*attended, queries, mix_y, proj_y)
    mix_x, mix_c = x_swap(mix_y), c_swap(mix_y)
    proj_x, proj_c = z_swap(proj_y), c_swap(proj_y)
    attended = attend_forward(flags, queries, key_rows, value_rows, pairs, pairs, attended)
    attended, log_sums, mix_x, proj_x, cot_other = meet(*attended, mix_x, proj_x, cot_other)
    mix_others = (mix_y, mix_c, mix_x, c_swap(mix_x))
    proj_others = (proj_y, proj_c, proj_x, c_swap(proj_x))

    (normed_two, active, hidden_grad, out_mine, *out_send, middle_grad, branch_grad, attended_grad,
     middle_sums, own_sums, other_sums) = middle_stage(
        place, attended, res_own, res_other, cot_own, cot_other, gains[1:2], end_biases, fc_full,
        (out_own, fc_weight, proj_own, mix_others, proj_others))
    backward = functools.partial(attend_backward, flags, queries, key_rows, value_rows)
    restore = lambda mine, got: jnp.where(
        tensor_at == 0, jnp.stack([mine, got]), jnp.stack([got, mine]))[:, :, : D - 1]

    def small_outputs(small):
        part, first = hid // n_dp, half // n_dp
        return (jnp.concatenate([small[0:1, :D], small[0:1, D : 2 * D]], 0),
                lax.dynamic_slice(small, (0, 2 * D + hid + dp_at * first), (2, first)),
                lax.dynamic_slice(small, (0, 2 * D + dp_at * part), (1, part)).reshape(part),
                small[1:3, D : 2 * D - 1])

    if n_dp == 4 and n_group == 4:
        out_got = [y_swap(value) for value in out_send]
        proj_k, proj_s = proj_grad(after(place, middle_sums), active, cot_own, cot_other)
        proj_k, proj_s, out_got[0] = meet(proj_k, proj_s, out_got[0])
        proj_c = c_swap(proj_s)
        weights_of = lambda gate, side: fc_out_grad(
            after(place, gate), normed_two, hidden_grad, attended, branch_grad, side)
        fo_k, fo_s = weights_of(proj_k, 1)
        fo_k, fo_s, proj_k, proj_c = meet(fo_k, fo_s, proj_k, proj_c)
        fo_c = c_swap(fo_s)
        proj_f = add_low(proj_k[1], proj_c[1])
        proj_x = x_swap(proj_f)
        fm_k, fm_s = weights_of(proj_f, 0)
        fm_k, fm_s, fo_k, fo_c, *out_got = meet(fm_k, fm_s, fo_k, fo_c, *out_got)
        fm_c = c_swap(fm_s)
        fc_away = add_low(fo_k, fo_c)
        fc_y = y_swap(fc_away)
        first, first_sums = backward(after(attended_grad, fc_away), log_sums, pairs, pairs)
        first, first_sums, proj_k, proj_c, proj_x, fm_k, fm_c = meet(
            first, first_sums, proj_k, proj_c, proj_x, fm_k, fm_c)
        proj_r = [add_low(proj_k[0, n], proj_c[0, n], proj_x[n]) for n in range(2)]
        proj_y = y_swap(proj_r[1])
        qo_k, qo_s, qo_sum = qkv_grad(after(place, proj_r[1]), normed_one, [first], qkv_others)
        qo_k, qo_s, fm_k, fm_c, fc_y = meet(qo_k, qo_s, fm_k, fm_c, fc_y)
        qo_c = c_swap(qo_s)
        fc_far = add_low(fm_k[1], fm_c[1], fc_y[1])
        fc_x = x_swap(fc_far)
        own_a, sums_a = backward(after(attended_grad, fc_far), log_sums, 0, pairs - 1)
        own_a, sums_a, proj_y, fc_x, qo_k, qo_c = meet(own_a, sums_a, proj_y, fc_x, qo_k, qo_c)
        proj_shard = add_low(proj_r[0], proj_y)
        proj_z = chain_in(proj_shard)
        fc_shard = add_low(fm_k[0], fm_c[0], fc_y[0], fc_x)
        fc_z = chain_in(fc_shard)
        qo_f = add_low(qo_k[1], qo_c[1])
        qo_x = x_swap(qo_f)
        own_b, sums_b = backward(after(attended_grad, qo_f, proj_shard, fc_shard), log_sums, pairs - 1, 1)
        qm_k, qm_s, qm_sum = qkv_grad(after(place, own_b), normed_one, [own_a, own_b], [qkv_weight])
        qm_k, qm_s, qm_sum, qo_k, qo_c, qo_x, proj_shard, proj_z = meet(
            qm_k, qm_s, qm_sum, qo_k, qo_c, qo_x, proj_shard, proj_z)
        qm_c = c_swap(qm_s)
        qo_r = add_low(qo_k[0], qo_c[0], qo_x)
        qo_y = y_swap(qo_r)
        proj_shard = add_low(proj_shard, proj_z)
        proj_z = chain_across(proj_shard)
        in_sums = (qm_sum + qo_sum) / gains[0:1]
        small = jnp.concatenate([in_sums, middle_sums, own_sums, sums_a, sums_b], 1)
        small_y = y_swap(jnp.concatenate([in_sums, middle_sums, other_sums, first_sums], 1))
        qm_k, qm_c, qo_r, proj_shard, small, small_y = meet(qm_k, qm_c, qo_r, proj_shard, small, small_y)
        qm_f = add_low(qm_k[1], qm_c[1])
        qm_x = x_swap(qm_f)
        small = small + small_y
        small_c = c_swap(small)
        in_mine, in_send = input_grad(
            after(place, qm_f, small), [own_a, own_b], [first], res_own, res_other, middle_grad, gains[0:1],
            qkv_weight, qkv_others)
        in_mine, in_send, qm_x, qo_y, fc_shard, fc_z, proj_shard, proj_z, small, small_c = meet(
            in_mine, in_send, qm_x, qo_y, fc_shard, fc_z, proj_shard, proj_z, small, small_c)
        last = add_low(qm_k[0], qm_c[0], qm_x, qo_y)
        last_z = z_swap(last)
        fc_shard = add_low(fc_shard, fc_z)
        fc_z = chain_across(fc_shard)
        proj_shard = add_low(proj_shard, proj_z)
        proj_z = chain_out(proj_shard)
        in_got = y_swap(in_send)
        small = small + small_c
        small_x = x_swap(small)
        block_out = restore(after(out_mine, last, fc_shard, proj_shard, small), jnp.concatenate(out_got, 0))
        last, last_z, block_out, small, small_x = meet(last, last_z, block_out, small, small_x)
        low_part, high_part = add_low(last[:2], last_z[:2]), add_low(last[2:], last_z[2:])
        low_z = swap(low_part, "group", 2, n_group)
        high_z = swap(high_part, "group", 2, n_group)
        small = small + small_x
        small_z = z_swap(small)
        middle_one = (group_at == 1) | (group_at == 2)
        fc_shard, fc_z, proj_shard, proj_z, in_mine, in_got, low_part, low_z, small, small_z = meet(
            fc_shard, fc_z, proj_shard, proj_z, in_mine, in_got, low_part, low_z, small, small_z)
        fc_shard = add_low(fc_shard, fc_z)
        fc_z = chain_out(fc_shard)
        small = small + small_z
        small_z = swap(small, "group", 2, n_group)
        in_out = restore(after(in_mine, fc_shard, small), in_got)
        proj_shard = jnp.where(middle_one, proj_shard, proj_z)[:, : D - 1].astype(F32)
        low_part = add_low(low_part, low_z).astype(F32)
        in_out, proj_shard, low_part, small, small_z = meet(in_out, proj_shard, low_part, small, small_z)
        small = small_outputs(small + small_z)
        high_part, high_z, in_out, proj_shard, low_part, fc_shard, fc_z, *small = meet(
            high_part, high_z, in_out, proj_shard, low_part, fc_shard, fc_z, *small)
        qkv_shard = jnp.concatenate([low_part, add_low(high_part, high_z).astype(F32)], 0)
        fc_shard = jnp.where(middle_one, fc_shard, fc_z).astype(F32)
        rest = fc_shard[D // 4 :]
        out_shard = jnp.concatenate([rest[:, n : n + D - 1] for n in range(0, hid, D)], 0)
        fc_shard = fc_shard[: D // 4]
    else:
        first, first_sums = backward(attended_grad, log_sums, pairs, pairs)
        own, second_sums = backward(attended_grad, log_sums, 0, pairs)
        in_mine, in_send = input_grad(
            place, [own], [first], res_own, res_other, middle_grad, gains[0:1], qkv_weight, qkv_others)
        in_out = restore(in_mine, y_swap(in_send))
        block_out = restore(out_mine, y_swap(jnp.concatenate(out_send, 0)))
        qo_sum = qkv_grad(place, normed_one, [first], qkv_others)[2]
        qm_sum = qkv_grad(place, normed_one, [own], [qkv_weight])[2]

        def scatter(own, other):
            total = [lax.psum_scatter(value.astype(BF16), "dp", scatter_dimension=0, tiled=True)
                     for value in (own, other)]
            return lax.psum(add_low(total[0], y_swap(total[1])), "group")

        cot_rows = jnp.where(tensor_at == 0, jnp.concatenate([cot_own, cot_other]),
                             jnp.concatenate([cot_other, cot_own]))
        proj_shard = scatter(dot_tn(active[:, :hid], cot_rows), dot_tn(active[:, hid:], cot_rows))
        fc_shard = scatter(dot_tn(normed_two, hidden_grad[:, :hid]), dot_tn(normed_two, hidden_grad[:, hid:]))
        out_shard = scatter(dot_tn(attended[:, :half], branch_grad), dot_tn(attended[:, half:], branch_grad))
        proj_shard, out_shard = proj_shard[:, : D - 1].astype(F32), out_shard[:, : D - 1].astype(F32)
        fc_shard = fc_shard.astype(F32)
        qkv_shard = jnp.swapaxes(scatter(
            *[jnp.stack([dot_tn(normed_one, part[c]) for c in range(3)], 1) for part in (own, first)]), 0, 1)
        in_sums = (qm_sum + qo_sum) / gains[0:1]
        small = jnp.concatenate([in_sums, middle_sums, own_sums, second_sums], 1)
        small = small + y_swap(jnp.concatenate([in_sums, middle_sums, other_sums, first_sums], 1))
        small = small_outputs(lax.psum(small, ("dp", "group")))

    grad_gains, grad_qv_bias, grad_fc_bias, grad_out_biases = small
    return (
        block_out,
        in_out,
        grad_gains,
        qkv_shard.astype(F32),
        grad_qv_bias,
        out_shard,
        fc_shard,
        grad_fc_bias,
        proj_shard,
        grad_out_biases,
    )


def solution(mesh):
    sizes = dict(mesh.shape)
    in_specs = (
        P(("dp", "group"), "tensor", None),
        P(("dp", "group"), None),
        P(),
        P(None, None, "tensor"),
        P(None, "tensor"),
        P("tensor", None),
        P(None, "tensor"),
        P("tensor"),
        P("tensor", None),
        P(),
        P(("dp", "group"), "tensor", None),
    )
    out_specs = (
        P(("dp", "group"), "tensor", None),
        P(("dp", "group"), "tensor", None),
        P(),
        P(None, "dp", "tensor"),
        P(None, ("tensor", "dp")),
        P(("tensor", "dp"), None),
        P("dp", "tensor"),
        P(("tensor", "dp")),
        P(("tensor", "dp"), None),
        P(),
    )
    return jax.shard_map(
        functools.partial(on_device, sizes), mesh=mesh, in_specs=in_specs, out_specs=out_specs,
        check_vma=False)
```

```python
import functools
import jax
import jax.numpy as jnp
from jax import lax
from jax.sharding import PartitionSpec as P
from jax.experimental import pallas as pl
from jax.experimental.pallas import tpu as pltpu

D = 768
HD = 64
EPSILON = 1e-05
MASKED = -1e30
VMEM_CAP = 60 * 1024 * 1024
F32 = jnp.float32
BF16 = jnp.bfloat16
COST_FLOPS = 0.4e9


def cost(micros):
    return pl.CostEstimate(flops=int(micros * COST_FLOPS), bytes_accessed=int(micros * 4e5), transcendentals=0)


def after(value, *others):
    return lax.optimization_barrier((value, *others))[0]


def dot_nn(a, b):
    return lax.dot_general(a, b, (((1,), (0,)), ((), ())), preferred_element_type=F32)


def dot_nt(a, b):
    return lax.dot_general(a, b, (((1,), (1,)), ((), ())), preferred_element_type=F32)


def dot_tn(a, b):
    return lax.dot_general(a, b, (((0,), (0,)), ((), ())), preferred_element_type=F32)


def dot_tn_halves(left, right):
    half = left.shape[0] // 2
    return (dot_tn(left[pl.ds(0, half), :], right[pl.ds(0, half), :])
            + dot_tn(left[pl.ds(half, half), :], right[pl.ds(half, half), :]))


def column_sum(values):
    return jnp.sum(values, axis=0, keepdims=True)


def lane_of(shape):
    return lax.broadcasted_iota(jnp.int32, shape, len(shape) - 1)


def attend_forward_kernel(flags_ref, q_ref, k_ref, v_ref, out_ref, log_ref, *, block):
    length = q_ref.shape[0]
    key_at = lax.broadcasted_iota(jnp.int32, (block, block), 0)
    query_at = lax.broadcasted_iota(jnp.int32, (block, block), 1)
    causal = key_at <= query_at
    head_lane = lane_of((block, 128)) // HD
    for at in range(length // block):
        rows = pl.ds(at * block, block)
        reach = (at + 1) * block
        keys = pl.ds(0, reach)
        seen = causal | (flags_ref[at] > 0)
        parts = []
        for head in range(2):
            q_head = jnp.where(head_lane == head, q_ref[rows, :], jnp.zeros((block, 128), BF16))
            scores = dot_nt(k_ref[keys, :], q_head)
            last = jnp.where(seen, scores[reach - block :], MASKED)
            scores = last if at == 0 else jnp.concatenate([scores[: reach - block], last], 0)
            top = jnp.max(scores, axis=0, keepdims=True)
            probs = jnp.exp(scores - top)
            total = jnp.sum(probs, axis=0, keepdims=True)
            log_ref[0, pl.ds(head, 1), rows] = top + jnp.log(total)
            probs = (probs * (1.0 / total)).astype(BF16)
            parts.append(dot_tn(probs, v_ref[keys, :]).astype(BF16))
        out_ref[rows, :] = jnp.where(head_lane == 0, parts[0], parts[1])


def attend_forward(flags, queries, key_rows, value_rows, first, pairs, into=None):
    length, width = queries.shape
    block = length // 4
    tile = pl.BlockSpec((length, 128), lambda h, f: (0, h + first))
    more = [] if into is None else list(into)

    def body(flags_ref, q_ref, k_ref, v_ref, *rest):
        attend_forward_kernel(flags_ref, q_ref, k_ref, v_ref, *rest[len(more):], block=block)

    return pl.pallas_call(
        body,
        grid_spec=pltpu.PrefetchScalarGridSpec(
            num_scalar_prefetch=1, grid=(pairs,),
            in_specs=[tile, tile, tile] + [pl.BlockSpec(memory_space=pl.ANY)] * len(more),
            out_specs=[tile, pl.BlockSpec((1, 8, length), lambda h, f: (h + first, 0, 0))]),
        out_shape=[jax.ShapeDtypeStruct((length, width), BF16),
                   jax.ShapeDtypeStruct((width // 128, 8, length), F32)],
        input_output_aliases={4 + n: n for n in range(len(more))},
        compiler_params=pltpu.CompilerParams(vmem_limit_bytes=VMEM_CAP),
        cost_estimate=cost(3.8 * pairs),
        name="attend_forward",
    )(flags, queries, key_rows, value_rows, *more)


def attend_backward_kernel(flags_ref, q_ref, k_ref, v_ref, up_ref, log_ref,
                           grad_ref, sum_ref, dk_acc, dv_acc, *, block):
    length = q_ref.shape[0]
    count = length // block
    key_at = lax.broadcasted_iota(jnp.int32, (block, block), 0)
    query_at = lax.broadcasted_iota(jnp.int32, (block, block), 1)
    causal = key_at <= query_at
    head_lane = lane_of((block, 128)) // HD
    full_lane = lane_of((length, 128)) // HD
    dq_sum = jnp.zeros((1, 128), F32)
    for at in reversed(range(count)):
        rows = pl.ds(at * block, block)
        reach = (at + 1) * block
        keys = pl.ds(0, reach)
        seen = causal | (flags_ref[at] > 0)
        dq = None
        for head in range(2):
            q_head = jnp.where(head_lane == head, q_ref[rows, :], jnp.zeros((block, 128), BF16))
            up_head = jnp.where(head_lane == head, up_ref[rows, :], jnp.zeros((block, 128), BF16))
            logs = log_ref[0, pl.ds(head, 1), rows]
            scores = dot_nt(k_ref[keys, :], q_head)
            last = jnp.where(seen, scores[reach - block :], MASKED)
            scores = last if at == 0 else jnp.concatenate([scores[: reach - block], last], 0)
            probs = jnp.exp(scores - logs)
            along = dot_nt(v_ref[keys, :], up_head)
            inner = jnp.sum(probs * along, axis=0, keepdims=True)
            low_grad = (probs * (along - inner)).astype(BF16)
            dv = dot_nn(probs.astype(BF16), up_head)
            dk = dot_nn(low_grad, q_head)
            if at == count - 1 and head == 0:
                dv_acc[keys, :] = dv
                dk_acc[keys, :] = dk
            else:
                dv_acc[keys, :] += dv
                dk_acc[keys, :] += dk
            k_head = jnp.where(full_lane[:reach] == head, k_ref[keys, :], jnp.zeros((reach, 128), BF16))
            part = dot_tn(low_grad, k_head)
            dq = part if dq is None else dq + part
        low_dq = (dq * HD ** (-0.5)).astype(BF16)
        grad_ref[0, rows, :] = low_dq
        dq_sum = dq_sum + column_sum(low_dq.astype(F32))
    grad_ref[1] = dk_acc[...].astype(BF16)
    low_dv = dv_acc[...].astype(BF16)
    grad_ref[2] = low_dv
    sum_ref[...] = jnp.zeros_like(sum_ref)
    sum_ref[0:1, :] = dq_sum
    sum_ref[1:2, :] = column_sum(low_dv.astype(F32))


def attend_backward(flags, queries, key_rows, value_rows, upstream, log_sums, first, pairs):
    length = queries.shape[0]
    tile = pl.BlockSpec((length, 128), lambda h, f: (0, h + first))
    return pl.pallas_call(
        functools.partial(attend_backward_kernel, block=length // 4),
        grid_spec=pltpu.PrefetchScalarGridSpec(
            num_scalar_prefetch=1, grid=(pairs,),
            in_specs=[tile, tile, tile, tile,
                      pl.BlockSpec((1, 8, length), lambda h, f: (h + first, 0, 0))],
            out_specs=[pl.BlockSpec((3, length, 128), lambda h, f: (0, 0, h)),
                       pl.BlockSpec((8, 128), lambda h, f: (0, h))],
            scratch_shapes=[pltpu.VMEM((length, 128), F32), pltpu.VMEM((length, 128), F32)]),
        out_shape=[jax.ShapeDtypeStruct((3, length, pairs * 128), BF16),
                   jax.ShapeDtypeStruct((8, pairs * 128), F32)],
        compiler_params=pltpu.CompilerParams(vmem_limit_bytes=VMEM_CAP),
        cost_estimate=cost(1 + 6 * pairs),
        name="attend_backward",
    )(flags, queries, key_rows, value_rows, upstream, log_sums)


def unpack_kernel(place_ref, rows_ref, *refs):
    own_ref, send_ref = refs[-2:]
    packed = rows_ref[...]
    packed = packed.reshape(packed.shape[0] * 2, packed.shape[2])
    shape = (packed.shape[0], D)
    row = lax.broadcasted_iota(jnp.int32, shape, 0)
    column = lax.broadcasted_iota(jnp.int32, shape, 1)
    pick = lambda seq: dot_tn(packed, jnp.where(row == 2 * column + seq, 1.0, 0.0).astype(BF16)).astype(BF16)
    count = own_ref.shape[0]
    send_ref[pl.ds(0, count), :] = pick(1 - place_ref[0])
    if len(refs) > 2:
        send_ref[pl.ds(count, refs[0].shape[0]), :] = refs[0][...]
    own_ref[...] = pick(place_ref[0])


def unpack_rows(place, rows, *extra):
    packed = rows.transpose(2, 0, 1)
    count = rows.shape[1]
    counts = [count, count + sum(value.shape[0] for value in extra)]
    fixed = lambda value: pl.BlockSpec(value.shape, lambda i, s: (0,) * len(value.shape))
    return pl.pallas_call(
        unpack_kernel,
        grid_spec=pltpu.PrefetchScalarGridSpec(
            num_scalar_prefetch=1, grid=(1,),
            in_specs=[fixed(packed)] + [fixed(value) for value in extra],
            out_specs=[pl.BlockSpec((n, D), lambda i, s: (0, 0)) for n in counts]),
        out_shape=[jax.ShapeDtypeStruct((n, D), BF16) for n in counts],
        compiler_params=pltpu.CompilerParams(vmem_limit_bytes=VMEM_CAP),
        cost_estimate=cost(5),
        name="unpack_rows",
    )(place, packed, *extra)


def decompress(compact):
    total = jnp.sum(compact, axis=-1, keepdims=True)
    return jnp.where(lane_of(compact.shape) == D - 1, -total, compact)


def crms_back(normal, factor, gain, grad):
    scaled = gain * grad
    du = factor * (scaled - normal * jnp.mean(scaled * normal, axis=-1, keepdims=True))
    lane = lane_of(du.shape)
    last = jnp.sum(jnp.where(lane == D - 1, du, 0.0), axis=-1, keepdims=True)
    return jnp.where(lane == D - 1, 0.0, du - last)


def crms_normal(compact):
    full = decompress(compact)
    factor = lax.rsqrt(jnp.mean(full * full, axis=-1, keepdims=True) + EPSILON)
    return full * factor, factor


def project_kernel(place_ref, own_ref, other_ref, gain_ref, bias_ref, w_own, w_quarter,
                   normed_ref, q_ref, k_ref, v_ref, weight, sems, *, steps):
    at = pl.program_id(0)
    quarter = D // 4
    half = w_own.shape[2]

    def copies():
        out = [pltpu.make_async_copy(w_own, weight.at[:, :, pl.ds(0, half)], sems.at[0])]
        for rel in range(4):
            place = pl.multiple_of((place_ref[1] ^ rel) * quarter, quarter)
            out.append(pltpu.make_async_copy(
                w_quarter[rel], weight.at[:, pl.ds(place, quarter), pl.ds(half, half)],
                sems.at[rel + 1]))
        return out

    @pl.when(at == 0)
    def _():
        for copy in copies():
            copy.start()

    compact = jnp.where(at < steps // 2, own_ref[...], other_ref[...]).astype(F32)
    normal, _ = crms_normal(compact)
    normed = (normal * gain_ref[...]).astype(BF16)
    normed_ref[...] = normed

    @pl.when(at == 0)
    def _():
        for copy in copies():
            copy.wait()

    q_ref[...] = ((dot_nn(normed, weight[0]) + bias_ref[0:1, :]).astype(BF16).astype(F32)
                  * HD ** (-0.5)).astype(BF16)
    k_ref[...] = dot_nn(normed, weight[1]).astype(BF16)
    v_ref[...] = (dot_nn(normed, weight[2]) + bias_ref[1:2, :]).astype(BF16)


def row_maps(steps):
    half = steps // 2
    own = lambda i, s: (jnp.minimum(i, half - 1), 0)
    other = lambda i, s: (jnp.maximum(i - half, 0), 0)
    whole = lambda i, s: (jnp.where(i < half, s[0] * half + i, (1 - s[0]) * half + i - half), 0)
    return own, other, whole


ANY = pl.BlockSpec(memory_space=pl.ANY)


def project(place, own, other, gain, bias, w_own, w_quarter, steps=4):
    length = own.shape[0] * 2
    block = length // steps
    own_map, other_map, whole_map = row_maps(steps)
    fixed = lambda i, s: (0, 0)
    wide = pl.BlockSpec((block, D), whole_map)
    out = jax.ShapeDtypeStruct((length, D), BF16)

    def body(place_ref, own_ref, other_ref, gain_ref, bias_ref, w_own, a, b, c, d, *rest):
        project_kernel(place_ref, own_ref, other_ref, gain_ref, bias_ref, w_own, (a, b, c, d),
                       *rest, steps=steps)

    return pl.pallas_call(
        body,
        grid_spec=pltpu.PrefetchScalarGridSpec(
            num_scalar_prefetch=1, grid=(steps,),
            in_specs=[pl.BlockSpec((block, D), own_map), pl.BlockSpec((block, D), other_map),
                      pl.BlockSpec((1, D), fixed), pl.BlockSpec((2, D), fixed)] + [ANY] * 5,
            out_specs=[wide] * 4,
            scratch_shapes=[pltpu.VMEM((3, D, D), BF16), pltpu.SemaphoreType.DMA((5,))]),
        out_shape=[out] * 4,
        compiler_params=pltpu.CompilerParams(vmem_limit_bytes=VMEM_CAP),
        cost_estimate=cost(10),
        name="norm_project",
    )(place, own, other, gain, bias, w_own, *w_quarter)


SQRT_2_PI = 0.7978845608028654


def gelu_pair(v):
    square = v * v
    inner = v * (SQRT_2_PI + (SQRT_2_PI * 0.044715) * square)
    tanh = jnp.tanh(inner)
    cdf = 0.5 + 0.5 * tanh
    slope = SQRT_2_PI + (3 * SQRT_2_PI * 0.044715) * square
    back = cdf + (0.5 * v) * (1.0 - tanh * tanh) * slope
    return v * cdf, back


def middle_kernel(place_ref, att_ref, res_own, res_other, cot_own, cot_other, gain_ref, end_ref,
                  fcb_ref, weights, two_ref, active_ref, hidden_ref, own_out, send_first, send_second,
                  mid_ref, branch_ref, upgrad_ref, sums_ref, own_sums, other_sums,
                  out_w, fc_w, proj_w, sems, *, steps, chunk):
    at = pl.program_id(0)
    hid = fc_w.shape[1]
    half = hid // 2
    o_own, f_own, p_own, quarters, proj_quarters = weights

    def copies(which):
        if which == 0:
            own, target = o_own, out_w.at[pl.ds(0, D // 2), :]
        elif which == 1:
            own, target = f_own, fc_w.at[:, pl.ds(0, half)]
        else:
            own, target = p_own, proj_w.at[pl.ds(0, half), :]
        out = [pltpu.make_async_copy(own, target, sems.at[which, 0])]
        for rel in range(4):
            source = proj_quarters[rel] if which == 2 else quarters[rel]
            to = place_ref[2 if which == 2 else 1] ^ rel
            if which == 0:
                moves = [(0, D // 8, out_w, D // 2 + to * (D // 8), None)]
            elif which == 1:
                moves = [(D // 8 + n * (D // 4), D // 4, fc_w, to * (D // 4), half + n * D)
                         for n in range(half // D)]
            else:
                moves = [(0, half // 4, proj_w, half + to * (half // 4), None)]
            for n, (start, rows, into, row, col) in enumerate(moves):
                spot = pl.ds(pl.multiple_of(row, rows), rows)
                out.append(pltpu.make_async_copy(
                    source.at[pl.ds(start, rows), :],
                    into.at[spot, :] if col is None else into.at[spot, pl.ds(col, D)],
                    sems.at[which, 1 + 2 * rel + n]))
        return out

    @pl.when(at == 0)
    def _():
        for which in range(3):
            for copy in copies(which):
                copy.start()
        for ref in (sums_ref, own_sums, other_sums):
            ref[...] = jnp.zeros_like(ref)
        for copy in copies(0):
            copy.wait()

    mine = at < steps // 2
    compact = jnp.where(mine, res_own[...], res_other[...]).astype(F32)
    cot_low = jnp.where(mine, cot_own[...], cot_other[...])
    middle = compact + dot_nn(att_ref[...], out_w[...]) + end_ref[0:1, :]
    normal, factor = crms_normal(middle)
    gain = gain_ref[...]
    two = (normal * gain).astype(BF16)
    two_ref[...] = two

    @pl.when(at == 0)
    def _():
        for which in (1, 2):
            for copy in copies(which):
                copy.wait()

    mlp = jnp.zeros((two.shape[0], D), F32)
    two_grad = jnp.zeros((two.shape[0], D), F32)
    for start in range(0, hid, chunk):
        cols = pl.ds(start, chunk)
        pre = dot_nn(two, fc_w[:, cols]) + fcb_ref[0:1, cols]
        act, slope = gelu_pair(pre)
        act = act.astype(BF16)
        active_ref[:, cols] = act
        mlp = mlp + dot_nn(act, proj_w[cols, :])
        hidden = (dot_nt(cot_low, proj_w[cols, :]) * slope).astype(BF16)
        hidden_ref[:, cols] = hidden
        to = own_sums if start < half else other_sums
        to[0:1, pl.ds(start % half, chunk)] += column_sum(hidden.astype(F32))
        two_grad = two_grad + dot_nt(hidden, fc_w[:, cols])
    block_out = (middle + mlp + end_ref[1:2, :]).astype(BF16)

    @pl.when(mine)
    def _():
        own_out[...] = block_out

    @pl.when(at == steps // 2)
    def _():
        send_first[...] = block_out

    @pl.when(at == steps // 2 + 1)
    def _():
        send_second[...] = block_out

    cot = cot_low.astype(F32)
    mid_grad = cot + crms_back(normal, factor, gain, two_grad)
    mid_ref[...] = mid_grad
    branch = mid_grad.astype(BF16)
    branch_ref[...] = branch
    upgrad_ref[...] = dot_nt(branch, out_w[...]).astype(BF16)
    sums_ref[0:1, :] += column_sum(two_grad * normal)
    sums_ref[1:2, :] += column_sum(branch.astype(F32))
    sums_ref[2:3, :] += column_sum(cot)


def middle_stage(place, att, res_own, res_other, cot_own, cot_other, gain, end_bias, fc_bias, weights,
                 steps=4, chunk=768):
    length = att.shape[0]
    hid = fc_bias.shape[1]
    block = length // steps
    own_map, other_map, whole_map = row_maps(steps)
    fixed = lambda i, s: (0, 0)
    flat = [*weights[:3], *weights[3], *weights[4]]
    spec = lambda w, m: pl.BlockSpec((block, w), m)

    def body(place_ref, *refs):
        ins, rest = refs[:8], refs[8:]
        w, rest = rest[:11], rest[11:]
        packed = (*w[:3], w[3:7], w[7:])
        middle_kernel(place_ref, *ins, packed, *rest, steps=steps, chunk=chunk)

    sd = jax.ShapeDtypeStruct
    return pl.pallas_call(
        body,
        grid_spec=pltpu.PrefetchScalarGridSpec(
            num_scalar_prefetch=1, grid=(steps,),
            in_specs=[spec(D, whole_map), spec(D, own_map), spec(D, other_map), spec(D, own_map),
                      spec(D, other_map), pl.BlockSpec((1, D), fixed), pl.BlockSpec((2, D), fixed),
                      pl.BlockSpec((1, hid), fixed)] + [ANY] * 11,
            out_specs=[spec(D, whole_map), spec(hid, whole_map), spec(hid, whole_map),
                       spec(D, own_map), spec(D, fixed), spec(D, fixed),
                       spec(D, whole_map), spec(D, whole_map), spec(D, whole_map),
                       pl.BlockSpec((8, D), fixed), pl.BlockSpec((8, hid // 2), fixed),
                       pl.BlockSpec((8, hid // 2), fixed)],
            scratch_shapes=[pltpu.VMEM((D, D), BF16), pltpu.VMEM((D, hid), BF16),
                            pltpu.VMEM((hid, D), BF16), pltpu.SemaphoreType.DMA((3, 9))]),
        out_shape=[sd((length, D), BF16), sd((length, hid), BF16), sd((length, hid), BF16),
                   sd((length // 2, D), BF16), sd((block, D), BF16), sd((block, D), BF16),
                   sd((length, D), F32), sd((length, D), BF16), sd((length, D), BF16),
                   sd((8, D), F32), sd((8, hid // 2), F32), sd((8, hid // 2), F32)],
        compiler_params=pltpu.CompilerParams(vmem_limit_bytes=VMEM_CAP),
        cost_estimate=cost(38),
        name="middle_stage",
    )(place, att, res_own, res_other, cot_own, cot_other, gain, end_bias, fc_bias, *flat)


def fc_grad_kernel(place_ref, left_ref, right_ref, keep_ref, send_ref, *, rows):
    flip = (place_ref[1] & 1) == 1
    both = dot_tn_halves(left_ref, right_ref).astype(BF16)
    for pair in range(2):
        to = pair ^ (place_ref[1] >> 1)
        low, high = both[2 * pair * rows : (2 * pair + 1) * rows], both[(2 * pair + 1) * rows : (2 * pair + 2) * rows]
        keep_ref[to] = jnp.where(flip, high, low)
        send_ref[to] = jnp.where(flip, low, high)


def fc_grad(place, left, right, side, chunk=768):
    length, width = left.shape
    rows = width // 4
    half = right.shape[1] // 2
    parts = half // chunk
    out = jax.ShapeDtypeStruct((2, rows, half), BF16)
    out_spec = pl.BlockSpec((2, rows, chunk), lambda n, s: (0, 0, n))
    return pl.pallas_call(
        functools.partial(fc_grad_kernel, rows=rows),
        grid_spec=pltpu.PrefetchScalarGridSpec(
            num_scalar_prefetch=1, grid=(parts,),
            in_specs=[pl.BlockSpec((length, width), lambda n, s: (0, 0)),
                      pl.BlockSpec((length, chunk), lambda n, s: (0, n + side * parts))],
            out_specs=[out_spec, out_spec]),
        out_shape=[out, out],
        compiler_params=pltpu.CompilerParams(vmem_limit_bytes=VMEM_CAP),
        cost_estimate=cost(6),
        name="fc_grad",
    )(place, left, right)


def qkv_grad_kernel(place_ref, left_ref, *refs, rows, parts, pieces):
    right_refs, weight_refs = refs[:parts], refs[parts : parts + pieces]
    keep_ref, send_ref, sum_ref, total = refs[parts + pieces :]
    flip = (place_ref[1] & 1) == 1
    half = left_ref.shape[0] // 2
    width = sum(ref.shape[2] for ref in right_refs)
    both = None
    for n in range(2):
        part = pl.ds(n * half, half)
        right = jnp.concatenate([ref[c, part, :] for c in range(3) for ref in right_refs], axis=1)
        here = dot_tn(left_ref[part, :], right)
        both = here if both is None else both + here
    low_both = both.astype(BF16)
    for pair in range(2):
        to = pair ^ (place_ref[1] >> 1)
        for c in range(3):
            cols = slice(c * width, (c + 1) * width)
            low = low_both[2 * pair * rows : (2 * pair + 1) * rows, cols]
            high = low_both[(2 * pair + 1) * rows : (2 * pair + 2) * rows, cols]
            keep_ref[to, c] = jnp.where(flip, high, low)
            send_ref[to, c] = jnp.where(flip, low, high)
    sum_ref[...] = jnp.zeros_like(sum_ref)
    if pieces > 1:
        total[...] = both
    span = both.shape[0] // pieces
    for n in range(pieces):
        at = pl.multiple_of((place_ref[1] ^ n) * span, span) if pieces > 1 else 0
        folded = jnp.zeros((span, 128), F32)
        for c in range(3):
            here = total[pl.ds(at, span), pl.ds(c * width, width)] if pieces > 1 else both[:, c * width : (c + 1) * width]
            product = here * weight_refs[n][c].astype(F32)
            for k in range(0, width, 128):
                folded = folded + product[:, k : k + 128]
        total[pl.ds(at, span), pl.ds(0, 128)] = folded
    sum_ref[0:1, :] = column_sum(jnp.transpose(total[:, 0:128]))


def qkv_grad(place, left, rights, weights, col_at=0):
    length, width = left.shape
    rows = width // 4
    cols = sum(value.shape[2] for value in rights)
    out = jax.ShapeDtypeStruct((2, 3, rows, cols), BF16)
    whole = lambda value: pl.BlockSpec(value.shape, lambda i, s: (0,) * len(value.shape))
    sums = jax.ShapeDtypeStruct((8, width), F32)
    return pl.pallas_call(
        functools.partial(qkv_grad_kernel, rows=rows, parts=len(rights), pieces=len(weights)),
        grid_spec=pltpu.PrefetchScalarGridSpec(
            num_scalar_prefetch=1, grid=(1,),
            in_specs=[whole(value) for value in (left, *rights)]
            + [pl.BlockSpec((3, value.shape[1], cols), lambda i, s: (0, 0, col_at)) for value in weights],
            out_specs=[whole(out), whole(out), whole(sums)],
            scratch_shapes=[pltpu.VMEM((width, 3 * cols), F32)]),
        out_shape=[out, out, sums],
        compiler_params=pltpu.CompilerParams(vmem_limit_bytes=VMEM_CAP),
        cost_estimate=cost(6.5),
        name="qkv_grad",
    )(place, left, *rights, *weights)


def proj_grad_kernel(place_ref, own_act, other_act, own_cot, other_cot, att_ref, branch_ref, keep_ref, send_ref, rest,
                     *, rows):
    side, pair = pl.program_id(0), pl.program_id(1)
    flip = (place_ref[1] & 1) == 1
    out_rows = att_ref.shape[1] // 8

    @pl.when((side == 0) & (pair == 0))
    def _():
        rest[...] = dot_tn_halves(att_ref, branch_ref).astype(BF16)

    both = (dot_tn(own_act[...], own_cot[...]) + dot_tn(other_act[...], other_cot[...])).astype(BF16)
    base = pl.multiple_of((side * 4 + pair * 2) * out_rows, out_rows)
    more_low, more_high = rest[pl.ds(base, out_rows), :], rest[pl.ds(base + out_rows, out_rows), :]
    low, high = both[:rows], both[rows:]
    keep_ref[0, 0, pl.ds(0, rows), :] = jnp.where(flip, high, low)
    send_ref[0, 0, pl.ds(0, rows), :] = jnp.where(flip, low, high)
    keep_ref[0, 0, pl.ds(rows, out_rows), :] = jnp.where(flip, more_high, more_low)
    send_ref[0, 0, pl.ds(rows, out_rows), :] = jnp.where(flip, more_low, more_high)


def proj_grad(place, active, cot_own, cot_other, attended, branch):
    length, width = active.shape
    rows = width // 8
    out_rows = attended.shape[1] // 8
    out = jax.ShapeDtypeStruct((2, 2, rows + out_rows, D), BF16)
    out_spec = pl.BlockSpec((1, 1, rows + out_rows, D), lambda n, j, s: (j ^ (s[1] >> 1), n, 0, 0))
    fixed = lambda count: pl.BlockSpec((count, D), lambda n, j, s: (0, 0))
    return pl.pallas_call(
        functools.partial(proj_grad_kernel, rows=rows),
        grid_spec=pltpu.PrefetchScalarGridSpec(
            num_scalar_prefetch=1, grid=(2, 2),
            in_specs=[pl.BlockSpec((length // 2, 2 * rows), lambda n, j, s: (s[0], n * 2 + j)),
                      pl.BlockSpec((length // 2, 2 * rows), lambda n, j, s: (1 - s[0], n * 2 + j)),
                      fixed(length // 2), fixed(length // 2), fixed(length), fixed(length)],
            out_specs=[out_spec, out_spec],
            scratch_shapes=[pltpu.VMEM((attended.shape[1], D), BF16)]),
        out_shape=[out, out],
        compiler_params=pltpu.CompilerParams(vmem_limit_bytes=VMEM_CAP),
        cost_estimate=cost(13),
        name="proj_grad",
    )(place, active, active, cot_own, cot_other, attended, branch)


def input_grad_kernel(place_ref, own_grads, other_grads, res_own, res_other, mid_ref, gain_ref, w_own, w_quarter,
                      own_out, send_out, weight, sems, *, steps):
    at = pl.program_id(0)
    quarter = D // 4
    half = w_own.shape[2]

    def copies():
        out = []
        for c in range(3):
            out.append(pltpu.make_async_copy(
                w_own.at[c], weight.at[:, pl.ds(c * half, half)], sems.at[c, 0]))
            for rel in range(4):
                place = pl.multiple_of((place_ref[1] ^ rel) * quarter, quarter)
                out.append(pltpu.make_async_copy(
                    w_quarter[rel].at[c], weight.at[pl.ds(place, quarter), pl.ds((3 + c) * half, half)],
                    sems.at[c, rel + 1]))
        return out

    @pl.when(at == 0)
    def _():
        for copy in copies():
            copy.start()

    mine = at < steps // 2
    compact = jnp.where(mine, res_own[...], res_other[...]).astype(F32)
    normal, factor = crms_normal(compact)

    @pl.when(at == 0)
    def _():
        for copy in copies():
            copy.wait()

    left = jnp.concatenate([ref[c] for part in (own_grads, other_grads) for c in range(3) for ref in part], axis=1)
    grad = dot_nt(left, weight[...])
    result = (mid_ref[...] + crms_back(normal, factor, gain_ref[...], grad)).astype(BF16)

    @pl.when(mine)
    def _():
        own_out[...] = result

    @pl.when(jnp.logical_not(mine))
    def _():
        send_out[...] = result


def input_grad(place, own_grads, other_grads, res_own, res_other, mid, gain, w_own, w_quarter, steps=4):
    length = mid.shape[0]
    block = length // steps
    own_map, other_map, whole_map = row_maps(steps)
    fixed = lambda i, s: (0, 0)
    mine, many = len(own_grads), len(own_grads) + len(other_grads)
    grad_spec = lambda value: pl.BlockSpec((3, block, value.shape[2]), lambda i, s: (0, whole_map(i, s)[0], 0))

    def body(place_ref, *refs):
        rest = refs[many:]
        input_grad_kernel(place_ref, refs[:mine], refs[mine:many], *rest[:5], rest[5:9], *rest[9:], steps=steps)

    sd = jax.ShapeDtypeStruct
    return pl.pallas_call(
        body,
        grid_spec=pltpu.PrefetchScalarGridSpec(
            num_scalar_prefetch=1, grid=(steps,),
            in_specs=[grad_spec(value) for value in (*own_grads, *other_grads)] + [pl.BlockSpec((block, D), own_map), pl.BlockSpec((block, D), other_map),
                      pl.BlockSpec((block, D), whole_map), pl.BlockSpec((1, D), fixed)] + [ANY] * 5,
            out_specs=[pl.BlockSpec((block, D), own_map), pl.BlockSpec((block, D), other_map)],
            scratch_shapes=[pltpu.VMEM((D, 3 * D), BF16), pltpu.SemaphoreType.DMA((3, 5))]),
        out_shape=[sd((length // 2, D), BF16), sd((length // 2, D), BF16)],
        compiler_params=pltpu.CompilerParams(vmem_limit_bytes=VMEM_CAP),
        cost_estimate=cost(9),
        name="input_grad",
    )(place, *own_grads, *other_grads, res_own, res_other, mid, gain, w_own, *w_quarter)


def pack_kernel(place_ref, own_ref, first_ref, second_ref, out_ref, *, steps):
    straight = place_ref[0] == 0
    own = jnp.transpose(own_ref[...].astype(F32))
    other = jnp.where(pl.program_id(0) < steps // 2, first_ref[...], second_ref[...])
    other = jnp.transpose(other.astype(F32))
    count = out_ref.shape[0]
    both = [jnp.where(straight, own, other)[:count], jnp.where(straight, other, own)[:count]]
    out_ref[...] = jnp.stack(both, 1).astype(BF16)


def pack_rows(place, own, first, second):
    positions = own.shape[0]
    steps = positions // 128
    own_map, other_map, _ = row_maps(steps)
    if second.shape[0] == positions:
        other_map = lambda i, s: (jnp.maximum(i, steps // 2), 0)
    packed = pl.pallas_call(
        functools.partial(pack_kernel, steps=steps),
        grid_spec=pltpu.PrefetchScalarGridSpec(
            num_scalar_prefetch=1, grid=(steps,),
            in_specs=[pl.BlockSpec((128, D), lambda i, s: (i, 0)), pl.BlockSpec((128, D), own_map),
                      pl.BlockSpec((128, D), other_map)],
            out_specs=pl.BlockSpec((D - 1, 2, 128), lambda i, s: (0, 0, i))),
        out_shape=jax.ShapeDtypeStruct((D - 1, 2, positions), BF16),
        compiler_params=pltpu.CompilerParams(vmem_limit_bytes=VMEM_CAP),
        cost_estimate=cost(0.1),
        name="pack_rows",
    )(place, own, first, second)
    return packed.transpose(1, 2, 0)


def swap(value, axis, bit, size):
    return lax.ppermute(value, axis, [(n, n ^ bit) for n in range(size)])


def meet(*values):
    return lax.optimization_barrier(values)


def add_low(*values):
    total = values[0].astype(F32)
    for value in values[1:]:
        total = total + value.astype(F32)
    return total.astype(BF16)


def chain_in(value):
    return lax.ppermute(value, "group", [(0, 1), (3, 2)])


def chain_across(value):
    return lax.ppermute(value, "group", [(1, 2), (2, 1)])


def chain_out(value):
    return lax.ppermute(value, "group", [(1, 0), (2, 3)])


def on_device(sizes, residual_in, piece_ids, norm_gains, qkv_weight, qv_bias, out_weight, fc_weight,
              fc_bias, proj_weight, out_biases, cotangent):
    n_dp, n_group, n_tensor = sizes["dp"], sizes["group"], sizes["tensor"]
    dp_at = lax.axis_index("dp")
    group_at = lax.axis_index("group")
    tensor_at = lax.axis_index("tensor")
    quarter_at = dp_at & 3
    proj_at = (dp_at & 1) | ((group_at & 1) << 1)
    place = jnp.stack([tensor_at, quarter_at, proj_at]).astype(jnp.int32)
    pad = ((0, 0), (0, 1))
    half = qv_bias.shape[1]
    hid = fc_bias.shape[0]
    pairs = half // 128
    y_swap = lambda value: swap(value, "tensor", 1, n_tensor)
    x_swap = lambda value: swap(value, "dp", 2, n_dp)
    c_swap = lambda value: swap(value, "dp", 1, n_dp)
    z_swap = lambda value: swap(value, "group", 1, n_group)

    def piece_of(shard, dim, at):
        rows = shard.shape[dim] // 4
        return lax.dynamic_slice_in_dim(shard, at * rows, rows, dim)

    qkv_piece = piece_of(qkv_weight, 1, quarter_at)
    qkv_y = y_swap(qkv_piece)
    bias_rows = jnp.concatenate([fc_bias.reshape(-1, D), qv_bias.reshape(1, D), jnp.zeros((13, D), BF16)], 0)
    res_own, res_send = unpack_rows(after(place, qkv_piece), residual_in, bias_rows)
    qkv_y, res_own, res_send, out_gated, fc_gated, proj_gated = meet(
        qkv_y, res_own, res_send, out_weight, fc_weight, proj_weight)
    res_other = y_swap(res_send)
    qkv_x = x_swap(qkv_y)
    qkv_c = c_swap(qkv_y)
    fc_piece = piece_of(fc_gated, 0, quarter_at)
    mix = jnp.concatenate([jnp.pad(piece_of(out_gated, 0, quarter_at), pad)]
                          + [fc_piece[:, n : n + D] for n in range(0, hid, D)], 0)
    proj_piece = jnp.pad(piece_of(proj_gated, 0, proj_at), pad)
    qkv_c, mix, proj_piece = meet(qkv_c, mix, proj_piece)
    mix_y, proj_y = y_swap(mix), y_swap(proj_piece)
    cot_own, cot_send = unpack_rows(after(place, mix, proj_piece), cotangent)
    out_own = jnp.pad(out_gated, pad)
    proj_own = jnp.pad(proj_gated, pad)
    qkv_x, res_other, out_own, proj_own, cot_send = meet(qkv_x, res_other, out_own, proj_own, cot_send)
    qkv_cx = c_swap(qkv_x)
    qkv_others = (qkv_y, qkv_c, qkv_x, qkv_cx)

    gains = norm_gains.astype(F32)
    end_biases = jnp.pad(out_biases, pad).astype(F32)
    count = residual_in.shape[1]
    bias_other = res_other[count : count + 8].astype(F32)
    fc_rows = hid // D
    qv_full = jnp.concatenate([qv_bias.astype(F32), bias_other[fc_rows].reshape(2, half)], axis=1)
    fc_full = jnp.concatenate([fc_bias.astype(F32).reshape(1, -1), bias_other[:fc_rows].reshape(1, -1)], axis=1)
    length = piece_ids.shape[1]
    flags = (lax.dynamic_index_in_dim(piece_ids, tensor_at, 0, keepdims=False)[:: length // 4] >= 0)
    flags = flags.astype(jnp.int32)

    normed_one, queries, key_rows, value_rows = project(
        place, res_own, res_other, gains[0:1], qv_full, qkv_weight, qkv_others)
    queries, cot_send = meet(queries, cot_send)
    cot_other = y_swap(cot_send)
    attended = attend_forward(flags, queries, key_rows, value_rows, 0, pairs)
    *attended, queries, mix_y, proj_y = meet(*attended, queries, mix_y, proj_y)
    mix_x, mix_c = x_swap(mix_y), c_swap(mix_y)
    proj_x, proj_c = z_swap(proj_y), c_swap(proj_y)
    attended = attend_forward(flags, queries, key_rows, value_rows, pairs, pairs, attended)
    attended, log_sums, mix_x, proj_x, cot_other = meet(*attended, mix_x, proj_x, cot_other)
    mix_others = (mix_y, mix_c, mix_x, c_swap(mix_x))
    proj_others = (proj_y, proj_c, proj_x, c_swap(proj_x))

    (normed_two, active, hidden_grad, out_mine, *out_send, middle_grad, branch_grad, attended_grad,
     middle_sums, own_sums, other_sums) = middle_stage(
        place, attended, res_own, res_other, cot_own, cot_other, gains[1:2], end_biases, fc_full,
        (out_own, fc_weight, proj_own, mix_others, proj_others))
    backward = functools.partial(attend_backward, flags, queries, key_rows, value_rows)
    restore = functools.partial(pack_rows, place)

    def small_outputs(small):
        part, first = hid // n_dp, half // n_dp
        return (jnp.concatenate([small[0:1, :D], small[0:1, D : 2 * D]], 0),
                lax.dynamic_slice(small, (0, 2 * D + hid + dp_at * first), (2, first)),
                lax.dynamic_slice(small, (0, 2 * D + dp_at * part), (1, part)).reshape(part),
                small[1:3, D : 2 * D - 1])

    if n_dp == 4 and n_group == 4:
        out_got = [y_swap(value) for value in out_send]
        proj_k, proj_s = proj_grad(after(place, middle_sums), active, cot_own, cot_other, attended, branch_grad)
        proj_k, proj_s, out_got[0] = meet(proj_k, proj_s, out_got[0])
        proj_c = c_swap(proj_s)
        fo_k, fo_s = fc_grad(after(place, proj_k), normed_two, hidden_grad, 1)
        fo_k, fo_s, proj_k, proj_c = meet(fo_k, fo_s, proj_k, proj_c)
        fo_c = c_swap(fo_s)
        proj_fo = add_low(proj_k[1, 1], proj_c[1, 1])
        proj_xo = x_swap(proj_fo)
        proj_fm = add_low(proj_k[1, 0], after(proj_c, proj_fo)[1, 0])
        proj_xm = x_swap(proj_fm)
        fm_k, fm_s = fc_grad(after(place, proj_fo, proj_fm), normed_two, hidden_grad, 0)
        fm_k, fm_s, fo_k, fo_c, *out_got = meet(fm_k, fm_s, fo_k, fo_c, *out_got)
        fm_c = c_swap(fm_s)
        fc_away = add_low(fo_k, fo_c)
        fc_y = y_swap(fc_away)
        first, first_sums = backward(after(attended_grad, fc_away), log_sums, pairs, pairs)
        first, first_sums, proj_k, proj_c, proj_xo, fm_k, fm_c = meet(
            first, first_sums, proj_k, proj_c, proj_xo, fm_k, fm_c)
        proj_r = add_low(proj_k[0, 1], proj_c[0, 1], proj_xo)
        proj_y = y_swap(proj_r)
        qo_k, qo_s, qo_sum = qkv_grad(after(place, proj_r), normed_one, [first], qkv_others)
        qo_k, qo_s, fm_k, fm_c, fc_y = meet(qo_k, qo_s, fm_k, fm_c, fc_y)
        qo_c = c_swap(qo_s)
        fc_far = add_low(fm_k[1], fm_c[1], fc_y[1])
        fc_x = x_swap(fc_far)
        own_a, sums_a = backward(after(attended_grad, fc_far), log_sums, 0, pairs - 1)
        own_a, sums_a, proj_y, proj_xm, proj_k, proj_c, fc_x, qo_k, qo_c = meet(
            own_a, sums_a, proj_y, proj_xm, proj_k, proj_c, fc_x, qo_k, qo_c)
        proj_shard = add_low(proj_k[0, 0], proj_c[0, 0], proj_xm, proj_y)
        proj_z = chain_in(proj_shard)
        fc_shard = add_low(fm_k[0], fm_c[0], fc_y[0], fc_x)
        fc_z = chain_in(fc_shard)
        qo_f = add_low(qo_k[1], qo_c[1])
        qo_x = x_swap(qo_f)
        own_b, sums_b = backward(after(attended_grad, qo_f, proj_shard, fc_shard), log_sums, pairs - 1, 1)
        qm_k, qm_s, qm_sum = qkv_grad(after(place, own_b), normed_one, [own_a, own_b], [qkv_weight])
        qm_k, qm_s, qm_sum, qo_k, qo_c, qo_x, proj_shard, proj_z = meet(
            qm_k, qm_s, qm_sum, qo_k, qo_c, qo_x, proj_shard, proj_z)
        qm_c = c_swap(qm_s)
        in_sums = (qm_sum + qo_sum) / gains[0:1]
        small = jnp.concatenate([in_sums, middle_sums, own_sums, other_sums, sums_a, sums_b, first_sums], 1)
        small_z = z_swap(small)
        qo_r = add_low(qo_k[0], qo_c[0], qo_x)
        qo_y = y_swap(qo_r)
        proj_shard = add_low(proj_shard, proj_z)
        proj_z = chain_across(proj_shard)
        qm_k, qm_c, qo_r, proj_shard = meet(qm_k, qm_c, qo_r, proj_shard)
        qm_f = add_low(qm_k[1], qm_c[1])
        qm_x = x_swap(qm_f)
        in_mine, in_send = input_grad(
            after(place, qm_f), [own_a, own_b], [first], res_own, res_other, middle_grad, gains[0:1],
            qkv_weight, qkv_others)
        in_mine, in_send, qm_x, qo_y, proj_shard, proj_z, fc_shard, fc_z, small, small_z = meet(
            in_mine, in_send, qm_x, qo_y, proj_shard, proj_z, fc_shard, fc_z, small, small_z)
        small = small + small_z
        small_z = swap(small, "group", 2, n_group)
        last = add_low(qm_k[0], qm_c[0], qm_x, qo_y)
        last_z = chain_in(last)
        fc_shard = add_low(fc_shard, fc_z)
        fc_z = chain_across(fc_shard)
        proj_shard = add_low(proj_shard, proj_z)
        proj_z = chain_out(proj_shard)
        in_got = y_swap(in_send)
        block_out = restore(after(out_mine, last, proj_shard, fc_shard, small), *out_got)
        last, last_z, block_out, small, small_z, fc_shard, fc_z = meet(
            last, last_z, block_out, small, small_z, fc_shard, fc_z)
        small = small + small_z
        small_c = c_swap(small)
        last = add_low(last, last_z)
        last_z = chain_across(last)
        fc_shard = add_low(fc_shard, fc_z)
        fc_z = chain_out(fc_shard)
        middle_one = (group_at == 1) | (group_at == 2)
        small, small_c, last, fc_shard, proj_shard, proj_z = meet(small, small_c, last, fc_shard, proj_shard, proj_z)
        small = small + small_c
        small_x = x_swap(small)
        proj_shard = jnp.where(middle_one, proj_shard, proj_z)
        out_shard = proj_shard[hid // 4 :, : D - 1].astype(F32)
        proj_shard = proj_shard[: hid // 4, : D - 1].astype(F32)
        small, small_x, in_mine, in_got, last, last_z, fc_shard, proj_shard, out_shard = meet(
            small, small_x, in_mine, in_got, last, last_z, fc_shard, proj_shard, out_shard)
        last = add_low(last, last_z)
        last_z = chain_out(last)
        small = small + small_x
        split = 2 * D + hid
        mine = jnp.concatenate([small[:, :split], small[:, split + hid : split + hid + half]], 1)
        other = jnp.concatenate([small[:, : 2 * D], small[:, split : split + hid], small[:, split + hid + half :]], 1)
        small_y = y_swap(other)
        in_out = restore(after(in_mine, last), in_got, in_got)
        in_out, mine, small_y, fc_shard, fc_z = meet(in_out, mine, small_y, fc_shard, fc_z)
        small = small_outputs(mine + small_y)
        fc_shard = jnp.where(middle_one, fc_shard, fc_z).astype(F32)
        last, last_z, in_out, proj_shard, out_shard, fc_shard, *small = meet(
            last, last_z, in_out, proj_shard, out_shard, fc_shard, *small)
        qkv_shard = jnp.where(middle_one, last, last_z)
    else:
        first, first_sums = backward(attended_grad, log_sums, pairs, pairs)
        own, second_sums = backward(attended_grad, log_sums, 0, pairs)
        in_mine, in_send = input_grad(
            place, [own], [first], res_own, res_other, middle_grad, gains[0:1], qkv_weight, qkv_others)
        in_got = y_swap(in_send)
        in_out = restore(in_mine, in_got, in_got)
        block_out = restore(out_mine, *[y_swap(value) for value in out_send])
        qo_sum = qkv_grad(place, normed_one, [first], qkv_others)[2]
        qm_sum = qkv_grad(place, normed_one, [own], [qkv_weight])[2]

        def scatter(own, other):
            total = [lax.psum_scatter(value.astype(BF16), "dp", scatter_dimension=0, tiled=True)
                     for value in (own, other)]
            return lax.psum(add_low(total[0], y_swap(total[1])), "group")

        cot_rows = jnp.where(tensor_at == 0, jnp.concatenate([cot_own, cot_other]),
                             jnp.concatenate([cot_other, cot_own]))
        proj_shard = scatter(dot_tn(active[:, :hid], cot_rows), dot_tn(active[:, hid:], cot_rows))
        fc_shard = scatter(dot_tn(normed_two, hidden_grad[:, :hid]), dot_tn(normed_two, hidden_grad[:, hid:]))
        out_shard = scatter(dot_tn(attended[:, :half], branch_grad), dot_tn(attended[:, half:], branch_grad))
        proj_shard, out_shard = proj_shard[:, : D - 1].astype(F32), out_shard[:, : D - 1].astype(F32)
        fc_shard = fc_shard.astype(F32)
        qkv_shard = jnp.swapaxes(scatter(
            *[jnp.stack([dot_tn(normed_one, part[c]) for c in range(3)], 1) for part in (own, first)]), 0, 1)
        in_sums = (qm_sum + qo_sum) / gains[0:1]
        small = jnp.concatenate([in_sums, middle_sums, own_sums, second_sums], 1)
        small = small + y_swap(jnp.concatenate([in_sums, middle_sums, other_sums, first_sums], 1))
        small = small_outputs(lax.psum(small, ("dp", "group")))

    grad_gains, grad_qv_bias, grad_fc_bias, grad_out_biases = small
    return (
        block_out,
        in_out,
        grad_gains,
        qkv_shard.astype(F32),
        grad_qv_bias,
        out_shard,
        fc_shard,
        grad_fc_bias,
        proj_shard,
        grad_out_biases,
    )


def solution(mesh):
    sizes = dict(mesh.shape)
    in_specs = (
        P(("dp", "group"), "tensor", None),
        P(("dp", "group"), None),
        P(),
        P(None, None, "tensor"),
        P(None, "tensor"),
        P("tensor", None),
        P(None, "tensor"),
        P("tensor"),
        P("tensor", None),
        P(),
        P(("dp", "group"), "tensor", None),
    )
    out_specs = (
        P(("dp", "group"), "tensor", None),
        P(("dp", "group"), "tensor", None),
        P(),
        P(None, "dp", "tensor"),
        P(None, ("tensor", "dp")),
        P(("tensor", "dp"), None),
        P("dp", "tensor"),
        P(("tensor", "dp")),
        P(("tensor", "dp"), None),
        P(),
    )
    return jax.shard_map(
        functools.partial(on_device, sizes), mesh=mesh, in_specs=in_specs, out_specs=out_specs,
        check_vma=False)
```

```python
import functools
import jax
import jax.numpy as jnp
from jax import lax
from jax.sharding import PartitionSpec as P
from jax.experimental import pallas as pl
from jax.experimental.pallas import tpu as pltpu

D = 768
HD = 64
EPSILON = 1e-05
MASKED = -1e30
MIB = 1024 * 1024
F32 = jnp.float32
BF16 = jnp.bfloat16
COST_FLOPS = 0.4e9


def cost(micros):
    return pl.CostEstimate(flops=int(micros * COST_FLOPS), bytes_accessed=int(micros * 4e5), transcendentals=0)


def after(value, *others):
    return lax.optimization_barrier((value, *others))[0]


def dot_nn(a, b):
    return lax.dot_general(a, b, (((1,), (0,)), ((), ())), preferred_element_type=F32)


def dot_nt(a, b):
    return lax.dot_general(a, b, (((1,), (1,)), ((), ())), preferred_element_type=F32)


def dot_tn(a, b):
    return lax.dot_general(a, b, (((0,), (0,)), ((), ())), preferred_element_type=F32)


def dot_tn_halves(left, right):
    half = left.shape[0] // 2
    return (dot_tn(left[pl.ds(0, half), :], right[pl.ds(0, half), :])
            + dot_tn(left[pl.ds(half, half), :], right[pl.ds(half, half), :]))


def column_sum(values):
    return jnp.sum(values, axis=0, keepdims=True)


def lane_of(shape):
    return lax.broadcasted_iota(jnp.int32, shape, len(shape) - 1)


def attend_forward_kernel(flags_ref, q_ref, k_ref, v_ref, out_ref, log_ref, *, block):
    length = q_ref.shape[0]
    key_at = lax.broadcasted_iota(jnp.int32, (block, block), 0)
    query_at = lax.broadcasted_iota(jnp.int32, (block, block), 1)
    causal = key_at <= query_at
    head_lane = lane_of((block, 128)) // HD
    for at in range(length // block):
        rows = pl.ds(at * block, block)
        reach = (at + 1) * block
        keys = pl.ds(0, reach)
        seen = causal | (flags_ref[at] > 0)
        parts = []
        for head in range(2):
            q_head = jnp.where(head_lane == head, q_ref[rows, :], jnp.zeros((block, 128), BF16))
            scores = dot_nt(k_ref[keys, :], q_head)
            last = jnp.where(seen, scores[reach - block :], MASKED)
            scores = last if at == 0 else jnp.concatenate([scores[: reach - block], last], 0)
            top = jnp.max(scores, axis=0, keepdims=True)
            probs = jnp.exp(scores - top)
            total = jnp.sum(probs, axis=0, keepdims=True)
            log_ref[0, pl.ds(head, 1), rows] = top + jnp.log(total)
            probs = (probs * (1.0 / total)).astype(BF16)
            parts.append(dot_tn(probs, v_ref[keys, :]).astype(BF16))
        out_ref[rows, :] = jnp.where(head_lane == 0, parts[0], parts[1])


def attend_forward(flags, queries, key_rows, value_rows, first, pairs, into=None):
    length, width = queries.shape
    block = length // 4
    tile = pl.BlockSpec((length, 128), lambda h, f: (0, h + first))
    more = [] if into is None else list(into)

    def body(flags_ref, q_ref, k_ref, v_ref, *rest):
        attend_forward_kernel(flags_ref, q_ref, k_ref, v_ref, *rest[len(more):], block=block)

    return pl.pallas_call(
        body,
        grid_spec=pltpu.PrefetchScalarGridSpec(
            num_scalar_prefetch=1, grid=(pairs,),
            in_specs=[tile, tile, tile] + [pl.BlockSpec(memory_space=pl.ANY)] * len(more),
            out_specs=[tile, pl.BlockSpec((1, 8, length), lambda h, f: (h + first, 0, 0))]),
        out_shape=[jax.ShapeDtypeStruct((length, width), BF16),
                   jax.ShapeDtypeStruct((width // 128, 8, length), F32)],
        input_output_aliases={4 + n: n for n in range(len(more))},
        compiler_params=pltpu.CompilerParams(vmem_limit_bytes=6 * MIB),
        cost_estimate=cost(3.8 * pairs),
        name="attend_forward",
    )(flags, queries, key_rows, value_rows, *more)


def attend_backward_kernel(flags_ref, q_ref, k_ref, v_ref, up_ref, log_ref,
                           grad_ref, sum_ref, dk_acc, dv_acc, *, block):
    length = q_ref.shape[0]
    count = length // block
    key_at = lax.broadcasted_iota(jnp.int32, (block, block), 0)
    query_at = lax.broadcasted_iota(jnp.int32, (block, block), 1)
    causal = key_at <= query_at
    head_lane = lane_of((block, 128)) // HD
    full_lane = lane_of((length, 128)) // HD
    dq_sum = jnp.zeros((1, 128), F32)
    for at in reversed(range(count)):
        rows = pl.ds(at * block, block)
        reach = (at + 1) * block
        keys = pl.ds(0, reach)
        seen = causal | (flags_ref[at] > 0)
        dq = None
        for head in range(2):
            q_head = jnp.where(head_lane == head, q_ref[rows, :], jnp.zeros((block, 128), BF16))
            up_head = jnp.where(head_lane == head, up_ref[rows, :], jnp.zeros((block, 128), BF16))
            logs = log_ref[0, pl.ds(head, 1), rows]
            scores = dot_nt(k_ref[keys, :], q_head)
            last = jnp.where(seen, scores[reach - block :], MASKED)
            scores = last if at == 0 else jnp.concatenate([scores[: reach - block], last], 0)
            probs = jnp.exp(scores - logs)
            along = dot_nt(v_ref[keys, :], up_head)
            inner = jnp.sum(probs * along, axis=0, keepdims=True)
            low_grad = (probs * (along - inner)).astype(BF16)
            dv = dot_nn(probs.astype(BF16), up_head)
            dk = dot_nn(low_grad, q_head)
            if at == count - 1 and head == 0:
                dv_acc[keys, :] = dv
                dk_acc[keys, :] = dk
            else:
                dv_acc[keys, :] += dv
                dk_acc[keys, :] += dk
            k_head = jnp.where(full_lane[:reach] == head, k_ref[keys, :], jnp.zeros((reach, 128), BF16))
            part = dot_tn(low_grad, k_head)
            dq = part if dq is None else dq + part
        low_dq = (dq * HD ** (-0.5)).astype(BF16)
        grad_ref[0, rows, :] = low_dq
        dq_sum = dq_sum + column_sum(low_dq.astype(F32))
    grad_ref[1] = dk_acc[...].astype(BF16)
    low_dv = dv_acc[...].astype(BF16)
    grad_ref[2] = low_dv
    sum_ref[...] = jnp.zeros_like(sum_ref)
    sum_ref[0:1, :] = dq_sum
    sum_ref[1:2, :] = column_sum(low_dv.astype(F32))


def attend_backward(flags, queries, key_rows, value_rows, upstream, log_sums, first, pairs):
    length = queries.shape[0]
    tile = pl.BlockSpec((length, 128), lambda h, f: (0, h + first))
    return pl.pallas_call(
        functools.partial(attend_backward_kernel, block=length // 4),
        grid_spec=pltpu.PrefetchScalarGridSpec(
            num_scalar_prefetch=1, grid=(pairs,),
            in_specs=[tile, tile, tile, tile,
                      pl.BlockSpec((1, 8, length), lambda h, f: (h + first, 0, 0))],
            out_specs=[pl.BlockSpec((3, length, 128), lambda h, f: (0, 0, h)),
                       pl.BlockSpec((8, 128), lambda h, f: (0, h))],
            scratch_shapes=[pltpu.VMEM((length, 128), F32), pltpu.VMEM((length, 128), F32)]),
        out_shape=[jax.ShapeDtypeStruct((3, length, pairs * 128), BF16),
                   jax.ShapeDtypeStruct((8, pairs * 128), F32)],
        compiler_params=pltpu.CompilerParams(vmem_limit_bytes=9 * MIB),
        cost_estimate=cost(1 + 6 * pairs),
        name="attend_backward",
    )(flags, queries, key_rows, value_rows, upstream, log_sums)


def unpack_kernel(place_ref, rows_ref, *refs):
    own_ref, send_ref = refs[-2:]
    packed = rows_ref[...]
    packed = packed.reshape(packed.shape[0] * 2, packed.shape[2])
    shape = (packed.shape[0], D)
    row = lax.broadcasted_iota(jnp.int32, shape, 0)
    column = lax.broadcasted_iota(jnp.int32, shape, 1)
    pick = lambda seq: dot_tn(packed, jnp.where(row == 2 * column + seq, 1.0, 0.0).astype(BF16)).astype(BF16)
    count = own_ref.shape[0]
    send_ref[pl.ds(0, count), :] = pick(1 - place_ref[0])
    if len(refs) > 2:
        send_ref[pl.ds(count, refs[0].shape[0]), :] = refs[0][...]
    own_ref[...] = pick(place_ref[0])


def unpack_rows(place, rows, *extra):
    packed = rows.transpose(2, 0, 1)
    count = rows.shape[1]
    counts = [count, count + sum(value.shape[0] for value in extra)]
    fixed = lambda value: pl.BlockSpec(value.shape, lambda i, s: (0,) * len(value.shape))
    return pl.pallas_call(
        unpack_kernel,
        grid_spec=pltpu.PrefetchScalarGridSpec(
            num_scalar_prefetch=1, grid=(1,),
            in_specs=[fixed(packed)] + [fixed(value) for value in extra],
            out_specs=[pl.BlockSpec((n, D), lambda i, s: (0, 0)) for n in counts]),
        out_shape=[jax.ShapeDtypeStruct((n, D), BF16) for n in counts],
        compiler_params=pltpu.CompilerParams(vmem_limit_bytes=6 * MIB),
        cost_estimate=cost(5),
        name="unpack_rows",
    )(place, packed, *extra)


def decompress(compact):
    total = jnp.sum(compact, axis=-1, keepdims=True)
    return jnp.where(lane_of(compact.shape) == D - 1, -total, compact)


def crms_back(normal, factor, gain, grad):
    scaled = gain * grad
    du = factor * (scaled - normal * jnp.mean(scaled * normal, axis=-1, keepdims=True))
    lane = lane_of(du.shape)
    last = jnp.sum(jnp.where(lane == D - 1, du, 0.0), axis=-1, keepdims=True)
    return jnp.where(lane == D - 1, 0.0, du - last)


def crms_normal(compact):
    full = decompress(compact)
    factor = lax.rsqrt(jnp.mean(full * full, axis=-1, keepdims=True) + EPSILON)
    return full * factor, factor


def project_kernel(place_ref, own_ref, other_ref, gain_ref, bias_ref, w_own, w_quarter,
                   normed_ref, q_ref, k_ref, v_ref, weight, sems, *, steps):
    at = pl.program_id(0)
    quarter = D // 4
    half = w_own.shape[2]

    def copies():
        out = [pltpu.make_async_copy(w_own, weight.at[:, :, pl.ds(0, half)], sems.at[0])]
        for rel in range(4):
            place = pl.multiple_of((place_ref[1] ^ rel) * quarter, quarter)
            out.append(pltpu.make_async_copy(
                w_quarter[rel], weight.at[:, pl.ds(place, quarter), pl.ds(half, half)],
                sems.at[rel + 1]))
        return out

    @pl.when(at == 0)
    def _():
        for copy in copies():
            copy.start()

    compact = jnp.where(at < steps // 2, own_ref[...], other_ref[...]).astype(F32)
    normal, _ = crms_normal(compact)
    normed = (normal * gain_ref[...]).astype(BF16)
    normed_ref[...] = normed

    @pl.when(at == 0)
    def _():
        for copy in copies():
            copy.wait()

    q_ref[...] = ((dot_nn(normed, weight[0]) + bias_ref[0:1, :]).astype(BF16).astype(F32)
                  * HD ** (-0.5)).astype(BF16)
    k_ref[...] = dot_nn(normed, weight[1]).astype(BF16)
    v_ref[...] = (dot_nn(normed, weight[2]) + bias_ref[1:2, :]).astype(BF16)


def row_maps(steps):
    half = steps // 2
    own = lambda i, s: (jnp.minimum(i, half - 1), 0)
    other = lambda i, s: (jnp.maximum(i - half, 0), 0)
    whole = lambda i, s: (jnp.where(i < half, s[0] * half + i, (1 - s[0]) * half + i - half), 0)
    return own, other, whole


ANY = pl.BlockSpec(memory_space=pl.ANY)


def project(place, own, other, gain, bias, w_own, w_quarter, steps=4):
    length = own.shape[0] * 2
    block = length // steps
    own_map, other_map, whole_map = row_maps(steps)
    fixed = lambda i, s: (0, 0)
    wide = pl.BlockSpec((block, D), whole_map)
    out = jax.ShapeDtypeStruct((length, D), BF16)

    def body(place_ref, own_ref, other_ref, gain_ref, bias_ref, w_own, a, b, c, d, *rest):
        project_kernel(place_ref, own_ref, other_ref, gain_ref, bias_ref, w_own, (a, b, c, d),
                       *rest, steps=steps)

    return pl.pallas_call(
        body,
        grid_spec=pltpu.PrefetchScalarGridSpec(
            num_scalar_prefetch=1, grid=(steps,),
            in_specs=[pl.BlockSpec((block, D), own_map), pl.BlockSpec((block, D), other_map),
                      pl.BlockSpec((1, D), fixed), pl.BlockSpec((2, D), fixed)] + [ANY] * 5,
            out_specs=[wide] * 4,
            scratch_shapes=[pltpu.VMEM((3, D, D), BF16), pltpu.SemaphoreType.DMA((5,))]),
        out_shape=[out] * 4,
        compiler_params=pltpu.CompilerParams(vmem_limit_bytes=11 * MIB),
        cost_estimate=cost(10),
        name="norm_project",
    )(place, own, other, gain, bias, w_own, *w_quarter)


SQRT_2_PI = 0.7978845608028654


def gelu_pair(v):
    square = v * v
    inner = v * (SQRT_2_PI + (SQRT_2_PI * 0.044715) * square)
    tanh = jnp.tanh(inner)
    cdf = 0.5 + 0.5 * tanh
    slope = SQRT_2_PI + (3 * SQRT_2_PI * 0.044715) * square
    back = cdf + (0.5 * v) * (1.0 - tanh * tanh) * slope
    return v * cdf, back


def middle_kernel(place_ref, att_ref, res_own, res_other, cot_own, cot_other, gain_ref, end_ref,
                  fcb_ref, weights, two_ref, active_ref, hidden_ref, own_out, send_first, send_second,
                  mid_ref, branch_ref, upgrad_ref, sums_ref, own_sums, other_sums,
                  out_w, fc_w, proj_w, sems, *, steps, chunk):
    at = pl.program_id(0)
    hid = fc_w.shape[1]
    half = hid // 2
    o_own, f_own, p_own, quarters, proj_quarters = weights

    def copies(which):
        if which == 0:
            own, target = o_own, out_w.at[pl.ds(0, D // 2), :]
        elif which == 1:
            own, target = f_own, fc_w.at[:, pl.ds(0, half)]
        else:
            own, target = p_own, proj_w.at[pl.ds(0, half), :]
        out = [pltpu.make_async_copy(own, target, sems.at[which, 0])]
        for rel in range(4):
            source = proj_quarters[rel] if which == 2 else quarters[rel]
            to = place_ref[2 if which == 2 else 1] ^ rel
            if which == 0:
                moves = [(0, D // 8, out_w, D // 2 + to * (D // 8), None)]
            elif which == 1:
                moves = [(D // 8 + n * (D // 4), D // 4, fc_w, to * (D // 4), half + n * D)
                         for n in range(half // D)]
            else:
                moves = [(0, half // 4, proj_w, half + to * (half // 4), None)]
            for n, (start, rows, into, row, col) in enumerate(moves):
                spot = pl.ds(pl.multiple_of(row, rows), rows)
                out.append(pltpu.make_async_copy(
                    source.at[pl.ds(start, rows), :],
                    into.at[spot, :] if col is None else into.at[spot, pl.ds(col, D)],
                    sems.at[which, 1 + 2 * rel + n]))
        return out

    @pl.when(at == 0)
    def _():
        for which in range(3):
            for copy in copies(which):
                copy.start()
        for ref in (sums_ref, own_sums, other_sums):
            ref[...] = jnp.zeros_like(ref)
        for copy in copies(0):
            copy.wait()

    mine = at < steps // 2
    compact = jnp.where(mine, res_own[...], res_other[...]).astype(F32)
    cot_low = jnp.where(mine, cot_own[...], cot_other[...])
    middle = compact + dot_nn(att_ref[...], out_w[...]) + end_ref[0:1, :]
    normal, factor = crms_normal(middle)
    gain = gain_ref[...]
    two = (normal * gain).astype(BF16)
    two_ref[...] = two

    @pl.when(at == 0)
    def _():
        for which in (1, 2):
            for copy in copies(which):
                copy.wait()

    mlp = jnp.zeros((two.shape[0], D), F32)
    two_grad = jnp.zeros((two.shape[0], D), F32)
    for start in range(0, hid, chunk):
        cols = pl.ds(start, chunk)
        pre = dot_nn(two, fc_w[:, cols]) + fcb_ref[0:1, cols]
        act, slope = gelu_pair(pre)
        act = act.astype(BF16)
        active_ref[:, cols] = act
        mlp = mlp + dot_nn(act, proj_w[cols, :])
        hidden = (dot_nt(cot_low, proj_w[cols, :]) * slope).astype(BF16)
        hidden_ref[:, cols] = hidden
        to = own_sums if start < half else other_sums
        to[0:1, pl.ds(start % half, chunk)] += column_sum(hidden.astype(F32))
        two_grad = two_grad + dot_nt(hidden, fc_w[:, cols])
    block_out = (middle + mlp + end_ref[1:2, :]).astype(BF16)

    @pl.when(mine)
    def _():
        own_out[...] = block_out

    @pl.when(at == steps // 2)
    def _():
        send_first[...] = block_out

    @pl.when(at == steps // 2 + 1)
    def _():
        send_second[...] = block_out

    cot = cot_low.astype(F32)
    mid_grad = cot + crms_back(normal, factor, gain, two_grad)
    mid_ref[...] = mid_grad
    branch = mid_grad.astype(BF16)
    branch_ref[...] = branch
    upgrad_ref[...] = dot_nt(branch, out_w[...]).astype(BF16)
    sums_ref[0:1, :] += column_sum(two_grad * normal)
    sums_ref[1:2, :] += column_sum(branch.astype(F32))
    sums_ref[2:3, :] += column_sum(cot)


def middle_stage(place, att, res_own, res_other, cot_own, cot_other, gain, end_bias, fc_bias, weights,
                 steps=4, chunk=768):
    length = att.shape[0]
    hid = fc_bias.shape[1]
    block = length // steps
    own_map, other_map, whole_map = row_maps(steps)
    fixed = lambda i, s: (0, 0)
    flat = [*weights[:3], *weights[3], *weights[4]]
    spec = lambda w, m: pl.BlockSpec((block, w), m)

    def body(place_ref, *refs):
        ins, rest = refs[:8], refs[8:]
        w, rest = rest[:11], rest[11:]
        packed = (*w[:3], w[3:7], w[7:])
        middle_kernel(place_ref, *ins, packed, *rest, steps=steps, chunk=chunk)

    sd = jax.ShapeDtypeStruct
    return pl.pallas_call(
        body,
        grid_spec=pltpu.PrefetchScalarGridSpec(
            num_scalar_prefetch=1, grid=(steps,),
            in_specs=[spec(D, whole_map), spec(D, own_map), spec(D, other_map), spec(D, own_map),
                      spec(D, other_map), pl.BlockSpec((1, D), fixed), pl.BlockSpec((2, D), fixed),
                      pl.BlockSpec((1, hid), fixed)] + [ANY] * 11,
            out_specs=[spec(D, whole_map), spec(hid, whole_map), spec(hid, whole_map),
                       spec(D, own_map), spec(D, fixed), spec(D, fixed),
                       spec(D, whole_map), spec(D, whole_map), spec(D, whole_map),
                       pl.BlockSpec((8, D), fixed), pl.BlockSpec((8, hid // 2), fixed),
                       pl.BlockSpec((8, hid // 2), fixed)],
            scratch_shapes=[pltpu.VMEM((D, D), BF16), pltpu.VMEM((D, hid), BF16),
                            pltpu.VMEM((hid, D), BF16), pltpu.SemaphoreType.DMA((3, 9))]),
        out_shape=[sd((length, D), BF16), sd((length, hid), BF16), sd((length, hid), BF16),
                   sd((length // 2, D), BF16), sd((block, D), BF16), sd((block, D), BF16),
                   sd((length, D), F32), sd((length, D), BF16), sd((length, D), BF16),
                   sd((8, D), F32), sd((8, hid // 2), F32), sd((8, hid // 2), F32)],
        compiler_params=pltpu.CompilerParams(vmem_limit_bytes=36 * MIB),
        cost_estimate=cost(38),
        name="middle_stage",
    )(place, att, res_own, res_other, cot_own, cot_other, gain, end_bias, fc_bias, *flat)


def fc_grad_kernel(place_ref, left_ref, right_ref, keep_ref, send_ref, *, rows):
    flip = (place_ref[1] & 1) == 1
    both = dot_tn_halves(left_ref, right_ref).astype(BF16)
    for pair in range(2):
        to = pair ^ (place_ref[1] >> 1)
        low, high = both[2 * pair * rows : (2 * pair + 1) * rows], both[(2 * pair + 1) * rows : (2 * pair + 2) * rows]
        keep_ref[0, to] = jnp.where(flip, high, low)
        send_ref[0, to] = jnp.where(flip, low, high)


def fc_grad(place, left, right, chunk=768):
    length, width = left.shape
    rows = width // 4
    half = right.shape[1] // 2
    parts = half // chunk
    out = jax.ShapeDtypeStruct((2, 2, rows, half), BF16)
    out_spec = pl.BlockSpec((1, 2, rows, chunk), lambda n, s: (n // parts, 0, 0, n % parts))
    return pl.pallas_call(
        functools.partial(fc_grad_kernel, rows=rows),
        grid_spec=pltpu.PrefetchScalarGridSpec(
            num_scalar_prefetch=1, grid=(2 * parts,),
            in_specs=[pl.BlockSpec((length, width), lambda n, s: (0, 0)),
                      pl.BlockSpec((length, chunk), lambda n, s: (0, n))],
            out_specs=[out_spec, out_spec]),
        out_shape=[out, out],
        compiler_params=pltpu.CompilerParams(vmem_limit_bytes=12 * MIB),
        cost_estimate=cost(12),
        name="fc_grad",
    )(place, left, right)


def qkv_grad_kernel(place_ref, left_ref, *refs, rows, parts, pieces):
    right_refs, weight_refs = refs[:parts], refs[parts : parts + pieces]
    keep_ref, send_ref, sum_ref, total = refs[parts + pieces :]
    flip = (place_ref[1] & 1) == 1
    half = left_ref.shape[0] // 2
    width = sum(ref.shape[2] for ref in right_refs)
    both = None
    for n in range(2):
        part = pl.ds(n * half, half)
        right = jnp.concatenate([ref[c, part, :] for c in range(3) for ref in right_refs], axis=1)
        here = dot_tn(left_ref[part, :], right)
        both = here if both is None else both + here
    low_both = both.astype(BF16)
    for pair in range(2):
        to = pair ^ (place_ref[1] >> 1)
        for c in range(3):
            cols = slice(c * width, (c + 1) * width)
            low = low_both[2 * pair * rows : (2 * pair + 1) * rows, cols]
            high = low_both[(2 * pair + 1) * rows : (2 * pair + 2) * rows, cols]
            keep_ref[to, c] = jnp.where(flip, high, low)
            send_ref[to, c] = jnp.where(flip, low, high)
    sum_ref[...] = jnp.zeros_like(sum_ref)
    if pieces > 1:
        total[...] = both
    span = both.shape[0] // pieces
    for n in range(pieces):
        at = pl.multiple_of((place_ref[1] ^ n) * span, span) if pieces > 1 else 0
        folded = jnp.zeros((span, 128), F32)
        for c in range(3):
            here = total[pl.ds(at, span), pl.ds(c * width, width)] if pieces > 1 else both[:, c * width : (c + 1) * width]
            product = here * weight_refs[n][c].astype(F32)
            for k in range(0, width, 128):
                folded = folded + product[:, k : k + 128]
        total[pl.ds(at, span), pl.ds(0, 128)] = folded
    sum_ref[0:1, :] = column_sum(jnp.transpose(total[:, 0:128]))


def qkv_grad(place, left, rights, weights, col_at=0):
    length, width = left.shape
    rows = width // 4
    cols = sum(value.shape[2] for value in rights)
    out = jax.ShapeDtypeStruct((2, 3, rows, cols), BF16)
    whole = lambda value: pl.BlockSpec(value.shape, lambda i, s: (0,) * len(value.shape))
    sums = jax.ShapeDtypeStruct((8, width), F32)
    return pl.pallas_call(
        functools.partial(qkv_grad_kernel, rows=rows, parts=len(rights), pieces=len(weights)),
        grid_spec=pltpu.PrefetchScalarGridSpec(
            num_scalar_prefetch=1, grid=(1,),
            in_specs=[whole(value) for value in (left, *rights)]
            + [pl.BlockSpec((3, value.shape[1], cols), lambda i, s: (0, 0, col_at)) for value in weights],
            out_specs=[whole(out), whole(out), whole(sums)],
            scratch_shapes=[pltpu.VMEM((width, 3 * cols), F32)]),
        out_shape=[out, out, sums],
        compiler_params=pltpu.CompilerParams(vmem_limit_bytes=17 * MIB),
        cost_estimate=cost(6.5),
        name="qkv_grad",
    )(place, left, *rights, *weights)


def proj_grad_kernel(place_ref, own_act, other_act, own_cot, other_cot, att_ref, branch_ref, keep_ref, send_ref, rest,
                     *, rows):
    side, pair = pl.program_id(0), pl.program_id(1)
    flip = (place_ref[1] & 1) == 1
    out_rows = att_ref.shape[1] // 8

    @pl.when((side == 0) & (pair == 0))
    def _():
        rest[...] = dot_tn_halves(att_ref, branch_ref).astype(BF16)

    both = (dot_tn(own_act[...], own_cot[...]) + dot_tn(other_act[...], other_cot[...])).astype(BF16)
    base = pl.multiple_of((side * 4 + pair * 2) * out_rows, out_rows)
    more_low, more_high = rest[pl.ds(base, out_rows), :], rest[pl.ds(base + out_rows, out_rows), :]
    low, high = both[:rows], both[rows:]
    keep_ref[0, 0, pl.ds(0, rows), :] = jnp.where(flip, high, low)
    send_ref[0, 0, pl.ds(0, rows), :] = jnp.where(flip, low, high)
    keep_ref[0, 0, pl.ds(rows, out_rows), :] = jnp.where(flip, more_high, more_low)
    send_ref[0, 0, pl.ds(rows, out_rows), :] = jnp.where(flip, more_low, more_high)


def proj_grad(place, active, cot_own, cot_other, attended, branch):
    length, width = active.shape
    rows = width // 8
    out_rows = attended.shape[1] // 8
    out = jax.ShapeDtypeStruct((2, 2, rows + out_rows, D), BF16)
    out_spec = pl.BlockSpec((1, 1, rows + out_rows, D), lambda n, j, s: (j ^ (s[1] >> 1), n, 0, 0))
    fixed = lambda count: pl.BlockSpec((count, D), lambda n, j, s: (0, 0))
    return pl.pallas_call(
        functools.partial(proj_grad_kernel, rows=rows),
        grid_spec=pltpu.PrefetchScalarGridSpec(
            num_scalar_prefetch=1, grid=(2, 2),
            in_specs=[pl.BlockSpec((length // 2, 2 * rows), lambda n, j, s: (s[0], n * 2 + j)),
                      pl.BlockSpec((length // 2, 2 * rows), lambda n, j, s: (1 - s[0], n * 2 + j)),
                      fixed(length // 2), fixed(length // 2), fixed(length), fixed(length)],
            out_specs=[out_spec, out_spec],
            scratch_shapes=[pltpu.VMEM((attended.shape[1], D), BF16)]),
        out_shape=[out, out],
        compiler_params=pltpu.CompilerParams(vmem_limit_bytes=19 * MIB),
        cost_estimate=cost(13),
        name="proj_grad",
    )(place, active, active, cot_own, cot_other, attended, branch)


def input_grad_kernel(place_ref, own_grads, other_grads, res_own, res_other, mid_ref, gain_ref, w_own, w_quarter,
                      own_out, send_out, weight, sems, *, steps):
    at = pl.program_id(0)
    quarter = D // 4
    half = w_own.shape[2]

    def copies():
        out = []
        for c in range(3):
            out.append(pltpu.make_async_copy(
                w_own.at[c], weight.at[:, pl.ds(c * half, half)], sems.at[c, 0]))
            for rel in range(4):
                place = pl.multiple_of((place_ref[1] ^ rel) * quarter, quarter)
                out.append(pltpu.make_async_copy(
                    w_quarter[rel].at[c], weight.at[pl.ds(place, quarter), pl.ds((3 + c) * half, half)],
                    sems.at[c, rel + 1]))
        return out

    @pl.when(at == 0)
    def _():
        for copy in copies():
            copy.start()

    mine = at < steps // 2
    compact = jnp.where(mine, res_own[...], res_other[...]).astype(F32)
    normal, factor = crms_normal(compact)

    @pl.when(at == 0)
    def _():
        for copy in copies():
            copy.wait()

    left = jnp.concatenate([ref[c] for part in (own_grads, other_grads) for c in range(3) for ref in part], axis=1)
    grad = dot_nt(left, weight[...])
    result = (mid_ref[...] + crms_back(normal, factor, gain_ref[...], grad)).astype(BF16)

    @pl.when(mine)
    def _():
        own_out[...] = result

    @pl.when(jnp.logical_not(mine))
    def _():
        send_out[...] = result


def input_grad(place, own_grads, other_grads, res_own, res_other, mid, gain, w_own, w_quarter, steps=4):
    length = mid.shape[0]
    block = length // steps
    own_map, other_map, whole_map = row_maps(steps)
    fixed = lambda i, s: (0, 0)
    mine, many = len(own_grads), len(own_grads) + len(other_grads)
    grad_spec = lambda value: pl.BlockSpec((3, block, value.shape[2]), lambda i, s: (0, whole_map(i, s)[0], 0))

    def body(place_ref, *refs):
        rest = refs[many:]
        input_grad_kernel(place_ref, refs[:mine], refs[mine:many], *rest[:5], rest[5:9], *rest[9:], steps=steps)

    sd = jax.ShapeDtypeStruct
    return pl.pallas_call(
        body,
        grid_spec=pltpu.PrefetchScalarGridSpec(
            num_scalar_prefetch=1, grid=(steps,),
            in_specs=[grad_spec(value) for value in (*own_grads, *other_grads)] + [pl.BlockSpec((block, D), own_map), pl.BlockSpec((block, D), other_map),
                      pl.BlockSpec((block, D), whole_map), pl.BlockSpec((1, D), fixed)] + [ANY] * 5,
            out_specs=[pl.BlockSpec((block, D), own_map), pl.BlockSpec((block, D), other_map)],
            scratch_shapes=[pltpu.VMEM((D, 3 * D), BF16), pltpu.SemaphoreType.DMA((3, 5))]),
        out_shape=[sd((length // 2, D), BF16), sd((length // 2, D), BF16)],
        compiler_params=pltpu.CompilerParams(vmem_limit_bytes=14 * MIB),
        cost_estimate=cost(9),
        name="input_grad",
    )(place, *own_grads, *other_grads, res_own, res_other, mid, gain, w_own, *w_quarter)


def pack_kernel(place_ref, own_ref, first_ref, second_ref, out_ref, *, steps):
    straight = place_ref[0] == 0
    own = jnp.transpose(own_ref[...].astype(F32))
    other = jnp.where(pl.program_id(0) < steps // 2, first_ref[...], second_ref[...])
    other = jnp.transpose(other.astype(F32))
    count = out_ref.shape[0]
    both = [jnp.where(straight, own, other)[:count], jnp.where(straight, other, own)[:count]]
    out_ref[...] = jnp.stack(both, 1).astype(BF16)


def pack_rows(place, own, first, second):
    positions = own.shape[0]
    steps = positions // 128
    own_map, other_map, _ = row_maps(steps)
    if second.shape[0] == positions:
        other_map = lambda i, s: (jnp.maximum(i, steps // 2), 0)
    packed = pl.pallas_call(
        functools.partial(pack_kernel, steps=steps),
        grid_spec=pltpu.PrefetchScalarGridSpec(
            num_scalar_prefetch=1, grid=(steps,),
            in_specs=[pl.BlockSpec((128, D), lambda i, s: (i, 0)), pl.BlockSpec((128, D), own_map),
                      pl.BlockSpec((128, D), other_map)],
            out_specs=pl.BlockSpec((D - 1, 2, 128), lambda i, s: (0, 0, i))),
        out_shape=jax.ShapeDtypeStruct((D - 1, 2, positions), BF16),
        compiler_params=pltpu.CompilerParams(vmem_limit_bytes=4 * MIB),
        cost_estimate=cost(0.1),
        name="pack_rows",
    )(place, own, first, second)
    return packed.transpose(1, 2, 0)


def swap(value, axis, bit, size):
    return lax.ppermute(value, axis, [(n, n ^ bit) for n in range(size)])


def meet(*values):
    return lax.optimization_barrier(values)


def add_low(*values):
    total = values[0].astype(F32)
    for value in values[1:]:
        total = total + value.astype(F32)
    return total.astype(BF16)


def chain_in(value):
    return lax.ppermute(value, "group", [(0, 1), (3, 2)])


def chain_across(value):
    return lax.ppermute(value, "group", [(1, 2), (2, 1)])


def chain_out(value):
    return lax.ppermute(value, "group", [(1, 0), (2, 3)])


def on_device(sizes, residual_in, piece_ids, norm_gains, qkv_weight, qv_bias, out_weight, fc_weight,
              fc_bias, proj_weight, out_biases, cotangent):
    n_dp, n_group, n_tensor = sizes["dp"], sizes["group"], sizes["tensor"]
    dp_at = lax.axis_index("dp")
    group_at = lax.axis_index("group")
    tensor_at = lax.axis_index("tensor")
    quarter_at = dp_at & 3
    proj_at = (dp_at & 1) | ((group_at & 1) << 1)
    place = jnp.stack([tensor_at, quarter_at, proj_at]).astype(jnp.int32)
    pad = ((0, 0), (0, 1))
    half = qv_bias.shape[1]
    hid = fc_bias.shape[0]
    pairs = half // 128
    y_swap = lambda value: swap(value, "tensor", 1, n_tensor)
    x_swap = lambda value: swap(value, "dp", 2, n_dp)
    c_swap = lambda value: swap(value, "dp", 1, n_dp)
    z_swap = lambda value: swap(value, "group", 1, n_group)

    def piece_of(shard, dim, at):
        rows = shard.shape[dim] // 4
        return lax.dynamic_slice_in_dim(shard, at * rows, rows, dim)

    qkv_piece = piece_of(qkv_weight, 1, quarter_at)
    qkv_y = y_swap(qkv_piece)
    bias_rows = jnp.concatenate([fc_bias.reshape(-1, D), qv_bias.reshape(1, D), jnp.zeros((13, D), BF16)], 0)
    res_own, res_send = unpack_rows(after(place, qkv_piece), residual_in, bias_rows)
    qkv_y, res_own, res_send, out_gated, fc_gated, proj_gated = meet(
        qkv_y, res_own, res_send, out_weight, fc_weight, proj_weight)
    res_other = y_swap(res_send)
    qkv_x = x_swap(qkv_y)
    qkv_c = c_swap(qkv_y)
    fc_piece = piece_of(fc_gated, 0, quarter_at)
    mix = jnp.concatenate([jnp.pad(piece_of(out_gated, 0, quarter_at), pad)]
                          + [fc_piece[:, n : n + D] for n in range(0, hid, D)], 0)
    proj_piece = jnp.pad(piece_of(proj_gated, 0, proj_at), pad)
    qkv_c, mix, proj_piece = meet(qkv_c, mix, proj_piece)
    mix_y, proj_y = y_swap(mix), y_swap(proj_piece)
    cot_own, cot_send = unpack_rows(after(place, mix, proj_piece), cotangent)
    out_own = jnp.pad(out_gated, pad)
    proj_own = jnp.pad(proj_gated, pad)
    qkv_x, res_other, out_own, proj_own, cot_send = meet(qkv_x, res_other, out_own, proj_own, cot_send)
    qkv_cx = c_swap(qkv_x)
    qkv_others = (qkv_y, qkv_c, qkv_x, qkv_cx)

    gains = norm_gains.astype(F32)
    end_biases = jnp.pad(out_biases, pad).astype(F32)
    count = residual_in.shape[1]
    bias_other = res_other[count : count + 8].astype(F32)
    fc_rows = hid // D
    qv_full = jnp.concatenate([qv_bias.astype(F32), bias_other[fc_rows].reshape(2, half)], axis=1)
    fc_full = jnp.concatenate([fc_bias.astype(F32).reshape(1, -1), bias_other[:fc_rows].reshape(1, -1)], axis=1)
    length = piece_ids.shape[1]
    flags = (lax.dynamic_index_in_dim(piece_ids, tensor_at, 0, keepdims=False)[:: length // 4] >= 0)
    flags = flags.astype(jnp.int32)

    normed_one, queries, key_rows, value_rows = project(
        place, res_own, res_other, gains[0:1], qv_full, qkv_weight, qkv_others)
    queries, cot_send = meet(queries, cot_send)
    cot_other = y_swap(cot_send)
    attended = attend_forward(flags, queries, key_rows, value_rows, 0, pairs)
    *attended, queries, mix_y, proj_y = meet(*attended, queries, mix_y, proj_y)
    mix_x, mix_c = x_swap(mix_y), c_swap(mix_y)
    proj_x, proj_c = z_swap(proj_y), c_swap(proj_y)
    attended = attend_forward(flags, queries, key_rows, value_rows, pairs, pairs, attended)
    attended, log_sums, mix_x, proj_x, cot_other = meet(*attended, mix_x, proj_x, cot_other)
    mix_others = (mix_y, mix_c, mix_x, c_swap(mix_x))
    proj_others = (proj_y, proj_c, proj_x, c_swap(proj_x))

    (normed_two, active, hidden_grad, out_mine, *out_send, middle_grad, branch_grad, attended_grad,
     middle_sums, own_sums, other_sums) = middle_stage(
        place, attended, res_own, res_other, cot_own, cot_other, gains[1:2], end_biases, fc_full,
        (out_own, fc_weight, proj_own, mix_others, proj_others))
    backward = functools.partial(attend_backward, flags, queries, key_rows, value_rows)
    restore = functools.partial(pack_rows, place)

    def small_outputs(small):
        part, first = hid // n_dp, half // n_dp
        return (jnp.concatenate([small[0:1, :D], small[0:1, D : 2 * D]], 0),
                lax.dynamic_slice(small, (0, 2 * D + hid + dp_at * first), (2, first)),
                lax.dynamic_slice(small, (0, 2 * D + dp_at * part), (1, part)).reshape(part),
                small[1:3, D : 2 * D - 1])

    if n_dp == 4 and n_group == 4:
        out_got = [y_swap(value) for value in out_send]
        proj_k, proj_s = proj_grad(after(place, middle_sums), active, cot_own, cot_other, attended, branch_grad)
        proj_k, proj_s, out_got[0] = meet(proj_k, proj_s, out_got[0])
        proj_c = c_swap(proj_s)
        fc_k, fc_s = fc_grad(after(place, proj_k), normed_two, hidden_grad)
        fc_k, fc_s, proj_k, proj_c, *out_got = meet(fc_k, fc_s, proj_k, proj_c, *out_got)
        fc_c = c_swap(fc_s)
        proj_fo = add_low(proj_k[1, 1], proj_c[1, 1])
        proj_xo = x_swap(proj_fo)
        proj_fm = add_low(proj_k[1, 0], after(proj_c, proj_fo)[1, 0])
        proj_xm = x_swap(proj_fm)
        fc_k, fc_c, proj_fo, proj_fm = meet(fc_k, fc_c, proj_fo, proj_fm)
        fc_away = add_low(fc_k[1], fc_c[1])
        fc_y = y_swap(fc_away)
        first, first_sums = backward(after(attended_grad, fc_away), log_sums, pairs, pairs)
        first, first_sums, proj_k, proj_c, proj_xo = meet(first, first_sums, proj_k, proj_c, proj_xo)
        proj_r = add_low(proj_k[0, 1], proj_c[0, 1], proj_xo)
        proj_y = y_swap(proj_r)
        qo_k, qo_s, qo_sum = qkv_grad(after(place, proj_r), normed_one, [first], qkv_others)
        qo_k, qo_s, fc_k, fc_c, fc_y = meet(qo_k, qo_s, fc_k, fc_c, fc_y)
        qo_c = c_swap(qo_s)
        fc_far = add_low(fc_k[0, 1], fc_c[0, 1], fc_y[1])
        fc_x = x_swap(fc_far)
        own_a, sums_a = backward(after(attended_grad, fc_far), log_sums, 0, pairs - 1)
        own_a, sums_a, proj_y, proj_xm, proj_k, proj_c, fc_x, qo_k, qo_c = meet(
            own_a, sums_a, proj_y, proj_xm, proj_k, proj_c, fc_x, qo_k, qo_c)
        proj_shard = add_low(proj_k[0, 0], proj_c[0, 0], proj_xm, proj_y)
        proj_z = chain_in(proj_shard)
        fc_shard = add_low(fc_k[0, 0], fc_c[0, 0], fc_y[0], fc_x)
        fc_z = chain_in(fc_shard)
        qo_f = add_low(qo_k[1], qo_c[1])
        qo_x = x_swap(qo_f)
        own_b, sums_b = backward(after(attended_grad, qo_f, proj_shard, fc_shard), log_sums, pairs - 1, 1)
        qm_k, qm_s, qm_sum = qkv_grad(after(place, own_b), normed_one, [own_a, own_b], [qkv_weight])
        qm_k, qm_s, qm_sum, qo_k, qo_c, qo_x, proj_shard, proj_z = meet(
            qm_k, qm_s, qm_sum, qo_k, qo_c, qo_x, proj_shard, proj_z)
        qm_c = c_swap(qm_s)
        in_sums = (qm_sum + qo_sum) / gains[0:1]
        small = jnp.concatenate([in_sums, middle_sums, own_sums, other_sums, sums_a, sums_b, first_sums], 1)
        small_z = z_swap(small)
        qo_r = add_low(qo_k[0], qo_c[0], qo_x)
        qo_y = y_swap(qo_r)
        proj_shard = add_low(proj_shard, proj_z)
        proj_z = chain_across(proj_shard)
        qm_k, qm_c, qo_r, proj_shard = meet(qm_k, qm_c, qo_r, proj_shard)
        qm_f = add_low(qm_k[1], qm_c[1])
        qm_x = x_swap(qm_f)
        in_mine, in_send = input_grad(
            after(place, qm_f), [own_a, own_b], [first], res_own, res_other, middle_grad, gains[0:1],
            qkv_weight, qkv_others)
        in_mine, in_send, qm_x, qo_y, proj_shard, proj_z, fc_shard, fc_z, small, small_z = meet(
            in_mine, in_send, qm_x, qo_y, proj_shard, proj_z, fc_shard, fc_z, small, small_z)
        small = small + small_z
        small_z = swap(small, "group", 2, n_group)
        last = add_low(qm_k[0], qm_c[0], qm_x, qo_y)
        last_z = chain_in(last)
        fc_shard = add_low(fc_shard, fc_z)
        fc_z = chain_across(fc_shard)
        proj_shard = add_low(proj_shard, proj_z)
        proj_z = chain_out(proj_shard)
        in_got = y_swap(in_send)
        block_out = restore(after(out_mine, last, proj_shard, fc_shard, small), *out_got)
        last, last_z, block_out, small, small_z, fc_shard, fc_z = meet(
            last, last_z, block_out, small, small_z, fc_shard, fc_z)
        small = small + small_z
        small_c = c_swap(small)
        last = add_low(last, last_z)
        last_z = chain_across(last)
        fc_shard = add_low(fc_shard, fc_z)
        fc_z = chain_out(fc_shard)
        middle_one = (group_at == 1) | (group_at == 2)
        small, small_c, last, fc_shard, proj_shard, proj_z = meet(small, small_c, last, fc_shard, proj_shard, proj_z)
        small = small + small_c
        small_x = x_swap(small)
        proj_shard = jnp.where(middle_one, proj_shard, proj_z)
        out_shard = proj_shard[hid // 4 :, : D - 1].astype(F32)
        proj_shard = proj_shard[: hid // 4, : D - 1].astype(F32)
        small, small_x, in_mine, in_got, last, last_z, fc_shard, proj_shard, out_shard = meet(
            small, small_x, in_mine, in_got, last, last_z, fc_shard, proj_shard, out_shard)
        last = add_low(last, last_z)
        last_z = chain_out(last)
        small = small + small_x
        split = 2 * D + hid
        mine = jnp.concatenate([small[:, :split], small[:, split + hid : split + hid + half]], 1)
        other = jnp.concatenate([small[:, : 2 * D], small[:, split : split + hid], small[:, split + hid + half :]], 1)
        small_y = y_swap(other)
        in_out = restore(after(in_mine, last), in_got, in_got)
        in_out, mine, small_y, fc_shard, fc_z = meet(in_out, mine, small_y, fc_shard, fc_z)
        small = small_outputs(mine + small_y)
        fc_shard = jnp.where(middle_one, fc_shard, fc_z).astype(F32)
        last, last_z, in_out, proj_shard, out_shard, fc_shard, *small = meet(
            last, last_z, in_out, proj_shard, out_shard, fc_shard, *small)
        qkv_shard = jnp.where(middle_one, last, last_z)
    else:
        first, first_sums = backward(attended_grad, log_sums, pairs, pairs)
        own, second_sums = backward(attended_grad, log_sums, 0, pairs)
        in_mine, in_send = input_grad(
            place, [own], [first], res_own, res_other, middle_grad, gains[0:1], qkv_weight, qkv_others)
        in_got = y_swap(in_send)
        in_out = restore(in_mine, in_got, in_got)
        block_out = restore(out_mine, *[y_swap(value) for value in out_send])
        qo_sum = qkv_grad(place, normed_one, [first], qkv_others)[2]
        qm_sum = qkv_grad(place, normed_one, [own], [qkv_weight])[2]

        def scatter(own, other):
            total = [lax.psum_scatter(value.astype(BF16), "dp", scatter_dimension=0, tiled=True)
                     for value in (own, other)]
            return lax.psum(add_low(total[0], y_swap(total[1])), "group")

        cot_rows = jnp.where(tensor_at == 0, jnp.concatenate([cot_own, cot_other]),
                             jnp.concatenate([cot_other, cot_own]))
        proj_shard = scatter(dot_tn(active[:, :hid], cot_rows), dot_tn(active[:, hid:], cot_rows))
        fc_shard = scatter(dot_tn(normed_two, hidden_grad[:, :hid]), dot_tn(normed_two, hidden_grad[:, hid:]))
        out_shard = scatter(dot_tn(attended[:, :half], branch_grad), dot_tn(attended[:, half:], branch_grad))
        proj_shard, out_shard = proj_shard[:, : D - 1].astype(F32), out_shard[:, : D - 1].astype(F32)
        fc_shard = fc_shard.astype(F32)
        qkv_shard = jnp.swapaxes(scatter(
            *[jnp.stack([dot_tn(normed_one, part[c]) for c in range(3)], 1) for part in (own, first)]), 0, 1)
        in_sums = (qm_sum + qo_sum) / gains[0:1]
        small = jnp.concatenate([in_sums, middle_sums, own_sums, second_sums], 1)
        small = small + y_swap(jnp.concatenate([in_sums, middle_sums, other_sums, first_sums], 1))
        small = small_outputs(lax.psum(small, ("dp", "group")))

    grad_gains, grad_qv_bias, grad_fc_bias, grad_out_biases = small
    return (
        block_out,
        in_out,
        grad_gains,
        qkv_shard.astype(F32),
        grad_qv_bias,
        out_shard,
        fc_shard,
        grad_fc_bias,
        proj_shard,
        grad_out_biases,
    )


def solution(mesh):
    sizes = dict(mesh.shape)
    in_specs = (
        P(("dp", "group"), "tensor", None),
        P(("dp", "group"), None),
        P(),
        P(None, None, "tensor"),
        P(None, "tensor"),
        P("tensor", None),
        P(None, "tensor"),
        P("tensor"),
        P("tensor", None),
        P(),
        P(("dp", "group"), "tensor", None),
    )
    out_specs = (
        P(("dp", "group"), "tensor", None),
        P(("dp", "group"), "tensor", None),
        P(),
        P(None, "dp", "tensor"),
        P(None, ("tensor", "dp")),
        P(("tensor", "dp"), None),
        P("dp", "tensor"),
        P(("tensor", "dp")),
        P(("tensor", "dp"), None),
        P(),
    )
    return jax.shard_map(
        functools.partial(on_device, sizes), mesh=mesh, in_specs=in_specs, out_specs=out_specs,
        check_vma=False)
```

```python
import functools
import jax
import jax.numpy as jnp
from jax import lax
from jax.sharding import PartitionSpec as P
from jax.experimental import pallas as pl
from jax.experimental.pallas import tpu as pltpu

D = 768
HD = 64
EPSILON = 1e-05
MASKED = -1e30
MIB = 1024 * 1024
F32 = jnp.float32
BF16 = jnp.bfloat16
COST_FLOPS = 0.4e9


def cost(micros):
    return pl.CostEstimate(flops=int(micros * COST_FLOPS), bytes_accessed=int(micros * 4e5), transcendentals=0)


def after(value, *others):
    return lax.optimization_barrier((value, *others))[0]


def dot_nn(a, b):
    return lax.dot_general(a, b, (((1,), (0,)), ((), ())), preferred_element_type=F32)


def dot_nt(a, b):
    return lax.dot_general(a, b, (((1,), (1,)), ((), ())), preferred_element_type=F32)


def dot_tn(a, b):
    return lax.dot_general(a, b, (((0,), (0,)), ((), ())), preferred_element_type=F32)


def dot_tn_halves(left, right):
    half = left.shape[0] // 2
    return (dot_tn(left[pl.ds(0, half), :], right[pl.ds(0, half), :])
            + dot_tn(left[pl.ds(half, half), :], right[pl.ds(half, half), :]))


def column_sum(values):
    return jnp.sum(values, axis=0, keepdims=True)


def lane_of(shape):
    return lax.broadcasted_iota(jnp.int32, shape, len(shape) - 1)


def attend_forward_kernel(flags_ref, q_ref, k_ref, v_ref, out_ref, log_ref, *, block):
    length = q_ref.shape[0]
    key_at = lax.broadcasted_iota(jnp.int32, (block, block), 0)
    query_at = lax.broadcasted_iota(jnp.int32, (block, block), 1)
    causal = key_at <= query_at
    head_lane = lane_of((block, 128)) // HD
    for at in range(length // block):
        rows = pl.ds(at * block, block)
        reach = (at + 1) * block
        keys = pl.ds(0, reach)
        seen = causal | (flags_ref[at] > 0)
        parts = []
        for head in range(2):
            q_head = jnp.where(head_lane == head, q_ref[rows, :], jnp.zeros((block, 128), BF16))
            scores = dot_nt(k_ref[keys, :], q_head)
            last = jnp.where(seen, scores[reach - block :], MASKED)
            scores = last if at == 0 else jnp.concatenate([scores[: reach - block], last], 0)
            top = jnp.max(scores, axis=0, keepdims=True)
            probs = jnp.exp(scores - top)
            total = jnp.sum(probs, axis=0, keepdims=True)
            log_ref[0, pl.ds(head, 1), rows] = top + jnp.log(total)
            probs = (probs * (1.0 / total)).astype(BF16)
            parts.append(dot_tn(probs, v_ref[keys, :]).astype(BF16))
        out_ref[rows, :] = jnp.where(head_lane == 0, parts[0], parts[1])


def attend_forward(flags, queries, key_rows, value_rows, first, pairs, into=None):
    length, width = queries.shape
    block = length // 4
    tile = pl.BlockSpec((length, 128), lambda h, f: (0, h + first))
    more = [] if into is None else list(into)

    def body(flags_ref, q_ref, k_ref, v_ref, *rest):
        attend_forward_kernel(flags_ref, q_ref, k_ref, v_ref, *rest[len(more):], block=block)

    return pl.pallas_call(
        body,
        grid_spec=pltpu.PrefetchScalarGridSpec(
            num_scalar_prefetch=1, grid=(pairs,),
            in_specs=[tile, tile, tile] + [pl.BlockSpec(memory_space=pl.ANY)] * len(more),
            out_specs=[tile, pl.BlockSpec((1, 8, length), lambda h, f: (h + first, 0, 0))]),
        out_shape=[jax.ShapeDtypeStruct((length, width), BF16),
                   jax.ShapeDtypeStruct((width // 128, 8, length), F32)],
        input_output_aliases={4 + n: n for n in range(len(more))},
        compiler_params=pltpu.CompilerParams(vmem_limit_bytes=6 * MIB),
        cost_estimate=cost(3.8 * pairs),
        name="attend_forward",
    )(flags, queries, key_rows, value_rows, *more)


def attend_backward_kernel(flags_ref, q_ref, k_ref, v_ref, up_ref, log_ref,
                           grad_ref, sum_ref, dk_acc, dv_acc, *, block):
    length = q_ref.shape[0]
    count = length // block
    key_at = lax.broadcasted_iota(jnp.int32, (block, block), 0)
    query_at = lax.broadcasted_iota(jnp.int32, (block, block), 1)
    causal = key_at <= query_at
    head_lane = lane_of((block, 128)) // HD
    full_lane = lane_of((length, 128)) // HD
    dq_sum = jnp.zeros((1, 128), F32)
    for at in reversed(range(count)):
        rows = pl.ds(at * block, block)
        reach = (at + 1) * block
        keys = pl.ds(0, reach)
        seen = causal | (flags_ref[at] > 0)
        dq = None
        for head in range(2):
            q_head = jnp.where(head_lane == head, q_ref[rows, :], jnp.zeros((block, 128), BF16))
            up_head = jnp.where(head_lane == head, up_ref[rows, :], jnp.zeros((block, 128), BF16))
            logs = log_ref[0, pl.ds(head, 1), rows]
            scores = dot_nt(k_ref[keys, :], q_head)
            last = jnp.where(seen, scores[reach - block :], MASKED)
            scores = last if at == 0 else jnp.concatenate([scores[: reach - block], last], 0)
            probs = jnp.exp(scores - logs)
            along = dot_nt(v_ref[keys, :], up_head)
            inner = jnp.sum(probs * along, axis=0, keepdims=True)
            low_grad = (probs * (along - inner)).astype(BF16)
            dv = dot_nn(probs.astype(BF16), up_head)
            dk = dot_nn(low_grad, q_head)
            if at == count - 1 and head == 0:
                dv_acc[keys, :] = dv
                dk_acc[keys, :] = dk
            else:
                dv_acc[keys, :] += dv
                dk_acc[keys, :] += dk
            k_head = jnp.where(full_lane[:reach] == head, k_ref[keys, :], jnp.zeros((reach, 128), BF16))
            part = dot_tn(low_grad, k_head)
            dq = part if dq is None else dq + part
        low_dq = (dq * HD ** (-0.5)).astype(BF16)
        grad_ref[0, rows, :] = low_dq
        dq_sum = dq_sum + column_sum(low_dq.astype(F32))
    grad_ref[1] = dk_acc[...].astype(BF16)
    low_dv = dv_acc[...].astype(BF16)
    grad_ref[2] = low_dv
    sum_ref[...] = jnp.zeros_like(sum_ref)
    sum_ref[0:1, :] = dq_sum
    sum_ref[1:2, :] = column_sum(low_dv.astype(F32))


def attend_backward(flags, queries, key_rows, value_rows, upstream, log_sums, first, pairs):
    length = queries.shape[0]
    tile = pl.BlockSpec((length, 128), lambda h, f: (0, h + first))
    return pl.pallas_call(
        functools.partial(attend_backward_kernel, block=length // 4),
        grid_spec=pltpu.PrefetchScalarGridSpec(
            num_scalar_prefetch=1, grid=(pairs,),
            in_specs=[tile, tile, tile, tile,
                      pl.BlockSpec((1, 8, length), lambda h, f: (h + first, 0, 0))],
            out_specs=[pl.BlockSpec((3, length, 128), lambda h, f: (0, 0, h)),
                       pl.BlockSpec((8, 128), lambda h, f: (0, h))],
            scratch_shapes=[pltpu.VMEM((length, 128), F32), pltpu.VMEM((length, 128), F32)]),
        out_shape=[jax.ShapeDtypeStruct((3, length, pairs * 128), BF16),
                   jax.ShapeDtypeStruct((8, pairs * 128), F32)],
        compiler_params=pltpu.CompilerParams(vmem_limit_bytes=9 * MIB),
        cost_estimate=cost(1 + 6 * pairs),
        name="attend_backward",
    )(flags, queries, key_rows, value_rows, upstream, log_sums)


def unpack_kernel(place_ref, rows_ref, *refs):
    own_ref, send_ref = refs[-2:]
    packed = rows_ref[...]
    packed = packed.reshape(packed.shape[0] * 2, packed.shape[2])
    shape = (packed.shape[0], D)
    row = lax.broadcasted_iota(jnp.int32, shape, 0)
    column = lax.broadcasted_iota(jnp.int32, shape, 1)
    pick = lambda seq: dot_tn(packed, jnp.where(row == 2 * column + seq, 1.0, 0.0).astype(BF16)).astype(BF16)
    count = own_ref.shape[0]
    send_ref[pl.ds(0, count), :] = pick(1 - place_ref[0])
    if len(refs) > 2:
        send_ref[pl.ds(count, refs[0].shape[0]), :] = refs[0][...]
    own_ref[...] = pick(place_ref[0])


def unpack_rows(place, rows, *extra):
    packed = rows.transpose(2, 0, 1)
    count = rows.shape[1]
    counts = [count, count + sum(value.shape[0] for value in extra)]
    fixed = lambda value: pl.BlockSpec(value.shape, lambda i, s: (0,) * len(value.shape))
    return pl.pallas_call(
        unpack_kernel,
        grid_spec=pltpu.PrefetchScalarGridSpec(
            num_scalar_prefetch=1, grid=(1,),
            in_specs=[fixed(packed)] + [fixed(value) for value in extra],
            out_specs=[pl.BlockSpec((n, D), lambda i, s: (0, 0)) for n in counts]),
        out_shape=[jax.ShapeDtypeStruct((n, D), BF16) for n in counts],
        compiler_params=pltpu.CompilerParams(vmem_limit_bytes=6 * MIB),
        cost_estimate=cost(5),
        name="unpack_rows",
    )(place, packed, *extra)


def decompress(compact):
    total = jnp.sum(compact, axis=-1, keepdims=True)
    return jnp.where(lane_of(compact.shape) == D - 1, -total, compact)


def crms_back(normal, factor, gain, grad):
    scaled = gain * grad
    du = factor * (scaled - normal * jnp.mean(scaled * normal, axis=-1, keepdims=True))
    lane = lane_of(du.shape)
    last = jnp.sum(jnp.where(lane == D - 1, du, 0.0), axis=-1, keepdims=True)
    return jnp.where(lane == D - 1, 0.0, du - last)


def crms_normal(compact):
    full = decompress(compact)
    factor = lax.rsqrt(jnp.mean(full * full, axis=-1, keepdims=True) + EPSILON)
    return full * factor, factor


def project_kernel(place_ref, own_ref, other_ref, gain_ref, bias_ref, w_own, w_quarter,
                   normed_ref, q_ref, k_ref, v_ref, weight, sems, *, steps):
    at = pl.program_id(0)
    quarter = D // 4
    half = w_own.shape[2]

    def copies():
        out = [pltpu.make_async_copy(w_own, weight.at[:, :, pl.ds(0, half)], sems.at[0])]
        for rel in range(4):
            place = pl.multiple_of((place_ref[1] ^ rel) * quarter, quarter)
            out.append(pltpu.make_async_copy(
                w_quarter[rel], weight.at[:, pl.ds(place, quarter), pl.ds(half, half)],
                sems.at[rel + 1]))
        return out

    @pl.when(at == 0)
    def _():
        for copy in copies():
            copy.start()

    compact = jnp.where(at < steps // 2, own_ref[...], other_ref[...]).astype(F32)
    normal, _ = crms_normal(compact)
    normed = (normal * gain_ref[...]).astype(BF16)
    normed_ref[...] = normed

    @pl.when(at == 0)
    def _():
        for copy in copies():
            copy.wait()

    q_ref[...] = ((dot_nn(normed, weight[0]) + bias_ref[0:1, :]).astype(BF16).astype(F32)
                  * HD ** (-0.5)).astype(BF16)
    k_ref[...] = dot_nn(normed, weight[1]).astype(BF16)
    v_ref[...] = (dot_nn(normed, weight[2]) + bias_ref[1:2, :]).astype(BF16)


def row_maps(steps):
    half = steps // 2
    own = lambda i, s: (jnp.minimum(i, half - 1), 0)
    other = lambda i, s: (jnp.maximum(i - half, 0), 0)
    whole = lambda i, s: (jnp.where(i < half, s[0] * half + i, (1 - s[0]) * half + i - half), 0)
    return own, other, whole


ANY = pl.BlockSpec(memory_space=pl.ANY)


def project(place, own, other, gain, bias, w_own, w_quarter, steps=4):
    length = own.shape[0] * 2
    block = length // steps
    own_map, other_map, whole_map = row_maps(steps)
    fixed = lambda i, s: (0, 0)
    wide = pl.BlockSpec((block, D), whole_map)
    out = jax.ShapeDtypeStruct((length, D), BF16)

    def body(place_ref, own_ref, other_ref, gain_ref, bias_ref, w_own, a, b, c, d, *rest):
        project_kernel(place_ref, own_ref, other_ref, gain_ref, bias_ref, w_own, (a, b, c, d),
                       *rest, steps=steps)

    return pl.pallas_call(
        body,
        grid_spec=pltpu.PrefetchScalarGridSpec(
            num_scalar_prefetch=1, grid=(steps,),
            in_specs=[pl.BlockSpec((block, D), own_map), pl.BlockSpec((block, D), other_map),
                      pl.BlockSpec((1, D), fixed), pl.BlockSpec((2, D), fixed)] + [ANY] * 5,
            out_specs=[wide] * 4,
            scratch_shapes=[pltpu.VMEM((3, D, D), BF16), pltpu.SemaphoreType.DMA((5,))]),
        out_shape=[out] * 4,
        compiler_params=pltpu.CompilerParams(vmem_limit_bytes=11 * MIB),
        cost_estimate=cost(10),
        name="norm_project",
    )(place, own, other, gain, bias, w_own, *w_quarter)


SQRT_2_PI = 0.7978845608028654


def gelu_pair(v):
    square = v * v
    inner = v * (SQRT_2_PI + (SQRT_2_PI * 0.044715) * square)
    tanh = jnp.tanh(inner)
    cdf = 0.5 + 0.5 * tanh
    slope = SQRT_2_PI + (3 * SQRT_2_PI * 0.044715) * square
    back = cdf + (0.5 * v) * (1.0 - tanh * tanh) * slope
    return v * cdf, back


def middle_kernel(place_ref, att_ref, res_own, res_other, cot_own, cot_other, gain_ref, end_ref,
                  fcb_ref, weights, two_ref, active_ref, hidden_ref, own_out, send_first, send_second,
                  mid_ref, branch_ref, upgrad_ref, sums_ref, own_sums, other_sums,
                  out_w, fc_w, proj_w, sems, *, steps, chunk):
    at = pl.program_id(0)
    hid = fc_w.shape[1]
    half = hid // 2
    o_own, f_own, p_own, quarters, proj_quarters = weights

    def copies(which):
        if which == 0:
            own, target = o_own, out_w.at[pl.ds(0, D // 2), :]
        elif which == 1:
            own, target = f_own, fc_w.at[:, pl.ds(0, half)]
        else:
            own, target = p_own, proj_w.at[pl.ds(0, half), :]
        out = [pltpu.make_async_copy(own, target, sems.at[which, 0])]
        for rel in range(4):
            source = proj_quarters[rel] if which == 2 else quarters[rel]
            to = place_ref[2 if which == 2 else 1] ^ rel
            if which == 0:
                moves = [(0, D // 8, out_w, D // 2 + to * (D // 8), None)]
            elif which == 1:
                moves = [(D // 8 + n * (D // 4), D // 4, fc_w, to * (D // 4), half + n * D)
                         for n in range(half // D)]
            else:
                moves = [(0, half // 4, proj_w, half + to * (half // 4), None)]
            for n, (start, rows, into, row, col) in enumerate(moves):
                spot = pl.ds(pl.multiple_of(row, rows), rows)
                out.append(pltpu.make_async_copy(
                    source.at[pl.ds(start, rows), :],
                    into.at[spot, :] if col is None else into.at[spot, pl.ds(col, D)],
                    sems.at[which, 1 + 2 * rel + n]))
        return out

    @pl.when(at == 0)
    def _():
        for which in range(3):
            for copy in copies(which):
                copy.start()
        for ref in (sums_ref, own_sums, other_sums):
            ref[...] = jnp.zeros_like(ref)
        for copy in copies(0):
            copy.wait()

    mine = at < steps // 2
    compact = jnp.where(mine, res_own[...], res_other[...]).astype(F32)
    cot_low = jnp.where(mine, cot_own[...], cot_other[...])
    middle = compact + dot_nn(att_ref[...], out_w[...]) + end_ref[0:1, :]
    normal, factor = crms_normal(middle)
    gain = gain_ref[...]
    two = (normal * gain).astype(BF16)
    two_ref[...] = two

    @pl.when(at == 0)
    def _():
        for which in (1, 2):
            for copy in copies(which):
                copy.wait()

    mlp = jnp.zeros((two.shape[0], D), F32)
    two_grad = jnp.zeros((two.shape[0], D), F32)
    for start in range(0, hid, chunk):
        cols = pl.ds(start, chunk)
        pre = dot_nn(two, fc_w[:, cols]) + fcb_ref[0:1, cols]
        act, slope = gelu_pair(pre)
        act = act.astype(BF16)
        active_ref[:, cols] = act
        mlp = mlp + dot_nn(act, proj_w[cols, :])
        hidden = (dot_nt(cot_low, proj_w[cols, :]) * slope).astype(BF16)
        hidden_ref[:, cols] = hidden
        to = own_sums if start < half else other_sums
        to[0:1, pl.ds(start % half, chunk)] += column_sum(hidden.astype(F32))
        two_grad = two_grad + dot_nt(hidden, fc_w[:, cols])
    block_out = (middle + mlp + end_ref[1:2, :]).astype(BF16)

    @pl.when(mine)
    def _():
        own_out[...] = block_out

    @pl.when(at == steps // 2)
    def _():
        send_first[...] = block_out

    @pl.when(at == steps // 2 + 1)
    def _():
        send_second[...] = block_out

    cot = cot_low.astype(F32)
    mid_grad = cot + crms_back(normal, factor, gain, two_grad)
    mid_ref[...] = mid_grad
    branch = mid_grad.astype(BF16)
    branch_ref[...] = branch
    upgrad_ref[...] = dot_nt(branch, out_w[...]).astype(BF16)
    sums_ref[0:1, :] += column_sum(two_grad * normal)
    sums_ref[1:2, :] += column_sum(branch.astype(F32))
    sums_ref[2:3, :] += column_sum(cot)


def middle_stage(place, att, res_own, res_other, cot_own, cot_other, gain, end_bias, fc_bias, weights,
                 steps=4, chunk=768):
    length = att.shape[0]
    hid = fc_bias.shape[1]
    block = length // steps
    own_map, other_map, whole_map = row_maps(steps)
    fixed = lambda i, s: (0, 0)
    flat = [*weights[:3], *weights[3], *weights[4]]
    spec = lambda w, m: pl.BlockSpec((block, w), m)

    def body(place_ref, *refs):
        ins, rest = refs[:8], refs[8:]
        w, rest = rest[:11], rest[11:]
        packed = (*w[:3], w[3:7], w[7:])
        middle_kernel(place_ref, *ins, packed, *rest, steps=steps, chunk=chunk)

    sd = jax.ShapeDtypeStruct
    return pl.pallas_call(
        body,
        grid_spec=pltpu.PrefetchScalarGridSpec(
            num_scalar_prefetch=1, grid=(steps,),
            in_specs=[spec(D, whole_map), spec(D, own_map), spec(D, other_map), spec(D, own_map),
                      spec(D, other_map), pl.BlockSpec((1, D), fixed), pl.BlockSpec((2, D), fixed),
                      pl.BlockSpec((1, hid), fixed)] + [ANY] * 11,
            out_specs=[spec(D, whole_map), spec(hid, whole_map), spec(hid, whole_map),
                       spec(D, own_map), spec(D, fixed), spec(D, fixed),
                       spec(D, whole_map), spec(D, whole_map), spec(D, whole_map),
                       pl.BlockSpec((8, D), fixed), pl.BlockSpec((8, hid // 2), fixed),
                       pl.BlockSpec((8, hid // 2), fixed)],
            scratch_shapes=[pltpu.VMEM((D, D), BF16), pltpu.VMEM((D, hid), BF16),
                            pltpu.VMEM((hid, D), BF16), pltpu.SemaphoreType.DMA((3, 9))]),
        out_shape=[sd((length, D), BF16), sd((length, hid), BF16), sd((length, hid), BF16),
                   sd((length // 2, D), BF16), sd((block, D), BF16), sd((block, D), BF16),
                   sd((length, D), F32), sd((length, D), BF16), sd((length, D), BF16),
                   sd((8, D), F32), sd((8, hid // 2), F32), sd((8, hid // 2), F32)],
        compiler_params=pltpu.CompilerParams(vmem_limit_bytes=36 * MIB),
        cost_estimate=cost(38),
        name="middle_stage",
    )(place, att, res_own, res_other, cot_own, cot_other, gain, end_bias, fc_bias, *flat)


def fc_grad_kernel(place_ref, left_ref, right_ref, keep_ref, send_ref, *, rows):
    flip = (place_ref[1] & 1) == 1
    both = dot_tn_halves(left_ref, right_ref).astype(BF16)
    for pair in range(2):
        to = pair ^ (place_ref[1] >> 1)
        low, high = both[2 * pair * rows : (2 * pair + 1) * rows], both[(2 * pair + 1) * rows : (2 * pair + 2) * rows]
        keep_ref[0, to] = jnp.where(flip, high, low)
        send_ref[0, to] = jnp.where(flip, low, high)


def fc_grad(place, left, right, chunk=768):
    length, width = left.shape
    rows = width // 4
    half = right.shape[1] // 2
    parts = half // chunk
    out = jax.ShapeDtypeStruct((2, 2, rows, half), BF16)
    out_spec = pl.BlockSpec((1, 2, rows, chunk), lambda n, s: (n // parts, 0, 0, n % parts))
    return pl.pallas_call(
        functools.partial(fc_grad_kernel, rows=rows),
        grid_spec=pltpu.PrefetchScalarGridSpec(
            num_scalar_prefetch=1, grid=(2 * parts,),
            in_specs=[pl.BlockSpec((length, width), lambda n, s: (0, 0)),
                      pl.BlockSpec((length, chunk), lambda n, s: (0, n))],
            out_specs=[out_spec, out_spec]),
        out_shape=[out, out],
        compiler_params=pltpu.CompilerParams(vmem_limit_bytes=12 * MIB),
        cost_estimate=cost(12),
        name="fc_grad",
    )(place, left, right)


def qkv_grad_kernel(place_ref, left_ref, *refs, rows, parts, pieces):
    right_refs, weight_refs = refs[:parts], refs[parts : parts + pieces]
    keep_ref, send_ref, sum_ref, total = refs[parts + pieces :]
    flip = (place_ref[1] & 1) == 1
    half = left_ref.shape[0] // 2
    width = sum(ref.shape[2] for ref in right_refs)
    both = None
    for n in range(2):
        part = pl.ds(n * half, half)
        right = jnp.concatenate([ref[c, part, :] for c in range(3) for ref in right_refs], axis=1)
        here = dot_tn(left_ref[part, :], right)
        both = here if both is None else both + here
    low_both = both.astype(BF16)
    for pair in range(2):
        to = pair ^ (place_ref[1] >> 1)
        for c in range(3):
            cols = slice(c * width, (c + 1) * width)
            low = low_both[2 * pair * rows : (2 * pair + 1) * rows, cols]
            high = low_both[(2 * pair + 1) * rows : (2 * pair + 2) * rows, cols]
            keep_ref[to, c] = jnp.where(flip, high, low)
            send_ref[to, c] = jnp.where(flip, low, high)
    sum_ref[...] = jnp.zeros_like(sum_ref)
    if pieces > 1:
        total[...] = both
    span = both.shape[0] // pieces
    for n in range(pieces):
        at = pl.multiple_of((place_ref[1] ^ n) * span, span) if pieces > 1 else 0
        folded = jnp.zeros((span, 128), F32)
        for c in range(3):
            here = total[pl.ds(at, span), pl.ds(c * width, width)] if pieces > 1 else both[:, c * width : (c + 1) * width]
            product = here * weight_refs[n][c].astype(F32)
            for k in range(0, width, 128):
                folded = folded + product[:, k : k + 128]
        total[pl.ds(at, span), pl.ds(0, 128)] = folded
    sum_ref[0:1, :] = column_sum(jnp.transpose(total[:, 0:128]))


def qkv_grad(place, left, rights, weights, col_at=0):
    length, width = left.shape
    rows = width // 4
    cols = sum(value.shape[2] for value in rights)
    out = jax.ShapeDtypeStruct((2, 3, rows, cols), BF16)
    whole = lambda value: pl.BlockSpec(value.shape, lambda i, s: (0,) * len(value.shape))
    sums = jax.ShapeDtypeStruct((8, width), F32)
    return pl.pallas_call(
        functools.partial(qkv_grad_kernel, rows=rows, parts=len(rights), pieces=len(weights)),
        grid_spec=pltpu.PrefetchScalarGridSpec(
            num_scalar_prefetch=1, grid=(1,),
            in_specs=[whole(value) for value in (left, *rights)]
            + [pl.BlockSpec((3, value.shape[1], cols), lambda i, s: (0, 0, col_at)) for value in weights],
            out_specs=[whole(out), whole(out), whole(sums)],
            scratch_shapes=[pltpu.VMEM((width, 3 * cols), F32)]),
        out_shape=[out, out, sums],
        compiler_params=pltpu.CompilerParams(vmem_limit_bytes=17 * MIB),
        cost_estimate=cost(6.5),
        name="qkv_grad",
    )(place, left, *rights, *weights)


def proj_grad_kernel(place_ref, own_act, other_act, own_cot, other_cot, att_ref, branch_ref, keep_ref, send_ref, rest,
                     *, rows):
    side, pair = pl.program_id(0), pl.program_id(1)
    flip = (place_ref[1] & 1) == 1
    out_rows = att_ref.shape[1] // 8

    @pl.when((side == 0) & (pair == 0))
    def _():
        rest[...] = dot_tn_halves(att_ref, branch_ref).astype(BF16)

    both = (dot_tn(own_act[...], own_cot[...]) + dot_tn(other_act[...], other_cot[...])).astype(BF16)
    base = pl.multiple_of((side * 4 + pair * 2) * out_rows, out_rows)
    more_low, more_high = rest[pl.ds(base, out_rows), :], rest[pl.ds(base + out_rows, out_rows), :]
    low, high = both[:rows], both[rows:]
    keep_ref[0, 0, pl.ds(0, rows), :] = jnp.where(flip, high, low)
    send_ref[0, 0, pl.ds(0, rows), :] = jnp.where(flip, low, high)
    keep_ref[0, 0, pl.ds(rows, out_rows), :] = jnp.where(flip, more_high, more_low)
    send_ref[0, 0, pl.ds(rows, out_rows), :] = jnp.where(flip, more_low, more_high)


def proj_grad(place, active, cot_own, cot_other, attended, branch):
    length, width = active.shape
    rows = width // 8
    out_rows = attended.shape[1] // 8
    out = jax.ShapeDtypeStruct((2, 2, rows + out_rows, D), BF16)
    out_spec = pl.BlockSpec((1, 1, rows + out_rows, D), lambda n, j, s: (j ^ (s[1] >> 1), n, 0, 0))
    fixed = lambda count: pl.BlockSpec((count, D), lambda n, j, s: (0, 0))
    return pl.pallas_call(
        functools.partial(proj_grad_kernel, rows=rows),
        grid_spec=pltpu.PrefetchScalarGridSpec(
            num_scalar_prefetch=1, grid=(2, 2),
            in_specs=[pl.BlockSpec((length // 2, 2 * rows), lambda n, j, s: (s[0], n * 2 + j)),
                      pl.BlockSpec((length // 2, 2 * rows), lambda n, j, s: (1 - s[0], n * 2 + j)),
                      fixed(length // 2), fixed(length // 2), fixed(length), fixed(length)],
            out_specs=[out_spec, out_spec],
            scratch_shapes=[pltpu.VMEM((attended.shape[1], D), BF16)]),
        out_shape=[out, out],
        compiler_params=pltpu.CompilerParams(vmem_limit_bytes=19 * MIB),
        cost_estimate=cost(13),
        name="proj_grad",
    )(place, active, active, cot_own, cot_other, attended, branch)


def input_grad_kernel(place_ref, own_grads, other_grads, res_own, res_other, mid_ref, gain_ref, w_own, w_quarter,
                      own_out, send_out, weight, sems, *, steps):
    at = pl.program_id(0)
    quarter = D // 4
    half = w_own.shape[2]

    def copies():
        out = []
        for c in range(3):
            out.append(pltpu.make_async_copy(
                w_own.at[c], weight.at[:, pl.ds(c * half, half)], sems.at[c, 0]))
            for rel in range(4):
                place = pl.multiple_of((place_ref[1] ^ rel) * quarter, quarter)
                out.append(pltpu.make_async_copy(
                    w_quarter[rel].at[c], weight.at[pl.ds(place, quarter), pl.ds((3 + c) * half, half)],
                    sems.at[c, rel + 1]))
        return out

    @pl.when(at == 0)
    def _():
        for copy in copies():
            copy.start()

    mine = at < steps // 2
    compact = jnp.where(mine, res_own[...], res_other[...]).astype(F32)
    normal, factor = crms_normal(compact)

    @pl.when(at == 0)
    def _():
        for copy in copies():
            copy.wait()

    left = jnp.concatenate([ref[c] for part in (own_grads, other_grads) for c in range(3) for ref in part], axis=1)
    grad = dot_nt(left, weight[...])
    result = (mid_ref[...] + crms_back(normal, factor, gain_ref[...], grad)).astype(BF16)

    @pl.when(mine)
    def _():
        own_out[...] = result

    @pl.when(jnp.logical_not(mine))
    def _():
        send_out[...] = result


def input_grad(place, own_grads, other_grads, res_own, res_other, mid, gain, w_own, w_quarter, steps=4):
    length = mid.shape[0]
    block = length // steps
    own_map, other_map, whole_map = row_maps(steps)
    fixed = lambda i, s: (0, 0)
    mine, many = len(own_grads), len(own_grads) + len(other_grads)
    grad_spec = lambda value: pl.BlockSpec((3, block, value.shape[2]), lambda i, s: (0, whole_map(i, s)[0], 0))

    def body(place_ref, *refs):
        rest = refs[many:]
        input_grad_kernel(place_ref, refs[:mine], refs[mine:many], *rest[:5], rest[5:9], *rest[9:], steps=steps)

    sd = jax.ShapeDtypeStruct
    return pl.pallas_call(
        body,
        grid_spec=pltpu.PrefetchScalarGridSpec(
            num_scalar_prefetch=1, grid=(steps,),
            in_specs=[grad_spec(value) for value in (*own_grads, *other_grads)] + [pl.BlockSpec((block, D), own_map), pl.BlockSpec((block, D), other_map),
                      pl.BlockSpec((block, D), whole_map), pl.BlockSpec((1, D), fixed)] + [ANY] * 5,
            out_specs=[pl.BlockSpec((block, D), own_map), pl.BlockSpec((block, D), other_map)],
            scratch_shapes=[pltpu.VMEM((D, 3 * D), BF16), pltpu.SemaphoreType.DMA((3, 5))]),
        out_shape=[sd((length // 2, D), BF16), sd((length // 2, D), BF16)],
        compiler_params=pltpu.CompilerParams(vmem_limit_bytes=14 * MIB),
        cost_estimate=cost(9),
        name="input_grad",
    )(place, *own_grads, *other_grads, res_own, res_other, mid, gain, w_own, *w_quarter)


def pack_kernel(place_ref, own_ref, first_ref, second_ref, out_ref, *, steps):
    straight = place_ref[0] == 0
    own = jnp.transpose(own_ref[...].astype(F32))
    other = jnp.where(pl.program_id(0) < steps // 2, first_ref[...], second_ref[...])
    other = jnp.transpose(other.astype(F32))
    count = out_ref.shape[0]
    both = [jnp.where(straight, own, other)[:count], jnp.where(straight, other, own)[:count]]
    out_ref[...] = jnp.stack(both, 1).astype(BF16)


def pack_rows(place, own, first, second):
    positions = own.shape[0]
    steps = positions // 128
    own_map, other_map, _ = row_maps(steps)
    if second.shape[0] == positions:
        other_map = lambda i, s: (jnp.maximum(i, steps // 2), 0)
    packed = pl.pallas_call(
        functools.partial(pack_kernel, steps=steps),
        grid_spec=pltpu.PrefetchScalarGridSpec(
            num_scalar_prefetch=1, grid=(steps,),
            in_specs=[pl.BlockSpec((128, D), lambda i, s: (i, 0)), pl.BlockSpec((128, D), own_map),
                      pl.BlockSpec((128, D), other_map)],
            out_specs=pl.BlockSpec((D - 1, 2, 128), lambda i, s: (0, 0, i))),
        out_shape=jax.ShapeDtypeStruct((D - 1, 2, positions), BF16),
        compiler_params=pltpu.CompilerParams(vmem_limit_bytes=4 * MIB),
        cost_estimate=cost(0.1),
        name="pack_rows",
    )(place, own, first, second)
    return packed.transpose(1, 2, 0)


def swap(value, axis, bit, size):
    return lax.ppermute(value, axis, [(n, n ^ bit) for n in range(size)])


def meet(*values):
    return lax.optimization_barrier(values)


def add_low(*values):
    total = values[0].astype(F32)
    for value in values[1:]:
        total = total + value.astype(F32)
    return total.astype(BF16)


def chain_in(value):
    return lax.ppermute(value, "group", [(0, 1), (3, 2)])


def chain_across(value):
    return lax.ppermute(value, "group", [(1, 2), (2, 1)])


def chain_out(value):
    return lax.ppermute(value, "group", [(1, 0), (2, 3)])


def on_device(sizes, residual_in, piece_ids, norm_gains, qkv_weight, qv_bias, out_weight, fc_weight,
              fc_bias, proj_weight, out_biases, cotangent):
    n_dp, n_group, n_tensor = sizes["dp"], sizes["group"], sizes["tensor"]
    dp_at = lax.axis_index("dp")
    group_at = lax.axis_index("group")
    tensor_at = lax.axis_index("tensor")
    quarter_at = dp_at & 3
    proj_at = (dp_at & 1) | ((group_at & 1) << 1)
    place = jnp.stack([tensor_at, quarter_at, proj_at]).astype(jnp.int32)
    pad = ((0, 0), (0, 1))
    half = qv_bias.shape[1]
    hid = fc_bias.shape[0]
    pairs = half // 128
    y_swap = lambda value: swap(value, "tensor", 1, n_tensor)
    x_swap = lambda value: swap(value, "dp", 2, n_dp)
    c_swap = lambda value: swap(value, "dp", 1, n_dp)
    z_swap = lambda value: swap(value, "group", 1, n_group)

    def piece_of(shard, dim, at):
        rows = shard.shape[dim] // 4
        return lax.dynamic_slice_in_dim(shard, at * rows, rows, dim)

    qkv_piece = piece_of(qkv_weight, 1, quarter_at)
    qkv_y = y_swap(qkv_piece)
    bias_rows = jnp.concatenate([fc_bias.reshape(-1, D), qv_bias.reshape(1, D), jnp.zeros((13, D), BF16)], 0)
    res_own, res_send = unpack_rows(after(place, qkv_piece), residual_in, bias_rows)
    qkv_y, res_own, res_send, out_gated, fc_gated, proj_gated = meet(
        qkv_y, res_own, res_send, out_weight, fc_weight, proj_weight)
    res_other = y_swap(res_send)
    qkv_x = x_swap(qkv_y)
    qkv_c = c_swap(qkv_y)
    fc_piece = piece_of(fc_gated, 0, quarter_at)
    mix = jnp.concatenate([jnp.pad(piece_of(out_gated, 0, quarter_at), pad)]
                          + [fc_piece[:, n : n + D] for n in range(0, hid, D)], 0)
    proj_piece = jnp.pad(piece_of(proj_gated, 0, proj_at), pad)
    qkv_c, mix, proj_piece = meet(qkv_c, mix, proj_piece)
    mix_y, proj_y = y_swap(mix), y_swap(proj_piece)
    cot_own, cot_send = unpack_rows(after(place, mix, proj_piece), cotangent)
    out_own = jnp.pad(out_gated, pad)
    proj_own = jnp.pad(proj_gated, pad)
    qkv_x, res_other, out_own, proj_own, cot_send = meet(qkv_x, res_other, out_own, proj_own, cot_send)
    qkv_cx = c_swap(qkv_x)
    qkv_others = (qkv_y, qkv_c, qkv_x, qkv_cx)

    gains = norm_gains.astype(F32)
    end_biases = jnp.pad(out_biases, pad).astype(F32)
    count = residual_in.shape[1]
    bias_other = res_other[count : count + 8].astype(F32)
    fc_rows = hid // D
    qv_full = jnp.concatenate([qv_bias.astype(F32), bias_other[fc_rows].reshape(2, half)], axis=1)
    fc_full = jnp.concatenate([fc_bias.astype(F32).reshape(1, -1), bias_other[:fc_rows].reshape(1, -1)], axis=1)
    length = piece_ids.shape[1]
    flags = (lax.dynamic_index_in_dim(piece_ids, tensor_at, 0, keepdims=False)[:: length // 4] >= 0)
    flags = flags.astype(jnp.int32)

    normed_one, queries, key_rows, value_rows = project(
        place, res_own, res_other, gains[0:1], qv_full, qkv_weight, qkv_others)
    queries, cot_send = meet(queries, cot_send)
    cot_other = y_swap(cot_send)
    attended = attend_forward(flags, queries, key_rows, value_rows, 0, pairs)
    *attended, queries, mix_y, proj_y = meet(*attended, queries, mix_y, proj_y)
    mix_x, mix_c = x_swap(mix_y), c_swap(mix_y)
    proj_x, proj_c = z_swap(proj_y), c_swap(proj_y)
    attended = attend_forward(flags, queries, key_rows, value_rows, pairs, pairs, attended)
    attended, log_sums, mix_x, proj_x, cot_other = meet(*attended, mix_x, proj_x, cot_other)
    mix_others = (mix_y, mix_c, mix_x, c_swap(mix_x))
    proj_others = (proj_y, proj_c, proj_x, c_swap(proj_x))

    (normed_two, active, hidden_grad, out_mine, *out_send, middle_grad, branch_grad, attended_grad,
     middle_sums, own_sums, other_sums) = middle_stage(
        place, attended, res_own, res_other, cot_own, cot_other, gains[1:2], end_biases, fc_full,
        (out_own, fc_weight, proj_own, mix_others, proj_others))
    backward = functools.partial(attend_backward, flags, queries, key_rows, value_rows)
    restore = functools.partial(pack_rows, place)

    def small_outputs(small):
        part, first = hid // n_dp, half // n_dp
        return (jnp.concatenate([small[0:1, :D], small[0:1, D : 2 * D]], 0),
                lax.dynamic_slice(small, (0, 2 * D + hid + dp_at * first), (2, first)),
                lax.dynamic_slice(small, (0, 2 * D + dp_at * part), (1, part)).reshape(part),
                small[1:3, D : 2 * D - 1])

    if n_dp == 4 and n_group == 4:
        out_got = [y_swap(value) for value in out_send]
        proj_k, proj_s = proj_grad(after(place, middle_sums), active, cot_own, cot_other, attended, branch_grad)
        proj_k, proj_s, out_got[0] = meet(proj_k, proj_s, out_got[0])
        proj_c = c_swap(proj_s)
        fc_k, fc_s = fc_grad(after(place, proj_k), normed_two, hidden_grad)
        fc_k, fc_s, proj_k, proj_c, *out_got = meet(fc_k, fc_s, proj_k, proj_c, *out_got)
        fc_c = c_swap(fc_s)
        proj_fo = add_low(proj_k[1, 1], proj_c[1, 1])
        proj_xo = x_swap(proj_fo)
        proj_fm = add_low(proj_k[1, 0], after(proj_c, proj_fo)[1, 0])
        proj_xm = x_swap(proj_fm)
        fc_k, fc_c, proj_fo, proj_fm = meet(fc_k, fc_c, proj_fo, proj_fm)
        fc_away = add_low(fc_k[1], fc_c[1])
        fc_y = y_swap(fc_away)
        first, first_sums = backward(after(attended_grad, fc_away), log_sums, pairs, pairs)
        first, first_sums, proj_k, proj_c, proj_xo = meet(first, first_sums, proj_k, proj_c, proj_xo)
        proj_r = add_low(proj_k[0, 1], proj_c[0, 1], proj_xo)
        proj_y = y_swap(proj_r)
        qo_k, qo_s, qo_sum = qkv_grad(after(place, proj_r), normed_one, [first], qkv_others)
        qo_k, qo_s, fc_k, fc_c, fc_y = meet(qo_k, qo_s, fc_k, fc_c, fc_y)
        qo_c = c_swap(qo_s)
        fc_far = add_low(fc_k[0, 1], fc_c[0, 1], fc_y[1])
        fc_x = x_swap(fc_far)
        own_a, sums_a = backward(after(attended_grad, fc_far), log_sums, 0, pairs - 1)
        own_a, sums_a, proj_y, proj_xm, proj_k, proj_c, fc_x, qo_k, qo_c = meet(
            own_a, sums_a, proj_y, proj_xm, proj_k, proj_c, fc_x, qo_k, qo_c)
        proj_shard = add_low(proj_k[0, 0], proj_c[0, 0], proj_xm, proj_y)
        proj_z = chain_in(proj_shard)
        fc_shard = add_low(fc_k[0, 0], fc_c[0, 0], fc_y[0], fc_x)
        fc_z = chain_in(fc_shard)
        qo_f = add_low(qo_k[1], qo_c[1])
        qo_x = x_swap(qo_f)
        own_b, sums_b = backward(after(attended_grad, qo_f, proj_shard, fc_shard), log_sums, pairs - 1, 1)
        qm_k, qm_s, qm_sum = qkv_grad(after(place, own_b), normed_one, [own_a, own_b], [qkv_weight])
        qm_k, qm_s, qm_sum, qo_k, qo_c, qo_x = meet(qm_k, qm_s, qm_sum, qo_k, qo_c, qo_x)
        qm_c = c_swap(qm_s)
        in_sums = (qm_sum + qo_sum) / gains[0:1]
        small = jnp.concatenate([in_sums, middle_sums, own_sums, other_sums, sums_a, sums_b, first_sums], 1)
        small_c = c_swap(small)
        qo_r = add_low(qo_k[0], qo_c[0], qo_x)
        qo_y = y_swap(qo_r)
        qm_k, qm_c, qo_r, small, small_c = meet(qm_k, qm_c, qo_r, small, small_c)
        small = small + small_c
        small_x = x_swap(small)
        qm_f = add_low(after(qm_k, small)[1], qm_c[1])
        qm_x = x_swap(qm_f)
        qm_f, proj_shard, proj_z = meet(qm_f, proj_shard, proj_z)
        proj_shard = add_low(proj_shard, proj_z)
        proj_z = chain_across(proj_shard)
        block_out = restore(after(out_mine, proj_shard), *out_got)
        block_out, fc_shard, fc_z, small, small_x = meet(block_out, fc_shard, fc_z, small, small_x)
        fc_shard = add_low(fc_shard, fc_z)
        fc_z = chain_across(fc_shard)
        small = small + small_x
        split = 2 * D + hid
        mine = jnp.concatenate([small[:, :split], small[:, split + hid : split + hid + half]], 1)
        other = jnp.concatenate([small[:, : 2 * D], small[:, split : split + hid], small[:, split + hid + half :]], 1)
        small_y = y_swap(other)
        qm_k, qm_c, qm_x, qo_y, fc_shard, mine, small_y, proj_shard, proj_z = meet(
            qm_k, qm_c, qm_x, qo_y, fc_shard, mine, small_y, proj_shard, proj_z)
        last = add_low(qm_k[0], qm_c[0], qm_x, qo_y)
        last_z = chain_in(last)
        small = mine + small_y
        small_z = chain_in(small)
        proj_shard = add_low(after(proj_shard, last, small), proj_z)
        proj_z = chain_out(proj_shard)
        in_mine, in_send = input_grad(
            after(place, last, proj_shard, small), [own_a, own_b], [first], res_own, res_other, middle_grad,
            gains[0:1], qkv_weight, qkv_others)
        in_mine, in_send, last, last_z, fc_shard, fc_z, small, small_z = meet(
            in_mine, in_send, last, last_z, fc_shard, fc_z, small, small_z)
        last = add_low(last, last_z)
        last_z = chain_across(last)
        small = small + small_z
        small_z = chain_across(small)
        fc_shard = add_low(after(fc_shard, last, small), fc_z)
        fc_z = chain_out(fc_shard)
        in_got = y_swap(in_send)
        middle_one = (group_at == 1) | (group_at == 2)
        small, last, fc_shard, proj_shard, proj_z = meet(small, last, fc_shard, proj_shard, proj_z)
        proj_shard = jnp.where(middle_one, proj_shard, proj_z)
        out_shard = proj_shard[hid // 4 :, : D - 1].astype(F32)
        proj_shard = proj_shard[: hid // 4, : D - 1].astype(F32)
        small, small_z, last, last_z, proj_shard, out_shard = meet(
            small, small_z, last, last_z, proj_shard, out_shard)
        last = add_low(last, last_z)
        last_z = chain_out(last)
        small = small + small_z
        small_z = chain_out(small)
        in_mine, in_got, last, small = meet(in_mine, in_got, last, small)
        in_out = restore(in_mine, in_got, in_got)
        in_out, fc_shard, fc_z = meet(in_out, fc_shard, fc_z)
        fc_shard = jnp.where(middle_one, fc_shard, fc_z).astype(F32)
        fc_shard, small, small_z = meet(fc_shard, small, small_z)
        small = small_outputs(jnp.where(middle_one, small, small_z))
        last, last_z, in_out, proj_shard, out_shard, fc_shard, *small = meet(
            last, last_z, in_out, proj_shard, out_shard, fc_shard, *small)
        qkv_shard = jnp.where(middle_one, last, last_z)
    else:
        first, first_sums = backward(attended_grad, log_sums, pairs, pairs)
        own, second_sums = backward(attended_grad, log_sums, 0, pairs)
        in_mine, in_send = input_grad(
            place, [own], [first], res_own, res_other, middle_grad, gains[0:1], qkv_weight, qkv_others)
        in_got = y_swap(in_send)
        in_out = restore(in_mine, in_got, in_got)
        block_out = restore(out_mine, *[y_swap(value) for value in out_send])
        qo_sum = qkv_grad(place, normed_one, [first], qkv_others)[2]
        qm_sum = qkv_grad(place, normed_one, [own], [qkv_weight])[2]

        def scatter(own, other):
            total = [lax.psum_scatter(value.astype(BF16), "dp", scatter_dimension=0, tiled=True)
                     for value in (own, other)]
            return lax.psum(add_low(total[0], y_swap(total[1])), "group")

        cot_rows = jnp.where(tensor_at == 0, jnp.concatenate([cot_own, cot_other]),
                             jnp.concatenate([cot_other, cot_own]))
        proj_shard = scatter(dot_tn(active[:, :hid], cot_rows), dot_tn(active[:, hid:], cot_rows))
        fc_shard = scatter(dot_tn(normed_two, hidden_grad[:, :hid]), dot_tn(normed_two, hidden_grad[:, hid:]))
        out_shard = scatter(dot_tn(attended[:, :half], branch_grad), dot_tn(attended[:, half:], branch_grad))
        proj_shard, out_shard = proj_shard[:, : D - 1].astype(F32), out_shard[:, : D - 1].astype(F32)
        fc_shard = fc_shard.astype(F32)
        qkv_shard = jnp.swapaxes(scatter(
            *[jnp.stack([dot_tn(normed_one, part[c]) for c in range(3)], 1) for part in (own, first)]), 0, 1)
        in_sums = (qm_sum + qo_sum) / gains[0:1]
        small = jnp.concatenate([in_sums, middle_sums, own_sums, second_sums], 1)
        small = small + y_swap(jnp.concatenate([in_sums, middle_sums, other_sums, first_sums], 1))
        small = small_outputs(lax.psum(small, ("dp", "group")))

    grad_gains, grad_qv_bias, grad_fc_bias, grad_out_biases = small
    return (
        block_out,
        in_out,
        grad_gains,
        qkv_shard.astype(F32),
        grad_qv_bias,
        out_shard,
        fc_shard,
        grad_fc_bias,
        proj_shard,
        grad_out_biases,
    )


def solution(mesh):
    sizes = dict(mesh.shape)
    in_specs = (
        P(("dp", "group"), "tensor", None),
        P(("dp", "group"), None),
        P(),
        P(None, None, "tensor"),
        P(None, "tensor"),
        P("tensor", None),
        P(None, "tensor"),
        P("tensor"),
        P("tensor", None),
        P(),
        P(("dp", "group"), "tensor", None),
    )
    out_specs = (
        P(("dp", "group"), "tensor", None),
        P(("dp", "group"), "tensor", None),
        P(),
        P(None, "dp", "tensor"),
        P(None, ("tensor", "dp")),
        P(("tensor", "dp"), None),
        P("dp", "tensor"),
        P(("tensor", "dp")),
        P(("tensor", "dp"), None),
        P(),
    )
    return jax.shard_map(
        functools.partial(on_device, sizes), mesh=mesh, in_specs=in_specs, out_specs=out_specs,
        check_vma=False)
```

```python
import functools
import jax
import jax.numpy as jnp
from jax import lax
from jax.sharding import PartitionSpec as P
from jax.experimental import pallas as pl
from jax.experimental.pallas import tpu as pltpu

D = 768
HD = 64
EPSILON = 1e-05
MASKED = -1e30
MIB = 1024 * 1024
F32 = jnp.float32
BF16 = jnp.bfloat16
COST_FLOPS = 0.4e9


def cost(micros):
    return pl.CostEstimate(flops=int(micros * COST_FLOPS), bytes_accessed=int(micros * 4e5), transcendentals=0)


def after(value, *others):
    return lax.optimization_barrier((value, *others))[0]


def dot_nn(a, b):
    return lax.dot_general(a, b, (((1,), (0,)), ((), ())), preferred_element_type=F32)


def dot_nt(a, b):
    return lax.dot_general(a, b, (((1,), (1,)), ((), ())), preferred_element_type=F32)


def dot_tn(a, b):
    return lax.dot_general(a, b, (((0,), (0,)), ((), ())), preferred_element_type=F32)


def dot_tn_halves(left, right):
    half = left.shape[0] // 2
    return (dot_tn(left[pl.ds(0, half), :], right[pl.ds(0, half), :])
            + dot_tn(left[pl.ds(half, half), :], right[pl.ds(half, half), :]))


def column_sum(values):
    return jnp.sum(values, axis=0, keepdims=True)


def lane_of(shape):
    return lax.broadcasted_iota(jnp.int32, shape, len(shape) - 1)


def attend_forward_kernel(flags_ref, q_ref, k_ref, v_ref, out_ref, log_ref, *, block):
    length = q_ref.shape[0]
    key_at = lax.broadcasted_iota(jnp.int32, (block, block), 0)
    query_at = lax.broadcasted_iota(jnp.int32, (block, block), 1)
    causal = key_at <= query_at
    head_lane = lane_of((block, 128)) // HD
    for at in range(length // block):
        rows = pl.ds(at * block, block)
        reach = (at + 1) * block
        keys = pl.ds(0, reach)
        seen = causal | (flags_ref[at] > 0)
        parts = []
        for head in range(2):
            q_head = jnp.where(head_lane == head, q_ref[rows, :], jnp.zeros((block, 128), BF16))
            scores = dot_nt(k_ref[keys, :], q_head)
            last = jnp.where(seen, scores[reach - block :], MASKED)
            scores = last if at == 0 else jnp.concatenate([scores[: reach - block], last], 0)
            top = jnp.max(scores, axis=0, keepdims=True)
            probs = jnp.exp(scores - top)
            total = jnp.sum(probs, axis=0, keepdims=True)
            log_ref[0, pl.ds(head, 1), rows] = top + jnp.log(total)
            probs = (probs * (1.0 / total)).astype(BF16)
            parts.append(dot_tn(probs, v_ref[keys, :]).astype(BF16))
        out_ref[rows, :] = jnp.where(head_lane == 0, parts[0], parts[1])


def attend_forward(flags, queries, key_rows, value_rows, first, pairs, into=None):
    length, width = queries.shape
    block = length // 4
    tile = pl.BlockSpec((length, 128), lambda h, f: (0, h + first))
    more = [] if into is None else list(into)

    def body(flags_ref, q_ref, k_ref, v_ref, *rest):
        attend_forward_kernel(flags_ref, q_ref, k_ref, v_ref, *rest[len(more):], block=block)

    return pl.pallas_call(
        body,
        grid_spec=pltpu.PrefetchScalarGridSpec(
            num_scalar_prefetch=1, grid=(pairs,),
            in_specs=[tile, tile, tile] + [pl.BlockSpec(memory_space=pl.ANY)] * len(more),
            out_specs=[tile, pl.BlockSpec((1, 8, length), lambda h, f: (h + first, 0, 0))]),
        out_shape=[jax.ShapeDtypeStruct((length, width), BF16),
                   jax.ShapeDtypeStruct((width // 128, 8, length), F32)],
        input_output_aliases={4 + n: n for n in range(len(more))},
        compiler_params=pltpu.CompilerParams(vmem_limit_bytes=6 * MIB),
        cost_estimate=cost(3.8 * pairs),
        name="attend_forward",
    )(flags, queries, key_rows, value_rows, *more)


def attend_backward_kernel(flags_ref, q_ref, k_ref, v_ref, up_ref, log_ref,
                           grad_ref, sum_ref, dk_acc, dv_acc, *, block):
    length = q_ref.shape[0]
    count = length // block
    key_at = lax.broadcasted_iota(jnp.int32, (block, block), 0)
    query_at = lax.broadcasted_iota(jnp.int32, (block, block), 1)
    causal = key_at <= query_at
    head_lane = lane_of((block, 128)) // HD
    full_lane = lane_of((length, 128)) // HD
    dq_sum = jnp.zeros((1, 128), F32)
    for at in reversed(range(count)):
        rows = pl.ds(at * block, block)
        reach = (at + 1) * block
        keys = pl.ds(0, reach)
        seen = causal | (flags_ref[at] > 0)
        dq = None
        for head in range(2):
            q_head = jnp.where(head_lane == head, q_ref[rows, :], jnp.zeros((block, 128), BF16))
            up_head = jnp.where(head_lane == head, up_ref[rows, :], jnp.zeros((block, 128), BF16))
            logs = log_ref[0, pl.ds(head, 1), rows]
            scores = dot_nt(k_ref[keys, :], q_head)
            last = jnp.where(seen, scores[reach - block :], MASKED)
            scores = last if at == 0 else jnp.concatenate([scores[: reach - block], last], 0)
            probs = jnp.exp(scores - logs)
            along = dot_nt(v_ref[keys, :], up_head)
            inner = jnp.sum(probs * along, axis=0, keepdims=True)
            low_grad = (probs * (along - inner)).astype(BF16)
            dv = dot_nn(probs.astype(BF16), up_head)
            dk = dot_nn(low_grad, q_head)
            if at == count - 1 and head == 0:
                dv_acc[keys, :] = dv
                dk_acc[keys, :] = dk
            else:
                dv_acc[keys, :] += dv
                dk_acc[keys, :] += dk
            k_head = jnp.where(full_lane[:reach] == head, k_ref[keys, :], jnp.zeros((reach, 128), BF16))
            part = dot_tn(low_grad, k_head)
            dq = part if dq is None else dq + part
        low_dq = (dq * HD ** (-0.5)).astype(BF16)
        grad_ref[0, rows, :] = low_dq
        dq_sum = dq_sum + column_sum(low_dq.astype(F32))
    grad_ref[1] = dk_acc[...].astype(BF16)
    low_dv = dv_acc[...].astype(BF16)
    grad_ref[2] = low_dv
    sum_ref[...] = jnp.zeros_like(sum_ref)
    sum_ref[0:1, :] = dq_sum
    sum_ref[1:2, :] = column_sum(low_dv.astype(F32))


def attend_backward(flags, queries, key_rows, value_rows, upstream, log_sums, first, pairs):
    length = queries.shape[0]
    tile = pl.BlockSpec((length, 128), lambda h, f: (0, h + first))
    return pl.pallas_call(
        functools.partial(attend_backward_kernel, block=length // 4),
        grid_spec=pltpu.PrefetchScalarGridSpec(
            num_scalar_prefetch=1, grid=(pairs,),
            in_specs=[tile, tile, tile, tile,
                      pl.BlockSpec((1, 8, length), lambda h, f: (h + first, 0, 0))],
            out_specs=[pl.BlockSpec((3, length, 128), lambda h, f: (0, 0, h)),
                       pl.BlockSpec((8, 128), lambda h, f: (0, h))],
            scratch_shapes=[pltpu.VMEM((length, 128), F32), pltpu.VMEM((length, 128), F32)]),
        out_shape=[jax.ShapeDtypeStruct((3, length, pairs * 128), BF16),
                   jax.ShapeDtypeStruct((8, pairs * 128), F32)],
        compiler_params=pltpu.CompilerParams(vmem_limit_bytes=9 * MIB),
        cost_estimate=cost(1 + 6 * pairs),
        name="attend_backward",
    )(flags, queries, key_rows, value_rows, upstream, log_sums)


def unpack_kernel(place_ref, rows_ref, *refs):
    own_ref, send_ref = refs[-2:]
    packed = rows_ref[...]
    packed = packed.reshape(packed.shape[0] * 2, packed.shape[2])
    shape = (packed.shape[0], D)
    row = lax.broadcasted_iota(jnp.int32, shape, 0)
    column = lax.broadcasted_iota(jnp.int32, shape, 1)
    pick = lambda seq: dot_tn(packed, jnp.where(row == 2 * column + seq, 1.0, 0.0).astype(BF16)).astype(BF16)
    count = own_ref.shape[0]
    send_ref[pl.ds(0, count), :] = pick(1 - place_ref[0])
    if len(refs) > 2:
        send_ref[pl.ds(count, refs[0].shape[0]), :] = refs[0][...]
    own_ref[...] = pick(place_ref[0])


def unpack_rows(place, rows, *extra):
    packed = rows.transpose(2, 0, 1)
    count = rows.shape[1]
    counts = [count, count + sum(value.shape[0] for value in extra)]
    fixed = lambda value: pl.BlockSpec(value.shape, lambda i, s: (0,) * len(value.shape))
    return pl.pallas_call(
        unpack_kernel,
        grid_spec=pltpu.PrefetchScalarGridSpec(
            num_scalar_prefetch=1, grid=(1,),
            in_specs=[fixed(packed)] + [fixed(value) for value in extra],
            out_specs=[pl.BlockSpec((n, D), lambda i, s: (0, 0)) for n in counts]),
        out_shape=[jax.ShapeDtypeStruct((n, D), BF16) for n in counts],
        compiler_params=pltpu.CompilerParams(vmem_limit_bytes=6 * MIB),
        cost_estimate=cost(5),
        name="unpack_rows",
    )(place, packed, *extra)


def decompress(compact):
    total = jnp.sum(compact, axis=-1, keepdims=True)
    return jnp.where(lane_of(compact.shape) == D - 1, -total, compact)


def crms_back(normal, factor, gain, grad):
    scaled = gain * grad
    du = factor * (scaled - normal * jnp.mean(scaled * normal, axis=-1, keepdims=True))
    lane = lane_of(du.shape)
    last = jnp.sum(jnp.where(lane == D - 1, du, 0.0), axis=-1, keepdims=True)
    return jnp.where(lane == D - 1, 0.0, du - last)


def crms_normal(compact):
    full = decompress(compact)
    factor = lax.rsqrt(jnp.mean(full * full, axis=-1, keepdims=True) + EPSILON)
    return full * factor, factor


def project_kernel(place_ref, own_ref, other_ref, gain_ref, bias_ref, w_own, w_quarter,
                   normed_ref, q_ref, k_ref, v_ref, weight, sems, *, steps):
    at = pl.program_id(0)
    quarter = D // 4
    half = w_own.shape[2]

    def copies():
        out = [pltpu.make_async_copy(w_own, weight.at[:, :, pl.ds(0, half)], sems.at[0])]
        for rel in range(4):
            place = pl.multiple_of((place_ref[1] ^ rel) * quarter, quarter)
            out.append(pltpu.make_async_copy(
                w_quarter[rel], weight.at[:, pl.ds(place, quarter), pl.ds(half, half)],
                sems.at[rel + 1]))
        return out

    @pl.when(at == 0)
    def _():
        for copy in copies():
            copy.start()

    compact = jnp.where(at < steps // 2, own_ref[...], other_ref[...]).astype(F32)
    normal, _ = crms_normal(compact)
    normed = (normal * gain_ref[...]).astype(BF16)
    normed_ref[...] = normed

    @pl.when(at == 0)
    def _():
        for copy in copies():
            copy.wait()

    q_ref[...] = ((dot_nn(normed, weight[0]) + bias_ref[0:1, :]).astype(BF16).astype(F32)
                  * HD ** (-0.5)).astype(BF16)
    k_ref[...] = dot_nn(normed, weight[1]).astype(BF16)
    v_ref[...] = (dot_nn(normed, weight[2]) + bias_ref[1:2, :]).astype(BF16)


def row_maps(steps):
    half = steps // 2
    own = lambda i, s: (jnp.minimum(i, half - 1), 0)
    other = lambda i, s: (jnp.maximum(i - half, 0), 0)
    whole = lambda i, s: (jnp.where(i < half, s[0] * half + i, (1 - s[0]) * half + i - half), 0)
    return own, other, whole


ANY = pl.BlockSpec(memory_space=pl.ANY)


def project(place, own, other, gain, bias, w_own, w_quarter, steps=4):
    length = own.shape[0] * 2
    block = length // steps
    own_map, other_map, whole_map = row_maps(steps)
    fixed = lambda i, s: (0, 0)
    wide = pl.BlockSpec((block, D), whole_map)
    out = jax.ShapeDtypeStruct((length, D), BF16)

    def body(place_ref, own_ref, other_ref, gain_ref, bias_ref, w_own, a, b, c, d, *rest):
        project_kernel(place_ref, own_ref, other_ref, gain_ref, bias_ref, w_own, (a, b, c, d),
                       *rest, steps=steps)

    return pl.pallas_call(
        body,
        grid_spec=pltpu.PrefetchScalarGridSpec(
            num_scalar_prefetch=1, grid=(steps,),
            in_specs=[pl.BlockSpec((block, D), own_map), pl.BlockSpec((block, D), other_map),
                      pl.BlockSpec((1, D), fixed), pl.BlockSpec((2, D), fixed)] + [ANY] * 5,
            out_specs=[wide] * 4,
            scratch_shapes=[pltpu.VMEM((3, D, D), BF16), pltpu.SemaphoreType.DMA((5,))]),
        out_shape=[out] * 4,
        compiler_params=pltpu.CompilerParams(vmem_limit_bytes=11 * MIB),
        cost_estimate=cost(10),
        name="norm_project",
    )(place, own, other, gain, bias, w_own, *w_quarter)


SQRT_2_PI = 0.7978845608028654


def gelu_pair(v):
    square = v * v
    inner = v * (SQRT_2_PI + (SQRT_2_PI * 0.044715) * square)
    tanh = jnp.tanh(inner)
    cdf = 0.5 + 0.5 * tanh
    slope = SQRT_2_PI + (3 * SQRT_2_PI * 0.044715) * square
    back = cdf + (0.5 * v) * (1.0 - tanh * tanh) * slope
    return v * cdf, back


def middle_kernel(place_ref, att_ref, res_own, res_other, cot_own, cot_other, gain_ref, end_ref,
                  fcb_ref, weights, two_ref, active_ref, hidden_ref, own_out, send_first, send_second,
                  mid_ref, branch_ref, upgrad_ref, sums_ref, own_sums, other_sums,
                  out_w, fc_w, proj_w, sems, *, steps, chunk):
    at = pl.program_id(0)
    hid = fc_w.shape[1]
    half = hid // 2
    o_own, f_own, p_own, quarters, proj_quarters = weights

    def copies(which):
        if which == 0:
            own, target = o_own, out_w.at[pl.ds(0, D // 2), :]
        elif which == 1:
            own, target = f_own, fc_w.at[:, pl.ds(0, half)]
        else:
            own, target = p_own, proj_w.at[pl.ds(0, half), :]
        out = [pltpu.make_async_copy(own, target, sems.at[which, 0])]
        for rel in range(4):
            source = proj_quarters[rel] if which == 2 else quarters[rel]
            to = place_ref[2 if which == 2 else 1] ^ rel
            if which == 0:
                moves = [(0, D // 8, out_w, D // 2 + to * (D // 8), None)]
            elif which == 1:
                moves = [(D // 8 + n * (D // 4), D // 4, fc_w, to * (D // 4), half + n * D)
                         for n in range(half // D)]
            else:
                moves = [(0, half // 4, proj_w, half + to * (half // 4), None)]
            for n, (start, rows, into, row, col) in enumerate(moves):
                spot = pl.ds(pl.multiple_of(row, rows), rows)
                out.append(pltpu.make_async_copy(
                    source.at[pl.ds(start, rows), :],
                    into.at[spot, :] if col is None else into.at[spot, pl.ds(col, D)],
                    sems.at[which, 1 + 2 * rel + n]))
        return out

    @pl.when(at == 0)
    def _():
        for which in range(3):
            for copy in copies(which):
                copy.start()
        for ref in (sums_ref, own_sums, other_sums):
            ref[...] = jnp.zeros_like(ref)
        for copy in copies(0):
            copy.wait()

    mine = at < steps // 2
    compact = jnp.where(mine, res_own[...], res_other[...]).astype(F32)
    cot_low = jnp.where(mine, cot_own[...], cot_other[...])
    middle = compact + dot_nn(att_ref[...], out_w[...]) + end_ref[0:1, :]
    normal, factor = crms_normal(middle)
    gain = gain_ref[...]
    two = (normal * gain).astype(BF16)
    two_ref[...] = two

    @pl.when(at == 0)
    def _():
        for which in (1, 2):
            for copy in copies(which):
                copy.wait()

    mlp = jnp.zeros((two.shape[0], D), F32)
    two_grad = jnp.zeros((two.shape[0], D), F32)
    for start in range(0, hid, chunk):
        cols = pl.ds(start, chunk)
        pre = dot_nn(two, fc_w[:, cols]) + fcb_ref[0:1, cols]
        act, slope = gelu_pair(pre)
        act = act.astype(BF16)
        active_ref[:, cols] = act
        mlp = mlp + dot_nn(act, proj_w[cols, :])
        hidden = (dot_nt(cot_low, proj_w[cols, :]) * slope).astype(BF16)
        hidden_ref[:, cols] = hidden
        to = own_sums if start < half else other_sums
        to[0:1, pl.ds(start % half, chunk)] += column_sum(hidden.astype(F32))
        two_grad = two_grad + dot_nt(hidden, fc_w[:, cols])
    block_out = (middle + mlp + end_ref[1:2, :]).astype(BF16)

    @pl.when(mine)
    def _():
        own_out[...] = block_out

    @pl.when(at == steps // 2)
    def _():
        send_first[...] = block_out

    @pl.when(at == steps // 2 + 1)
    def _():
        send_second[...] = block_out

    cot = cot_low.astype(F32)
    mid_grad = cot + crms_back(normal, factor, gain, two_grad)
    mid_ref[...] = mid_grad
    branch = mid_grad.astype(BF16)
    branch_ref[...] = branch
    upgrad_ref[...] = dot_nt(branch, out_w[...]).astype(BF16)
    sums_ref[0:1, :] += column_sum(two_grad * normal)
    sums_ref[1:2, :] += column_sum(branch.astype(F32))
    sums_ref[2:3, :] += column_sum(cot)


def middle_stage(place, att, res_own, res_other, cot_own, cot_other, gain, end_bias, fc_bias, weights,
                 steps=4, chunk=768):
    length = att.shape[0]
    hid = fc_bias.shape[1]
    block = length // steps
    own_map, other_map, whole_map = row_maps(steps)
    fixed = lambda i, s: (0, 0)
    flat = [*weights[:3], *weights[3], *weights[4]]
    spec = lambda w, m: pl.BlockSpec((block, w), m)

    def body(place_ref, *refs):
        ins, rest = refs[:8], refs[8:]
        w, rest = rest[:11], rest[11:]
        packed = (*w[:3], w[3:7], w[7:])
        middle_kernel(place_ref, *ins, packed, *rest, steps=steps, chunk=chunk)

    sd = jax.ShapeDtypeStruct
    return pl.pallas_call(
        body,
        grid_spec=pltpu.PrefetchScalarGridSpec(
            num_scalar_prefetch=1, grid=(steps,),
            in_specs=[spec(D, whole_map), spec(D, own_map), spec(D, other_map), spec(D, own_map),
                      spec(D, other_map), pl.BlockSpec((1, D), fixed), pl.BlockSpec((2, D), fixed),
                      pl.BlockSpec((1, hid), fixed)] + [ANY] * 11,
            out_specs=[spec(D, whole_map), spec(hid, whole_map), spec(hid, whole_map),
                       spec(D, own_map), spec(D, fixed), spec(D, fixed),
                       spec(D, whole_map), spec(D, whole_map), spec(D, whole_map),
                       pl.BlockSpec((8, D), fixed), pl.BlockSpec((8, hid // 2), fixed),
                       pl.BlockSpec((8, hid // 2), fixed)],
            scratch_shapes=[pltpu.VMEM((D, D), BF16), pltpu.VMEM((D, hid), BF16),
                            pltpu.VMEM((hid, D), BF16), pltpu.SemaphoreType.DMA((3, 9))]),
        out_shape=[sd((length, D), BF16), sd((length, hid), BF16), sd((length, hid), BF16),
                   sd((length // 2, D), BF16), sd((block, D), BF16), sd((block, D), BF16),
                   sd((length, D), F32), sd((length, D), BF16), sd((length, D), BF16),
                   sd((8, D), F32), sd((8, hid // 2), F32), sd((8, hid // 2), F32)],
        compiler_params=pltpu.CompilerParams(vmem_limit_bytes=36 * MIB),
        cost_estimate=cost(38),
        name="middle_stage",
    )(place, att, res_own, res_other, cot_own, cot_other, gain, end_bias, fc_bias, *flat)


def fc_grad_kernel(place_ref, left_ref, right_ref, keep_ref, send_ref, *, rows):
    flip = (place_ref[1] & 1) == 1
    both = dot_tn_halves(left_ref, right_ref).astype(BF16)
    for pair in range(2):
        to = pair ^ (place_ref[1] >> 1)
        low, high = both[2 * pair * rows : (2 * pair + 1) * rows], both[(2 * pair + 1) * rows : (2 * pair + 2) * rows]
        keep_ref[0, to] = jnp.where(flip, high, low)
        send_ref[0, to] = jnp.where(flip, low, high)


def fc_grad(place, left, right, chunk=768):
    length, width = left.shape
    rows = width // 4
    half = right.shape[1] // 2
    parts = half // chunk
    out = jax.ShapeDtypeStruct((2, 2, rows, half), BF16)
    out_spec = pl.BlockSpec((1, 2, rows, chunk), lambda n, s: (n // parts, 0, 0, n % parts))
    return pl.pallas_call(
        functools.partial(fc_grad_kernel, rows=rows),
        grid_spec=pltpu.PrefetchScalarGridSpec(
            num_scalar_prefetch=1, grid=(2 * parts,),
            in_specs=[pl.BlockSpec((length, width), lambda n, s: (0, 0)),
                      pl.BlockSpec((length, chunk), lambda n, s: (0, n))],
            out_specs=[out_spec, out_spec]),
        out_shape=[out, out],
        compiler_params=pltpu.CompilerParams(vmem_limit_bytes=12 * MIB),
        cost_estimate=cost(12),
        name="fc_grad",
    )(place, left, right)


def qkv_grad_kernel(place_ref, left_ref, *refs, rows, parts, pieces):
    right_refs, weight_refs = refs[:parts], refs[parts : parts + pieces]
    keep_ref, send_ref, sum_ref, total = refs[parts + pieces :]
    flip = (place_ref[1] & 1) == 1
    half = left_ref.shape[0] // 2
    width = sum(ref.shape[2] for ref in right_refs)
    both = None
    for n in range(2):
        part = pl.ds(n * half, half)
        right = jnp.concatenate([ref[c, part, :] for c in range(3) for ref in right_refs], axis=1)
        here = dot_tn(left_ref[part, :], right)
        both = here if both is None else both + here
    low_both = both.astype(BF16)
    for pair in range(2):
        to = pair ^ (place_ref[1] >> 1)
        for c in range(3):
            cols = slice(c * width, (c + 1) * width)
            low = low_both[2 * pair * rows : (2 * pair + 1) * rows, cols]
            high = low_both[(2 * pair + 1) * rows : (2 * pair + 2) * rows, cols]
            keep_ref[to, c] = jnp.where(flip, high, low)
            send_ref[to, c] = jnp.where(flip, low, high)
    sum_ref[...] = jnp.zeros_like(sum_ref)
    if pieces > 1:
        total[...] = both
    span = both.shape[0] // pieces
    for n in range(pieces):
        at = pl.multiple_of((place_ref[1] ^ n) * span, span) if pieces > 1 else 0
        folded = jnp.zeros((span, 128), F32)
        for c in range(3):
            here = total[pl.ds(at, span), pl.ds(c * width, width)] if pieces > 1 else both[:, c * width : (c + 1) * width]
            product = here * weight_refs[n][c].astype(F32)
            for k in range(0, width, 128):
                folded = folded + product[:, k : k + 128]
        total[pl.ds(at, span), pl.ds(0, 128)] = folded
    sum_ref[0:1, :] = column_sum(jnp.transpose(total[:, 0:128]))


def qkv_grad(place, left, rights, weights, col_at=0):
    length, width = left.shape
    rows = width // 4
    cols = sum(value.shape[2] for value in rights)
    out = jax.ShapeDtypeStruct((2, 3, rows, cols), BF16)
    whole = lambda value: pl.BlockSpec(value.shape, lambda i, s: (0,) * len(value.shape))
    sums = jax.ShapeDtypeStruct((8, width), F32)
    return pl.pallas_call(
        functools.partial(qkv_grad_kernel, rows=rows, parts=len(rights), pieces=len(weights)),
        grid_spec=pltpu.PrefetchScalarGridSpec(
            num_scalar_prefetch=1, grid=(1,),
            in_specs=[whole(value) for value in (left, *rights)]
            + [pl.BlockSpec((3, value.shape[1], cols), lambda i, s: (0, 0, col_at)) for value in weights],
            out_specs=[whole(out), whole(out), whole(sums)],
            scratch_shapes=[pltpu.VMEM((width, 3 * cols), F32)]),
        out_shape=[out, out, sums],
        compiler_params=pltpu.CompilerParams(vmem_limit_bytes=17 * MIB),
        cost_estimate=cost(6.5),
        name="qkv_grad",
    )(place, left, *rights, *weights)


def proj_grad_kernel(place_ref, own_act, other_act, own_cot, other_cot, att_ref, branch_ref, keep_ref, send_ref, rest,
                     *, rows):
    side, pair = pl.program_id(0), pl.program_id(1)
    flip = (place_ref[1] & 1) == 1
    out_rows = att_ref.shape[1] // 8

    @pl.when((side == 0) & (pair == 0))
    def _():
        rest[...] = dot_tn_halves(att_ref, branch_ref).astype(BF16)

    both = (dot_tn(own_act[...], own_cot[...]) + dot_tn(other_act[...], other_cot[...])).astype(BF16)
    base = pl.multiple_of((side * 4 + pair * 2) * out_rows, out_rows)
    more_low, more_high = rest[pl.ds(base, out_rows), :], rest[pl.ds(base + out_rows, out_rows), :]
    low, high = both[:rows], both[rows:]
    keep_ref[0, 0, pl.ds(0, rows), :] = jnp.where(flip, high, low)
    send_ref[0, 0, pl.ds(0, rows), :] = jnp.where(flip, low, high)
    keep_ref[0, 0, pl.ds(rows, out_rows), :] = jnp.where(flip, more_high, more_low)
    send_ref[0, 0, pl.ds(rows, out_rows), :] = jnp.where(flip, more_low, more_high)


def proj_grad(place, active, cot_own, cot_other, attended, branch):
    length, width = active.shape
    rows = width // 8
    out_rows = attended.shape[1] // 8
    out = jax.ShapeDtypeStruct((2, 2, rows + out_rows, D), BF16)
    out_spec = pl.BlockSpec((1, 1, rows + out_rows, D), lambda n, j, s: (j ^ (s[1] >> 1), n, 0, 0))
    fixed = lambda count: pl.BlockSpec((count, D), lambda n, j, s: (0, 0))
    return pl.pallas_call(
        functools.partial(proj_grad_kernel, rows=rows),
        grid_spec=pltpu.PrefetchScalarGridSpec(
            num_scalar_prefetch=1, grid=(2, 2),
            in_specs=[pl.BlockSpec((length // 2, 2 * rows), lambda n, j, s: (s[0], n * 2 + j)),
                      pl.BlockSpec((length // 2, 2 * rows), lambda n, j, s: (1 - s[0], n * 2 + j)),
                      fixed(length // 2), fixed(length // 2), fixed(length), fixed(length)],
            out_specs=[out_spec, out_spec],
            scratch_shapes=[pltpu.VMEM((attended.shape[1], D), BF16)]),
        out_shape=[out, out],
        compiler_params=pltpu.CompilerParams(vmem_limit_bytes=19 * MIB),
        cost_estimate=cost(13),
        name="proj_grad",
    )(place, active, active, cot_own, cot_other, attended, branch)


def input_grad_kernel(place_ref, own_grads, other_grads, res_own, res_other, mid_ref, gain_ref, w_own, w_quarter,
                      own_out, send_out, weight, sems, *, steps):
    at = pl.program_id(0)
    quarter = D // 4
    half = w_own.shape[2]

    def copies():
        out = []
        for c in range(3):
            out.append(pltpu.make_async_copy(
                w_own.at[c], weight.at[:, pl.ds(c * half, half)], sems.at[c, 0]))
            for rel in range(4):
                place = pl.multiple_of((place_ref[1] ^ rel) * quarter, quarter)
                out.append(pltpu.make_async_copy(
                    w_quarter[rel].at[c], weight.at[pl.ds(place, quarter), pl.ds((3 + c) * half, half)],
                    sems.at[c, rel + 1]))
        return out

    @pl.when(at == 0)
    def _():
        for copy in copies():
            copy.start()

    mine = at < steps // 2
    compact = jnp.where(mine, res_own[...], res_other[...]).astype(F32)
    normal, factor = crms_normal(compact)

    @pl.when(at == 0)
    def _():
        for copy in copies():
            copy.wait()

    left = jnp.concatenate([ref[c] for part in (own_grads, other_grads) for c in range(3) for ref in part], axis=1)
    grad = dot_nt(left, weight[...])
    result = (mid_ref[...] + crms_back(normal, factor, gain_ref[...], grad)).astype(BF16)

    @pl.when(mine)
    def _():
        own_out[...] = result

    @pl.when(jnp.logical_not(mine))
    def _():
        send_out[...] = result


def input_grad(place, own_grads, other_grads, res_own, res_other, mid, gain, w_own, w_quarter, steps=4):
    length = mid.shape[0]
    block = length // steps
    own_map, other_map, whole_map = row_maps(steps)
    fixed = lambda i, s: (0, 0)
    mine, many = len(own_grads), len(own_grads) + len(other_grads)
    grad_spec = lambda value: pl.BlockSpec((3, block, value.shape[2]), lambda i, s: (0, whole_map(i, s)[0], 0))

    def body(place_ref, *refs):
        rest = refs[many:]
        input_grad_kernel(place_ref, refs[:mine], refs[mine:many], *rest[:5], rest[5:9], *rest[9:], steps=steps)

    sd = jax.ShapeDtypeStruct
    return pl.pallas_call(
        body,
        grid_spec=pltpu.PrefetchScalarGridSpec(
            num_scalar_prefetch=1, grid=(steps,),
            in_specs=[grad_spec(value) for value in (*own_grads, *other_grads)] + [pl.BlockSpec((block, D), own_map), pl.BlockSpec((block, D), other_map),
                      pl.BlockSpec((block, D), whole_map), pl.BlockSpec((1, D), fixed)] + [ANY] * 5,
            out_specs=[pl.BlockSpec((block, D), own_map), pl.BlockSpec((block, D), other_map)],
            scratch_shapes=[pltpu.VMEM((D, 3 * D), BF16), pltpu.SemaphoreType.DMA((3, 5))]),
        out_shape=[sd((length // 2, D), BF16), sd((length // 2, D), BF16)],
        compiler_params=pltpu.CompilerParams(vmem_limit_bytes=14 * MIB),
        cost_estimate=cost(9),
        name="input_grad",
    )(place, *own_grads, *other_grads, res_own, res_other, mid, gain, w_own, *w_quarter)


def pack_kernel(place_ref, own_ref, first_ref, second_ref, out_ref, *, steps):
    straight = place_ref[0] == 0
    own = jnp.transpose(own_ref[...].astype(F32))
    other = jnp.where(pl.program_id(0) < steps // 2, first_ref[...], second_ref[...])
    other = jnp.transpose(other.astype(F32))
    count = out_ref.shape[0]
    both = [jnp.where(straight, own, other)[:count], jnp.where(straight, other, own)[:count]]
    out_ref[...] = jnp.stack(both, 1).astype(BF16)


def pack_rows(place, own, first, second):
    positions = own.shape[0]
    steps = positions // 128
    own_map, other_map, _ = row_maps(steps)
    if second.shape[0] == positions:
        other_map = lambda i, s: (jnp.maximum(i, steps // 2), 0)
    packed = pl.pallas_call(
        functools.partial(pack_kernel, steps=steps),
        grid_spec=pltpu.PrefetchScalarGridSpec(
            num_scalar_prefetch=1, grid=(steps,),
            in_specs=[pl.BlockSpec((128, D), lambda i, s: (i, 0)), pl.BlockSpec((128, D), own_map),
                      pl.BlockSpec((128, D), other_map)],
            out_specs=pl.BlockSpec((D - 1, 2, 128), lambda i, s: (0, 0, i))),
        out_shape=jax.ShapeDtypeStruct((D - 1, 2, positions), BF16),
        compiler_params=pltpu.CompilerParams(vmem_limit_bytes=4 * MIB),
        cost_estimate=cost(0.1),
        name="pack_rows",
    )(place, own, first, second)
    return packed.transpose(1, 2, 0)


def swap(value, axis, bit, size):
    return lax.ppermute(value, axis, [(n, n ^ bit) for n in range(size)])


def meet(*values):
    return lax.optimization_barrier(values)


def add_low(*values):
    total = values[0].astype(F32)
    for value in values[1:]:
        total = total + value.astype(F32)
    return total.astype(BF16)


def chain_in(value):
    return lax.ppermute(value, "group", [(0, 1), (3, 2)])


def chain_across(value):
    return lax.ppermute(value, "group", [(1, 2), (2, 1)])


def chain_out(value):
    return lax.ppermute(value, "group", [(1, 0), (2, 3)])


def on_device(sizes, residual_in, piece_ids, norm_gains, qkv_weight, qv_bias, out_weight, fc_weight,
              fc_bias, proj_weight, out_biases, cotangent):
    n_dp, n_group, n_tensor = sizes["dp"], sizes["group"], sizes["tensor"]
    dp_at = lax.axis_index("dp")
    group_at = lax.axis_index("group")
    tensor_at = lax.axis_index("tensor")
    quarter_at = dp_at & 3
    proj_at = (dp_at & 1) | ((group_at & 1) << 1)
    place = jnp.stack([tensor_at, quarter_at, proj_at]).astype(jnp.int32)
    pad = ((0, 0), (0, 1))
    half = qv_bias.shape[1]
    hid = fc_bias.shape[0]
    pairs = half // 128
    y_swap = lambda value: swap(value, "tensor", 1, n_tensor)
    x_swap = lambda value: swap(value, "dp", 2, n_dp)
    c_swap = lambda value: swap(value, "dp", 1, n_dp)
    z_swap = lambda value: swap(value, "group", 1, n_group)

    def piece_of(shard, dim, at):
        rows = shard.shape[dim] // 4
        return lax.dynamic_slice_in_dim(shard, at * rows, rows, dim)

    qkv_piece = piece_of(qkv_weight, 1, quarter_at)
    qkv_y = y_swap(qkv_piece)
    bias_rows = jnp.concatenate([fc_bias.reshape(-1, D), qv_bias.reshape(1, D), jnp.zeros((13, D), BF16)], 0)
    res_own, res_send = unpack_rows(after(place, qkv_piece), residual_in, bias_rows)
    res_other = y_swap(res_send)
    qkv_y, res_own, out_gated, fc_gated, proj_gated = meet(qkv_y, res_own, out_weight, fc_weight, proj_weight)
    qkv_x = x_swap(qkv_y)
    qkv_c = c_swap(qkv_y)
    fc_piece = piece_of(fc_gated, 0, quarter_at)
    mix = jnp.concatenate([jnp.pad(piece_of(out_gated, 0, quarter_at), pad)]
                          + [fc_piece[:, n : n + D] for n in range(0, hid, D)], 0)
    proj_piece = jnp.pad(piece_of(proj_gated, 0, proj_at), pad)
    qkv_c, mix, proj_piece = meet(qkv_c, mix, proj_piece)
    mix_y, proj_y = y_swap(mix), y_swap(proj_piece)
    cot_own, cot_send = unpack_rows(after(place, mix, proj_piece), cotangent)
    out_own = jnp.pad(out_gated, pad)
    proj_own = jnp.pad(proj_gated, pad)
    qkv_x, res_other, out_own, proj_own, cot_send = meet(qkv_x, res_other, out_own, proj_own, cot_send)
    qkv_cx = c_swap(qkv_x)
    qkv_others = (qkv_y, qkv_c, qkv_x, qkv_cx)

    gains = norm_gains.astype(F32)
    end_biases = jnp.pad(out_biases, pad).astype(F32)
    count = residual_in.shape[1]
    bias_other = res_other[count : count + 8].astype(F32)
    fc_rows = hid // D
    qv_full = jnp.concatenate([qv_bias.astype(F32), bias_other[fc_rows].reshape(2, half)], axis=1)
    fc_full = jnp.concatenate([fc_bias.astype(F32).reshape(1, -1), bias_other[:fc_rows].reshape(1, -1)], axis=1)
    length = piece_ids.shape[1]
    flags = (lax.dynamic_index_in_dim(piece_ids, tensor_at, 0, keepdims=False)[:: length // 4] >= 0)
    flags = flags.astype(jnp.int32)

    normed_one, queries, key_rows, value_rows = project(
        place, res_own, res_other, gains[0:1], qv_full, qkv_weight, qkv_others)
    queries, cot_send = meet(queries, cot_send)
    cot_other = y_swap(cot_send)
    attended = attend_forward(flags, queries, key_rows, value_rows, 0, pairs)
    *attended, queries, mix_y, proj_y = meet(*attended, queries, mix_y, proj_y)
    mix_x, mix_c = x_swap(mix_y), c_swap(mix_y)
    proj_x, proj_c = z_swap(proj_y), c_swap(proj_y)
    attended = attend_forward(flags, queries, key_rows, value_rows, pairs, pairs, attended)
    attended, log_sums, mix_x, proj_x, cot_other = meet(*attended, mix_x, proj_x, cot_other)
    mix_others = (mix_y, mix_c, mix_x, c_swap(mix_x))
    proj_others = (proj_y, proj_c, proj_x, c_swap(proj_x))

    (normed_two, active, hidden_grad, out_mine, *out_send, middle_grad, branch_grad, attended_grad,
     middle_sums, own_sums, other_sums) = middle_stage(
        place, attended, res_own, res_other, cot_own, cot_other, gains[1:2], end_biases, fc_full,
        (out_own, fc_weight, proj_own, mix_others, proj_others))
    backward = functools.partial(attend_backward, flags, queries, key_rows, value_rows)
    restore = functools.partial(pack_rows, place)

    def small_outputs(small):
        part, first = hid // n_dp, half // n_dp
        return (jnp.concatenate([small[0:1, :D], small[0:1, D : 2 * D]], 0),
                lax.dynamic_slice(small, (0, 2 * D + hid + dp_at * first), (2, first)),
                lax.dynamic_slice(small, (0, 2 * D + dp_at * part), (1, part)).reshape(part),
                small[1:3, D : 2 * D - 1])

    if n_dp == 4 and n_group == 4:
        out_got = [y_swap(value) for value in out_send]
        proj_k, proj_s = proj_grad(after(place, middle_sums), active, cot_own, cot_other, attended, branch_grad)
        proj_k, proj_s, out_got[0] = meet(proj_k, proj_s, out_got[0])
        proj_c = c_swap(proj_s)
        fc_k, fc_s = fc_grad(after(place, proj_k), normed_two, hidden_grad)
        fc_k, fc_s, proj_k, proj_c, *out_got = meet(fc_k, fc_s, proj_k, proj_c, *out_got)
        fc_c = c_swap(fc_s)
        proj_fo = add_low(proj_k[1, 1], proj_c[1, 1])
        proj_xo = x_swap(proj_fo)
        proj_fm = add_low(proj_k[1, 0], after(proj_c, proj_fo)[1, 0])
        proj_xm = x_swap(proj_fm)
        fc_k, fc_c, proj_fo, proj_fm = meet(fc_k, fc_c, proj_fo, proj_fm)
        fc_away = add_low(fc_k[1], fc_c[1])
        fc_y = y_swap(fc_away)
        first, first_sums = backward(after(attended_grad, fc_away), log_sums, pairs, pairs)
        first, first_sums, proj_k, proj_c, proj_xo = meet(first, first_sums, proj_k, proj_c, proj_xo)
        proj_r = add_low(proj_k[0, 1], proj_c[0, 1], proj_xo)
        proj_y = y_swap(proj_r)
        qo_k, qo_s, qo_sum = qkv_grad(after(place, proj_r), normed_one, [first], qkv_others)
        qo_k, qo_s, fc_k, fc_c, fc_y = meet(qo_k, qo_s, fc_k, fc_c, fc_y)
        qo_c = c_swap(qo_s)
        fc_far = add_low(fc_k[0, 1], fc_c[0, 1], fc_y[1])
        fc_x = x_swap(fc_far)
        own_a, sums_a = backward(after(attended_grad, fc_far), log_sums, 0, pairs - 1)
        own_a, sums_a, proj_y, proj_xm, proj_k, proj_c = meet(own_a, sums_a, proj_y, proj_xm, proj_k, proj_c)
        proj_shard = add_low(proj_k[0, 0], proj_c[0, 0], proj_xm, proj_y)
        proj_z = chain_in(proj_shard)
        proj_shard, fc_x, qo_k, qo_c = meet(proj_shard, fc_x, qo_k, qo_c)
        fc_shard = add_low(fc_k[0, 0], fc_c[0, 0], fc_y[0], fc_x)
        fc_z = chain_in(fc_shard)
        qo_f = add_low(qo_k[1], qo_c[1])
        qo_x = x_swap(qo_f)
        own_b, sums_b = backward(after(attended_grad, qo_f, proj_shard, fc_shard), log_sums, pairs - 1, 1)
        qm_k, qm_s, qm_sum = qkv_grad(after(place, own_b), normed_one, [own_a, own_b], [qkv_weight])
        qm_k, qm_s, qm_sum, qo_k, qo_c, qo_x = meet(qm_k, qm_s, qm_sum, qo_k, qo_c, qo_x)
        qm_c = c_swap(qm_s)
        in_sums = (qm_sum + qo_sum) / gains[0:1]
        small = jnp.concatenate(
            [value[:4] for value in (in_sums, middle_sums, own_sums, other_sums, sums_a, sums_b, first_sums)], 1)
        small_c = c_swap(small)
        qo_r = add_low(qo_k[0], qo_c[0], qo_x)
        qo_y = y_swap(qo_r)
        qm_k, qm_c, qo_r, small, small_c = meet(qm_k, qm_c, qo_r, small, small_c)
        small = small + small_c
        small_x = x_swap(small)
        qm_f = add_low(after(qm_k, small)[1], qm_c[1])
        qm_x = x_swap(qm_f)
        qm_f, proj_shard, proj_z = meet(qm_f, proj_shard, proj_z)
        proj_shard = add_low(proj_shard, proj_z)
        proj_z = chain_across(proj_shard)
        block_out = restore(after(out_mine, proj_shard), *out_got)
        block_out, small, small_x = meet(block_out, small, small_x)
        small = small + small_x
        split = 2 * D + hid
        mine = jnp.concatenate([small[:, :split], small[:, split + hid : split + hid + half]], 1)
        other = jnp.concatenate([small[:, : 2 * D], small[:, split : split + hid], small[:, split + hid + half :]], 1)
        small_y = y_swap(other)
        qm_k, qm_c, qm_x, qo_y, mine, small_y = meet(qm_k, qm_c, qm_x, qo_y, mine, small_y)
        last = add_low(qm_k[0], qm_c[0], qm_x, qo_y)
        last_z = chain_in(last)
        small = mine + small_y
        small_z = chain_in(small)
        fc_shard, fc_z, proj_shard, proj_z, last, small = meet(fc_shard, fc_z, proj_shard, proj_z, last, small)
        fc_shard = add_low(fc_shard, fc_z)
        fc_z = chain_across(fc_shard)
        proj_shard = add_low(proj_shard, proj_z)
        proj_z = chain_out(proj_shard)
        in_mine, in_send = input_grad(
            after(place, last, proj_shard, fc_shard, small), [own_a, own_b], [first], res_own, res_other, middle_grad,
            gains[0:1], qkv_weight, qkv_others)
        in_mine, in_send, last, last_z, fc_shard, fc_z, small, small_z = meet(
            in_mine, in_send, last, last_z, fc_shard, fc_z, small, small_z)
        last = add_low(last, last_z)
        last_z = chain_across(last)
        small = small + small_z
        small_z = chain_across(small)
        fc_shard = add_low(after(fc_shard, last, small), fc_z)
        fc_z = chain_out(fc_shard)
        in_got = y_swap(in_send)
        middle_one = (group_at == 1) | (group_at == 2)
        small, last, fc_shard, proj_shard, proj_z = meet(small, last, fc_shard, proj_shard, proj_z)
        proj_shard = jnp.where(middle_one, proj_shard, proj_z)
        out_shard = proj_shard[hid // 4 :, : D - 1].astype(F32)
        proj_shard = proj_shard[: hid // 4, : D - 1].astype(F32)
        small, small_z, last, last_z, proj_shard, out_shard = meet(
            small, small_z, last, last_z, proj_shard, out_shard)
        last = add_low(last, last_z)
        last_z = chain_out(last)
        small = small + small_z
        small_z = chain_out(small)
        in_mine, in_got, last, small = meet(in_mine, in_got, last, small)
        in_out = restore(in_mine, in_got, in_got)
        in_out, fc_shard, fc_z = meet(in_out, fc_shard, fc_z)
        fc_shard = jnp.where(middle_one, fc_shard, fc_z).astype(F32)
        fc_shard, small, small_z = meet(fc_shard, small, small_z)
        small = small_outputs(jnp.where(middle_one, small, small_z))
        last, last_z, in_out, proj_shard, out_shard, fc_shard, *small = meet(
            last, last_z, in_out, proj_shard, out_shard, fc_shard, *small)
        qkv_shard = jnp.where(middle_one, last, last_z)
    else:
        first, first_sums = backward(attended_grad, log_sums, pairs, pairs)
        own, second_sums = backward(attended_grad, log_sums, 0, pairs)
        in_mine, in_send = input_grad(
            place, [own], [first], res_own, res_other, middle_grad, gains[0:1], qkv_weight, qkv_others)
        in_got = y_swap(in_send)
        in_out = restore(in_mine, in_got, in_got)
        block_out = restore(out_mine, *[y_swap(value) for value in out_send])
        qo_sum = qkv_grad(place, normed_one, [first], qkv_others)[2]
        qm_sum = qkv_grad(place, normed_one, [own], [qkv_weight])[2]

        def scatter(own, other):
            total = [lax.psum_scatter(value.astype(BF16), "dp", scatter_dimension=0, tiled=True)
                     for value in (own, other)]
            return lax.psum(add_low(total[0], y_swap(total[1])), "group")

        cot_rows = jnp.where(tensor_at == 0, jnp.concatenate([cot_own, cot_other]),
                             jnp.concatenate([cot_other, cot_own]))
        proj_shard = scatter(dot_tn(active[:, :hid], cot_rows), dot_tn(active[:, hid:], cot_rows))
        fc_shard = scatter(dot_tn(normed_two, hidden_grad[:, :hid]), dot_tn(normed_two, hidden_grad[:, hid:]))
        out_shard = scatter(dot_tn(attended[:, :half], branch_grad), dot_tn(attended[:, half:], branch_grad))
        proj_shard, out_shard = proj_shard[:, : D - 1].astype(F32), out_shard[:, : D - 1].astype(F32)
        fc_shard = fc_shard.astype(F32)
        qkv_shard = jnp.swapaxes(scatter(
            *[jnp.stack([dot_tn(normed_one, part[c]) for c in range(3)], 1) for part in (own, first)]), 0, 1)
        in_sums = (qm_sum + qo_sum) / gains[0:1]
        small = jnp.concatenate([in_sums, middle_sums, own_sums, second_sums], 1)
        small = small + y_swap(jnp.concatenate([in_sums, middle_sums, other_sums, first_sums], 1))
        small = small_outputs(lax.psum(small, ("dp", "group")))

    grad_gains, grad_qv_bias, grad_fc_bias, grad_out_biases = small
    return (
        block_out,
        in_out,
        grad_gains,
        qkv_shard.astype(F32),
        grad_qv_bias,
        out_shard,
        fc_shard,
        grad_fc_bias,
        proj_shard,
        grad_out_biases,
    )


def solution(mesh):
    sizes = dict(mesh.shape)
    in_specs = (
        P(("dp", "group"), "tensor", None),
        P(("dp", "group"), None),
        P(),
        P(None, None, "tensor"),
        P(None, "tensor"),
        P("tensor", None),
        P(None, "tensor"),
        P("tensor"),
        P("tensor", None),
        P(),
        P(("dp", "group"), "tensor", None),
    )
    out_specs = (
        P(("dp", "group"), "tensor", None),
        P(("dp", "group"), "tensor", None),
        P(),
        P(None, "dp", "tensor"),
        P(None, ("tensor", "dp")),
        P(("tensor", "dp"), None),
        P("dp", "tensor"),
        P(("tensor", "dp")),
        P(("tensor", "dp"), None),
        P(),
    )
    return jax.shard_map(
        functools.partial(on_device, sizes), mesh=mesh, in_specs=in_specs, out_specs=out_specs,
        check_vma=False)
```

```python
import functools
import jax
import jax.numpy as jnp
from jax import lax
from jax.sharding import PartitionSpec as P
from jax.experimental import pallas as pl
from jax.experimental.pallas import tpu as pltpu

D = 768
HD = 64
EPSILON = 1e-05
MASKED = -1e30
MIB = 1024 * 1024
F32 = jnp.float32
BF16 = jnp.bfloat16
COST_FLOPS = 0.4e9


def cost(micros):
    return pl.CostEstimate(flops=int(micros * COST_FLOPS), bytes_accessed=int(micros * 4e5), transcendentals=0)


def after(value, *others):
    return lax.optimization_barrier((value, *others))[0]


def dot_nn(a, b):
    return lax.dot_general(a, b, (((1,), (0,)), ((), ())), preferred_element_type=F32)


def dot_nt(a, b):
    return lax.dot_general(a, b, (((1,), (1,)), ((), ())), preferred_element_type=F32)


def dot_tn(a, b):
    return lax.dot_general(a, b, (((0,), (0,)), ((), ())), preferred_element_type=F32)


def dot_tn_halves(left, right):
    half = left.shape[0] // 2
    return (dot_tn(left[pl.ds(0, half), :], right[pl.ds(0, half), :])
            + dot_tn(left[pl.ds(half, half), :], right[pl.ds(half, half), :]))


def column_sum(values):
    return jnp.sum(values, axis=0, keepdims=True)


def lane_of(shape):
    return lax.broadcasted_iota(jnp.int32, shape, len(shape) - 1)


def attend_forward_kernel(flags_ref, q_ref, k_ref, v_ref, out_ref, log_ref, *, block):
    length = q_ref.shape[0]
    key_at = lax.broadcasted_iota(jnp.int32, (block, block), 0)
    query_at = lax.broadcasted_iota(jnp.int32, (block, block), 1)
    causal = key_at <= query_at
    head_lane = lane_of((block, 128)) // HD
    for at in range(length // block):
        rows = pl.ds(at * block, block)
        reach = (at + 1) * block
        keys = pl.ds(0, reach)
        seen = causal | (flags_ref[at] > 0)
        parts = []
        for head in range(2):
            q_head = jnp.where(head_lane == head, q_ref[rows, :], jnp.zeros((block, 128), BF16))
            scores = dot_nt(k_ref[keys, :], q_head)
            last = jnp.where(seen, scores[reach - block :], MASKED)
            scores = last if at == 0 else jnp.concatenate([scores[: reach - block], last], 0)
            top = jnp.max(scores, axis=0, keepdims=True)
            probs = jnp.exp(scores - top)
            total = jnp.sum(probs, axis=0, keepdims=True)
            log_ref[0, pl.ds(head, 1), rows] = top + jnp.log(total)
            probs = (probs * (1.0 / total)).astype(BF16)
            parts.append(dot_tn(probs, v_ref[keys, :]).astype(BF16))
        out_ref[rows, :] = jnp.where(head_lane == 0, parts[0], parts[1])


def attend_forward(flags, queries, key_rows, value_rows, first, pairs, into=None):
    length, width = queries.shape
    block = length // 4
    tile = pl.BlockSpec((length, 128), lambda h, f: (0, h + first))
    more = [] if into is None else list(into)

    def body(flags_ref, q_ref, k_ref, v_ref, *rest):
        attend_forward_kernel(flags_ref, q_ref, k_ref, v_ref, *rest[len(more):], block=block)

    return pl.pallas_call(
        body,
        grid_spec=pltpu.PrefetchScalarGridSpec(
            num_scalar_prefetch=1, grid=(pairs,),
            in_specs=[tile, tile, tile] + [pl.BlockSpec(memory_space=pl.ANY)] * len(more),
            out_specs=[tile, pl.BlockSpec((1, 8, length), lambda h, f: (h + first, 0, 0))]),
        out_shape=[jax.ShapeDtypeStruct((length, width), BF16),
                   jax.ShapeDtypeStruct((width // 128, 8, length), F32)],
        input_output_aliases={4 + n: n for n in range(len(more))},
        compiler_params=pltpu.CompilerParams(vmem_limit_bytes=6 * MIB),
        cost_estimate=cost(3.8 * pairs),
        name="attend_forward",
    )(flags, queries, key_rows, value_rows, *more)


def attend_backward_kernel(flags_ref, q_ref, k_ref, v_ref, up_ref, log_ref,
                           grad_ref, sum_ref, dk_acc, dv_acc, *, block):
    length = q_ref.shape[0]
    count = length // block
    key_at = lax.broadcasted_iota(jnp.int32, (block, block), 0)
    query_at = lax.broadcasted_iota(jnp.int32, (block, block), 1)
    causal = key_at <= query_at
    head_lane = lane_of((block, 128)) // HD
    full_lane = lane_of((length, 128)) // HD
    dq_sum = jnp.zeros((1, 128), F32)
    for at in reversed(range(count)):
        rows = pl.ds(at * block, block)
        reach = (at + 1) * block
        keys = pl.ds(0, reach)
        seen = causal | (flags_ref[at] > 0)
        dq = None
        for head in range(2):
            q_head = jnp.where(head_lane == head, q_ref[rows, :], jnp.zeros((block, 128), BF16))
            up_head = jnp.where(head_lane == head, up_ref[rows, :], jnp.zeros((block, 128), BF16))
            logs = log_ref[0, pl.ds(head, 1), rows]
            scores = dot_nt(k_ref[keys, :], q_head)
            last = jnp.where(seen, scores[reach - block :], MASKED)
            scores = last if at == 0 else jnp.concatenate([scores[: reach - block], last], 0)
            probs = jnp.exp(scores - logs)
            along = dot_nt(v_ref[keys, :], up_head)
            inner = jnp.sum(probs * along, axis=0, keepdims=True)
            low_grad = (probs * (along - inner)).astype(BF16)
            dv = dot_nn(probs.astype(BF16), up_head)
            dk = dot_nn(low_grad, q_head)
            if at == count - 1 and head == 0:
                dv_acc[keys, :] = dv
                dk_acc[keys, :] = dk
            else:
                dv_acc[keys, :] += dv
                dk_acc[keys, :] += dk
            k_head = jnp.where(full_lane[:reach] == head, k_ref[keys, :], jnp.zeros((reach, 128), BF16))
            part = dot_tn(low_grad, k_head)
            dq = part if dq is None else dq + part
        low_dq = (dq * HD ** (-0.5)).astype(BF16)
        grad_ref[0, rows, :] = low_dq
        dq_sum = dq_sum + column_sum(low_dq.astype(F32))
    grad_ref[1] = dk_acc[...].astype(BF16)
    low_dv = dv_acc[...].astype(BF16)
    grad_ref[2] = low_dv
    sum_ref[...] = jnp.zeros_like(sum_ref)
    sum_ref[0:1, :] = dq_sum
    sum_ref[1:2, :] = column_sum(low_dv.astype(F32))


def attend_backward(flags, queries, key_rows, value_rows, upstream, log_sums, first, pairs):
    length = queries.shape[0]
    tile = pl.BlockSpec((length, 128), lambda h, f: (0, h + first))
    return pl.pallas_call(
        functools.partial(attend_backward_kernel, block=length // 4),
        grid_spec=pltpu.PrefetchScalarGridSpec(
            num_scalar_prefetch=1, grid=(pairs,),
            in_specs=[tile, tile, tile, tile,
                      pl.BlockSpec((1, 8, length), lambda h, f: (h + first, 0, 0))],
            out_specs=[pl.BlockSpec((3, length, 128), lambda h, f: (0, 0, h)),
                       pl.BlockSpec((8, 128), lambda h, f: (0, h))],
            scratch_shapes=[pltpu.VMEM((length, 128), F32), pltpu.VMEM((length, 128), F32)]),
        out_shape=[jax.ShapeDtypeStruct((3, length, pairs * 128), BF16),
                   jax.ShapeDtypeStruct((8, pairs * 128), F32)],
        compiler_params=pltpu.CompilerParams(vmem_limit_bytes=9 * MIB),
        cost_estimate=cost(1 + 6 * pairs),
        name="attend_backward",
    )(flags, queries, key_rows, value_rows, upstream, log_sums)


def unpack_kernel(place_ref, rows_ref, *refs):
    own_ref, send_ref = refs[-2:]
    packed = rows_ref[...]
    packed = packed.reshape(packed.shape[0] * 2, packed.shape[2])
    shape = (packed.shape[0], D)
    row = lax.broadcasted_iota(jnp.int32, shape, 0)
    column = lax.broadcasted_iota(jnp.int32, shape, 1)
    pick = lambda seq: dot_tn(packed, jnp.where(row == 2 * column + seq, 1.0, 0.0).astype(BF16)).astype(BF16)
    count = own_ref.shape[0]
    send_ref[pl.ds(0, count), :] = pick(1 - place_ref[0])
    if len(refs) > 2:
        send_ref[pl.ds(count, refs[0].shape[0]), :] = refs[0][...]
    own_ref[...] = pick(place_ref[0])


def unpack_rows(place, rows, *extra):
    packed = rows.transpose(2, 0, 1)
    count = rows.shape[1]
    counts = [count, count + sum(value.shape[0] for value in extra)]
    fixed = lambda value: pl.BlockSpec(value.shape, lambda i, s: (0,) * len(value.shape))
    return pl.pallas_call(
        unpack_kernel,
        grid_spec=pltpu.PrefetchScalarGridSpec(
            num_scalar_prefetch=1, grid=(1,),
            in_specs=[fixed(packed)] + [fixed(value) for value in extra],
            out_specs=[pl.BlockSpec((n, D), lambda i, s: (0, 0)) for n in counts]),
        out_shape=[jax.ShapeDtypeStruct((n, D), BF16) for n in counts],
        compiler_params=pltpu.CompilerParams(vmem_limit_bytes=6 * MIB),
        cost_estimate=cost(5),
        name="unpack_rows",
    )(place, packed, *extra)


def decompress(compact):
    total = jnp.sum(compact, axis=-1, keepdims=True)
    return jnp.where(lane_of(compact.shape) == D - 1, -total, compact)


def crms_back(normal, factor, gain, grad):
    scaled = gain * grad
    du = factor * (scaled - normal * jnp.mean(scaled * normal, axis=-1, keepdims=True))
    lane = lane_of(du.shape)
    last = jnp.sum(jnp.where(lane == D - 1, du, 0.0), axis=-1, keepdims=True)
    return jnp.where(lane == D - 1, 0.0, du - last)


def crms_normal(compact):
    full = decompress(compact)
    factor = lax.rsqrt(jnp.mean(full * full, axis=-1, keepdims=True) + EPSILON)
    return full * factor, factor


def project_kernel(place_ref, own_ref, other_ref, gain_ref, bias_ref, w_own, w_quarter,
                   normed_ref, q_ref, k_ref, v_ref, weight, sems, *, steps):
    at = pl.program_id(0)
    quarter = D // 4
    half = w_own.shape[2]

    def copies():
        out = [pltpu.make_async_copy(w_own, weight.at[:, :, pl.ds(0, half)], sems.at[0])]
        for rel in range(4):
            place = pl.multiple_of((place_ref[1] ^ rel) * quarter, quarter)
            out.append(pltpu.make_async_copy(
                w_quarter[rel], weight.at[:, pl.ds(place, quarter), pl.ds(half, half)],
                sems.at[rel + 1]))
        return out

    @pl.when(at == 0)
    def _():
        for copy in copies():
            copy.start()

    compact = jnp.where(at < steps // 2, own_ref[...], other_ref[...]).astype(F32)
    normal, _ = crms_normal(compact)
    normed = (normal * gain_ref[...]).astype(BF16)
    normed_ref[...] = normed

    @pl.when(at == 0)
    def _():
        for copy in copies():
            copy.wait()

    q_ref[...] = ((dot_nn(normed, weight[0]) + bias_ref[0:1, :]).astype(BF16).astype(F32)
                  * HD ** (-0.5)).astype(BF16)
    k_ref[...] = dot_nn(normed, weight[1]).astype(BF16)
    v_ref[...] = (dot_nn(normed, weight[2]) + bias_ref[1:2, :]).astype(BF16)


def row_maps(steps):
    half = steps // 2
    own = lambda i, s: (jnp.minimum(i, half - 1), 0)
    other = lambda i, s: (jnp.maximum(i - half, 0), 0)
    whole = lambda i, s: (jnp.where(i < half, s[0] * half + i, (1 - s[0]) * half + i - half), 0)
    return own, other, whole


ANY = pl.BlockSpec(memory_space=pl.ANY)


def project(place, own, other, gain, bias, w_own, w_quarter, steps=4):
    length = own.shape[0] * 2
    block = length // steps
    own_map, other_map, whole_map = row_maps(steps)
    fixed = lambda i, s: (0, 0)
    wide = pl.BlockSpec((block, D), whole_map)
    out = jax.ShapeDtypeStruct((length, D), BF16)

    def body(place_ref, own_ref, other_ref, gain_ref, bias_ref, w_own, a, b, c, d, *rest):
        project_kernel(place_ref, own_ref, other_ref, gain_ref, bias_ref, w_own, (a, b, c, d),
                       *rest, steps=steps)

    return pl.pallas_call(
        body,
        grid_spec=pltpu.PrefetchScalarGridSpec(
            num_scalar_prefetch=1, grid=(steps,),
            in_specs=[pl.BlockSpec((block, D), own_map), pl.BlockSpec((block, D), other_map),
                      pl.BlockSpec((1, D), fixed), pl.BlockSpec((2, D), fixed)] + [ANY] * 5,
            out_specs=[wide] * 4,
            scratch_shapes=[pltpu.VMEM((3, D, D), BF16), pltpu.SemaphoreType.DMA((5,))]),
        out_shape=[out] * 4,
        compiler_params=pltpu.CompilerParams(vmem_limit_bytes=11 * MIB),
        cost_estimate=cost(10),
        name="norm_project",
    )(place, own, other, gain, bias, w_own, *w_quarter)


SQRT_2_PI = 0.7978845608028654


def gelu_pair(v):
    square = v * v
    inner = v * (SQRT_2_PI + (SQRT_2_PI * 0.044715) * square)
    tanh = jnp.tanh(inner)
    cdf = 0.5 + 0.5 * tanh
    slope = SQRT_2_PI + (3 * SQRT_2_PI * 0.044715) * square
    back = cdf + (0.5 * v) * (1.0 - tanh * tanh) * slope
    return v * cdf, back


def middle_kernel(place_ref, att_ref, res_own, res_other, cot_own, cot_other, gain_ref, end_ref,
                  fcb_ref, weights, two_ref, active_ref, hidden_ref, own_out, send_first, send_second,
                  mid_ref, branch_ref, upgrad_ref, sums_ref, own_sums, other_sums,
                  out_w, fc_w, proj_w, sems, *, steps, chunk):
    at = pl.program_id(0)
    hid = fc_w.shape[1]
    half = hid // 2
    o_own, f_own, p_own, quarters, proj_quarters = weights

    def copies(which):
        if which == 0:
            own, target = o_own, out_w.at[pl.ds(0, D // 2), :]
        elif which == 1:
            own, target = f_own, fc_w.at[:, pl.ds(0, half)]
        else:
            own, target = p_own, proj_w.at[pl.ds(0, half), :]
        out = [pltpu.make_async_copy(own, target, sems.at[which, 0])]
        for rel in range(4):
            source = proj_quarters[rel] if which == 2 else quarters[rel]
            to = place_ref[2 if which == 2 else 1] ^ rel
            if which == 0:
                moves = [(0, D // 8, out_w, D // 2 + to * (D // 8), None)]
            elif which == 1:
                moves = [(D // 8 + n * (D // 4), D // 4, fc_w, to * (D // 4), half + n * D)
                         for n in range(half // D)]
            else:
                moves = [(0, half // 4, proj_w, half + to * (half // 4), None)]
            for n, (start, rows, into, row, col) in enumerate(moves):
                spot = pl.ds(pl.multiple_of(row, rows), rows)
                out.append(pltpu.make_async_copy(
                    source.at[pl.ds(start, rows), :],
                    into.at[spot, :] if col is None else into.at[spot, pl.ds(col, D)],
                    sems.at[which, 1 + 2 * rel + n]))
        return out

    @pl.when(at == 0)
    def _():
        for which in range(3):
            for copy in copies(which):
                copy.start()
        for ref in (sums_ref, own_sums, other_sums):
            ref[...] = jnp.zeros_like(ref)
        for copy in copies(0):
            copy.wait()

    mine = at < steps // 2
    compact = jnp.where(mine, res_own[...], res_other[...]).astype(F32)
    cot_low = jnp.where(mine, cot_own[...], cot_other[...])
    middle = compact + dot_nn(att_ref[...], out_w[...]) + end_ref[0:1, :]
    normal, factor = crms_normal(middle)
    gain = gain_ref[...]
    two = (normal * gain).astype(BF16)
    two_ref[...] = two

    @pl.when(at == 0)
    def _():
        for which in (1, 2):
            for copy in copies(which):
                copy.wait()

    mlp = jnp.zeros((two.shape[0], D), F32)
    two_grad = jnp.zeros((two.shape[0], D), F32)
    for start in range(0, hid, chunk):
        cols = pl.ds(start, chunk)
        pre = dot_nn(two, fc_w[:, cols]) + fcb_ref[0:1, cols]
        act, slope = gelu_pair(pre)
        act = act.astype(BF16)
        active_ref[:, cols] = act
        mlp = mlp + dot_nn(act, proj_w[cols, :])
        hidden = (dot_nt(cot_low, proj_w[cols, :]) * slope).astype(BF16)
        hidden_ref[:, cols] = hidden
        to = own_sums if start < half else other_sums
        to[0:1, pl.ds(start % half, chunk)] += column_sum(hidden.astype(F32))
        two_grad = two_grad + dot_nt(hidden, fc_w[:, cols])
    block_out = (middle + mlp + end_ref[1:2, :]).astype(BF16)

    @pl.when(mine)
    def _():
        own_out[...] = block_out

    @pl.when(at == steps // 2)
    def _():
        send_first[...] = block_out

    @pl.when(at == steps // 2 + 1)
    def _():
        send_second[...] = block_out

    cot = cot_low.astype(F32)
    mid_grad = cot + crms_back(normal, factor, gain, two_grad)
    mid_ref[...] = mid_grad
    branch = mid_grad.astype(BF16)
    branch_ref[...] = branch
    upgrad_ref[...] = dot_nt(branch, out_w[...]).astype(BF16)
    sums_ref[0:1, :] += column_sum(two_grad * normal)
    sums_ref[1:2, :] += column_sum(branch.astype(F32))
    sums_ref[2:3, :] += column_sum(cot)


def middle_stage(place, att, res_own, res_other, cot_own, cot_other, gain, end_bias, fc_bias, weights,
                 steps=4, chunk=768):
    length = att.shape[0]
    hid = fc_bias.shape[1]
    block = length // steps
    own_map, other_map, whole_map = row_maps(steps)
    fixed = lambda i, s: (0, 0)
    flat = [*weights[:3], *weights[3], *weights[4]]
    spec = lambda w, m: pl.BlockSpec((block, w), m)

    def body(place_ref, *refs):
        ins, rest = refs[:8], refs[8:]
        w, rest = rest[:11], rest[11:]
        packed = (*w[:3], w[3:7], w[7:])
        middle_kernel(place_ref, *ins, packed, *rest, steps=steps, chunk=chunk)

    sd = jax.ShapeDtypeStruct
    return pl.pallas_call(
        body,
        grid_spec=pltpu.PrefetchScalarGridSpec(
            num_scalar_prefetch=1, grid=(steps,),
            in_specs=[spec(D, whole_map), spec(D, own_map), spec(D, other_map), spec(D, own_map),
                      spec(D, other_map), pl.BlockSpec((1, D), fixed), pl.BlockSpec((2, D), fixed),
                      pl.BlockSpec((1, hid), fixed)] + [ANY] * 11,
            out_specs=[spec(D, whole_map), spec(hid, whole_map), spec(hid, whole_map),
                       spec(D, own_map), spec(D, fixed), spec(D, fixed),
                       spec(D, whole_map), spec(D, whole_map), spec(D, whole_map),
                       pl.BlockSpec((8, D), fixed), pl.BlockSpec((8, hid // 2), fixed),
                       pl.BlockSpec((8, hid // 2), fixed)],
            scratch_shapes=[pltpu.VMEM((D, D), BF16), pltpu.VMEM((D, hid), BF16),
                            pltpu.VMEM((hid, D), BF16), pltpu.SemaphoreType.DMA((3, 9))]),
        out_shape=[sd((length, D), BF16), sd((length, hid), BF16), sd((length, hid), BF16),
                   sd((length // 2, D), BF16), sd((block, D), BF16), sd((block, D), BF16),
                   sd((length, D), F32), sd((length, D), BF16), sd((length, D), BF16),
                   sd((8, D), F32), sd((8, hid // 2), F32), sd((8, hid // 2), F32)],
        compiler_params=pltpu.CompilerParams(vmem_limit_bytes=36 * MIB),
        cost_estimate=cost(38),
        name="middle_stage",
    )(place, att, res_own, res_other, cot_own, cot_other, gain, end_bias, fc_bias, *flat)


def fc_grad_kernel(place_ref, left_ref, right_ref, keep_ref, send_ref, *, rows):
    flip = (place_ref[1] & 1) == 1
    both = dot_tn_halves(left_ref, right_ref).astype(BF16)
    for pair in range(2):
        to = pair ^ (place_ref[1] >> 1)
        low, high = both[2 * pair * rows : (2 * pair + 1) * rows], both[(2 * pair + 1) * rows : (2 * pair + 2) * rows]
        keep_ref[0, to] = jnp.where(flip, high, low)
        send_ref[0, to] = jnp.where(flip, low, high)


def fc_grad(place, left, right, chunk=768):
    length, width = left.shape
    rows = width // 4
    half = right.shape[1] // 2
    parts = half // chunk
    out = jax.ShapeDtypeStruct((2, 2, rows, half), BF16)
    out_spec = pl.BlockSpec((1, 2, rows, chunk), lambda n, s: (n // parts, 0, 0, n % parts))
    return pl.pallas_call(
        functools.partial(fc_grad_kernel, rows=rows),
        grid_spec=pltpu.PrefetchScalarGridSpec(
            num_scalar_prefetch=1, grid=(2 * parts,),
            in_specs=[pl.BlockSpec((length, width), lambda n, s: (0, 0)),
                      pl.BlockSpec((length, chunk), lambda n, s: (0, n))],
            out_specs=[out_spec, out_spec]),
        out_shape=[out, out],
        compiler_params=pltpu.CompilerParams(vmem_limit_bytes=52 * MIB),
        cost_estimate=cost(12),
        name="fc_grad",
    )(place, left, right)


def qkv_grad_kernel(place_ref, left_ref, *refs, rows, parts, pieces):
    right_refs, weight_refs = refs[:parts], refs[parts : parts + pieces]
    keep_ref, send_ref, sum_ref, total = refs[parts + pieces :]
    flip = (place_ref[1] & 1) == 1
    half = left_ref.shape[0] // 2
    width = sum(ref.shape[2] for ref in right_refs)
    both = None
    for n in range(2):
        part = pl.ds(n * half, half)
        right = jnp.concatenate([ref[c, part, :] for c in range(3) for ref in right_refs], axis=1)
        here = dot_tn(left_ref[part, :], right)
        both = here if both is None else both + here
    low_both = both.astype(BF16)
    for pair in range(2):
        to = pair ^ (place_ref[1] >> 1)
        for c in range(3):
            cols = slice(c * width, (c + 1) * width)
            low = low_both[2 * pair * rows : (2 * pair + 1) * rows, cols]
            high = low_both[(2 * pair + 1) * rows : (2 * pair + 2) * rows, cols]
            keep_ref[to, c] = jnp.where(flip, high, low)
            send_ref[to, c] = jnp.where(flip, low, high)
    sum_ref[...] = jnp.zeros_like(sum_ref)
    if pieces > 1:
        total[...] = both
    span = both.shape[0] // pieces
    for n in range(pieces):
        at = pl.multiple_of((place_ref[1] ^ n) * span, span) if pieces > 1 else 0
        folded = jnp.zeros((span, 128), F32)
        for c in range(3):
            here = total[pl.ds(at, span), pl.ds(c * width, width)] if pieces > 1 else both[:, c * width : (c + 1) * width]
            product = here * weight_refs[n][c].astype(F32)
            for k in range(0, width, 128):
                folded = folded + product[:, k : k + 128]
        total[pl.ds(at, span), pl.ds(0, 128)] = folded
    sum_ref[0:1, :] = column_sum(jnp.transpose(total[:, 0:128]))


def qkv_grad(place, left, rights, weights, col_at=0):
    length, width = left.shape
    rows = width // 4
    cols = sum(value.shape[2] for value in rights)
    out = jax.ShapeDtypeStruct((2, 3, rows, cols), BF16)
    whole = lambda value: pl.BlockSpec(value.shape, lambda i, s: (0,) * len(value.shape))
    sums = jax.ShapeDtypeStruct((8, width), F32)
    return pl.pallas_call(
        functools.partial(qkv_grad_kernel, rows=rows, parts=len(rights), pieces=len(weights)),
        grid_spec=pltpu.PrefetchScalarGridSpec(
            num_scalar_prefetch=1, grid=(1,),
            in_specs=[whole(value) for value in (left, *rights)]
            + [pl.BlockSpec((3, value.shape[1], cols), lambda i, s: (0, 0, col_at)) for value in weights],
            out_specs=[whole(out), whole(out), whole(sums)],
            scratch_shapes=[pltpu.VMEM((width, 3 * cols), F32)]),
        out_shape=[out, out, sums],
        compiler_params=pltpu.CompilerParams(vmem_limit_bytes=17 * MIB),
        cost_estimate=cost(6.5),
        name="qkv_grad",
    )(place, left, *rights, *weights)


def proj_grad_kernel(place_ref, own_act, other_act, own_cot, other_cot, att_ref, branch_ref, keep_ref, send_ref, rest,
                     *, rows):
    side, pair = pl.program_id(0), pl.program_id(1)
    flip = (place_ref[1] & 1) == 1
    out_rows = att_ref.shape[1] // 8

    @pl.when((side == 0) & (pair == 0))
    def _():
        rest[...] = dot_tn_halves(att_ref, branch_ref).astype(BF16)

    both = (dot_tn(own_act[...], own_cot[...]) + dot_tn(other_act[...], other_cot[...])).astype(BF16)
    base = pl.multiple_of((side * 4 + pair * 2) * out_rows, out_rows)
    more_low, more_high = rest[pl.ds(base, out_rows), :], rest[pl.ds(base + out_rows, out_rows), :]
    low, high = both[:rows], both[rows:]
    keep_ref[0, 0, pl.ds(0, rows), :] = jnp.where(flip, high, low)
    send_ref[0, 0, pl.ds(0, rows), :] = jnp.where(flip, low, high)
    keep_ref[0, 0, pl.ds(rows, out_rows), :] = jnp.where(flip, more_high, more_low)
    send_ref[0, 0, pl.ds(rows, out_rows), :] = jnp.where(flip, more_low, more_high)


def proj_grad(place, active, cot_own, cot_other, attended, branch):
    length, width = active.shape
    rows = width // 8
    out_rows = attended.shape[1] // 8
    out = jax.ShapeDtypeStruct((2, 2, rows + out_rows, D), BF16)
    out_spec = pl.BlockSpec((1, 1, rows + out_rows, D), lambda n, j, s: (j ^ (s[1] >> 1), n, 0, 0))
    fixed = lambda count: pl.BlockSpec((count, D), lambda n, j, s: (0, 0))
    return pl.pallas_call(
        functools.partial(proj_grad_kernel, rows=rows),
        grid_spec=pltpu.PrefetchScalarGridSpec(
            num_scalar_prefetch=1, grid=(2, 2),
            in_specs=[pl.BlockSpec((length // 2, 2 * rows), lambda n, j, s: (s[0], n * 2 + j)),
                      pl.BlockSpec((length // 2, 2 * rows), lambda n, j, s: (1 - s[0], n * 2 + j)),
                      fixed(length // 2), fixed(length // 2), fixed(length), fixed(length)],
            out_specs=[out_spec, out_spec],
            scratch_shapes=[pltpu.VMEM((attended.shape[1], D), BF16)]),
        out_shape=[out, out],
        compiler_params=pltpu.CompilerParams(vmem_limit_bytes=40 * MIB),
        cost_estimate=cost(13),
        name="proj_grad",
    )(place, active, active, cot_own, cot_other, attended, branch)


def input_grad_kernel(place_ref, own_grads, other_grads, res_own, res_other, mid_ref, gain_ref, w_own, w_quarter,
                      own_out, send_out, weight, sems, *, steps):
    at = pl.program_id(0)
    quarter = D // 4
    half = w_own.shape[2]

    def copies():
        out = []
        for c in range(3):
            out.append(pltpu.make_async_copy(
                w_own.at[c], weight.at[:, pl.ds(c * half, half)], sems.at[c, 0]))
            for rel in range(4):
                place = pl.multiple_of((place_ref[1] ^ rel) * quarter, quarter)
                out.append(pltpu.make_async_copy(
                    w_quarter[rel].at[c], weight.at[pl.ds(place, quarter), pl.ds((3 + c) * half, half)],
                    sems.at[c, rel + 1]))
        return out

    @pl.when(at == 0)
    def _():
        for copy in copies():
            copy.start()

    mine = at < steps // 2
    compact = jnp.where(mine, res_own[...], res_other[...]).astype(F32)
    normal, factor = crms_normal(compact)

    @pl.when(at == 0)
    def _():
        for copy in copies():
            copy.wait()

    left = jnp.concatenate([ref[c] for part in (own_grads, other_grads) for c in range(3) for ref in part], axis=1)
    grad = dot_nt(left, weight[...])
    result = (mid_ref[...] + crms_back(normal, factor, gain_ref[...], grad)).astype(BF16)

    @pl.when(mine)
    def _():
        own_out[...] = result

    @pl.when(jnp.logical_not(mine))
    def _():
        send_out[...] = result


def input_grad(place, own_grads, other_grads, res_own, res_other, mid, gain, w_own, w_quarter, steps=4):
    length = mid.shape[0]
    block = length // steps
    own_map, other_map, whole_map = row_maps(steps)
    fixed = lambda i, s: (0, 0)
    mine, many = len(own_grads), len(own_grads) + len(other_grads)
    grad_spec = lambda value: pl.BlockSpec((3, block, value.shape[2]), lambda i, s: (0, whole_map(i, s)[0], 0))

    def body(place_ref, *refs):
        rest = refs[many:]
        input_grad_kernel(place_ref, refs[:mine], refs[mine:many], *rest[:5], rest[5:9], *rest[9:], steps=steps)

    sd = jax.ShapeDtypeStruct
    return pl.pallas_call(
        body,
        grid_spec=pltpu.PrefetchScalarGridSpec(
            num_scalar_prefetch=1, grid=(steps,),
            in_specs=[grad_spec(value) for value in (*own_grads, *other_grads)] + [pl.BlockSpec((block, D), own_map), pl.BlockSpec((block, D), other_map),
                      pl.BlockSpec((block, D), whole_map), pl.BlockSpec((1, D), fixed)] + [ANY] * 5,
            out_specs=[pl.BlockSpec((block, D), own_map), pl.BlockSpec((block, D), other_map)],
            scratch_shapes=[pltpu.VMEM((D, 3 * D), BF16), pltpu.SemaphoreType.DMA((3, 5))]),
        out_shape=[sd((length // 2, D), BF16), sd((length // 2, D), BF16)],
        compiler_params=pltpu.CompilerParams(vmem_limit_bytes=14 * MIB),
        cost_estimate=cost(9),
        name="input_grad",
    )(place, *own_grads, *other_grads, res_own, res_other, mid, gain, w_own, *w_quarter)


def pack_kernel(place_ref, own_ref, first_ref, second_ref, out_ref, *, steps):
    straight = place_ref[0] == 0
    own = jnp.transpose(own_ref[...].astype(F32))
    other = jnp.where(pl.program_id(0) < steps // 2, first_ref[...], second_ref[...])
    other = jnp.transpose(other.astype(F32))
    count = out_ref.shape[0]
    both = [jnp.where(straight, own, other)[:count], jnp.where(straight, other, own)[:count]]
    out_ref[...] = jnp.stack(both, 1).astype(BF16)


def pack_rows(place, own, first, second):
    positions = own.shape[0]
    steps = positions // 128
    own_map, other_map, _ = row_maps(steps)
    if second.shape[0] == positions:
        other_map = lambda i, s: (jnp.maximum(i, steps // 2), 0)
    packed = pl.pallas_call(
        functools.partial(pack_kernel, steps=steps),
        grid_spec=pltpu.PrefetchScalarGridSpec(
            num_scalar_prefetch=1, grid=(steps,),
            in_specs=[pl.BlockSpec((128, D), lambda i, s: (i, 0)), pl.BlockSpec((128, D), own_map),
                      pl.BlockSpec((128, D), other_map)],
            out_specs=pl.BlockSpec((D - 1, 2, 128), lambda i, s: (0, 0, i))),
        out_shape=jax.ShapeDtypeStruct((D - 1, 2, positions), BF16),
        compiler_params=pltpu.CompilerParams(vmem_limit_bytes=4 * MIB),
        cost_estimate=cost(0.1),
        name="pack_rows",
    )(place, own, first, second)
    return packed.transpose(1, 2, 0)


def swap(value, axis, bit, size):
    return lax.ppermute(value, axis, [(n, n ^ bit) for n in range(size)])


def meet(*values):
    return lax.optimization_barrier(values)


def add_low(*values):
    total = values[0].astype(F32)
    for value in values[1:]:
        total = total + value.astype(F32)
    return total.astype(BF16)


def chain_in(value):
    return lax.ppermute(value, "group", [(0, 1), (3, 2)])


def chain_across(value):
    return lax.ppermute(value, "group", [(1, 2), (2, 1)])


def chain_out(value):
    return lax.ppermute(value, "group", [(1, 0), (2, 3)])


def on_device(sizes, residual_in, piece_ids, norm_gains, qkv_weight, qv_bias, out_weight, fc_weight,
              fc_bias, proj_weight, out_biases, cotangent):
    n_dp, n_group, n_tensor = sizes["dp"], sizes["group"], sizes["tensor"]
    dp_at = lax.axis_index("dp")
    group_at = lax.axis_index("group")
    tensor_at = lax.axis_index("tensor")
    quarter_at = dp_at & 3
    proj_at = (dp_at & 1) | ((group_at & 1) << 1)
    place = jnp.stack([tensor_at, quarter_at, proj_at]).astype(jnp.int32)
    pad = ((0, 0), (0, 1))
    half = qv_bias.shape[1]
    hid = fc_bias.shape[0]
    pairs = half // 128
    y_swap = lambda value: swap(value, "tensor", 1, n_tensor)
    x_swap = lambda value: swap(value, "dp", 2, n_dp)
    c_swap = lambda value: swap(value, "dp", 1, n_dp)
    z_swap = lambda value: swap(value, "group", 1, n_group)

    def piece_of(shard, dim, at):
        rows = shard.shape[dim] // 4
        return lax.dynamic_slice_in_dim(shard, at * rows, rows, dim)

    qkv_piece = piece_of(qkv_weight, 1, quarter_at)
    qkv_y = y_swap(qkv_piece)
    bias_rows = jnp.concatenate([fc_bias.reshape(-1, D), qv_bias.reshape(1, D), jnp.zeros((13, D), BF16)], 0)
    res_own, res_send = unpack_rows(after(place, qkv_piece), residual_in, bias_rows)
    res_other = y_swap(res_send)
    qkv_y, res_own, out_gated, fc_gated, proj_gated = meet(qkv_y, res_own, out_weight, fc_weight, proj_weight)
    qkv_x = x_swap(qkv_y)
    qkv_c = c_swap(qkv_y)
    fc_piece = piece_of(fc_gated, 0, quarter_at)
    mix = jnp.concatenate([jnp.pad(piece_of(out_gated, 0, quarter_at), pad)]
                          + [fc_piece[:, n : n + D] for n in range(0, hid, D)], 0)
    proj_piece = jnp.pad(piece_of(proj_gated, 0, proj_at), pad)
    qkv_c, mix, proj_piece = meet(qkv_c, mix, proj_piece)
    mix_y, proj_y = y_swap(mix), y_swap(proj_piece)
    cot_own, cot_send = unpack_rows(after(place, mix, proj_piece), cotangent)
    out_own = jnp.pad(out_gated, pad)
    proj_own = jnp.pad(proj_gated, pad)
    qkv_x, res_other, out_own, proj_own, cot_send = meet(qkv_x, res_other, out_own, proj_own, cot_send)
    qkv_cx = c_swap(qkv_x)
    qkv_others = (qkv_y, qkv_c, qkv_x, qkv_cx)

    gains = norm_gains.astype(F32)
    end_biases = jnp.pad(out_biases, pad).astype(F32)
    count = residual_in.shape[1]
    bias_other = res_other[count : count + 8].astype(F32)
    fc_rows = hid // D
    qv_full = jnp.concatenate([qv_bias.astype(F32), bias_other[fc_rows].reshape(2, half)], axis=1)
    fc_full = jnp.concatenate([fc_bias.astype(F32).reshape(1, -1), bias_other[:fc_rows].reshape(1, -1)], axis=1)
    length = piece_ids.shape[1]
    flags = (lax.dynamic_index_in_dim(piece_ids, tensor_at, 0, keepdims=False)[:: length // 4] >= 0)
    flags = flags.astype(jnp.int32)

    normed_one, queries, key_rows, value_rows = project(
        place, res_own, res_other, gains[0:1], qv_full, qkv_weight, qkv_others)
    queries, cot_send = meet(queries, cot_send)
    cot_other = y_swap(cot_send)
    attended = attend_forward(flags, queries, key_rows, value_rows, 0, pairs)
    *attended, queries, mix_y, proj_y = meet(*attended, queries, mix_y, proj_y)
    mix_x, mix_c = x_swap(mix_y), c_swap(mix_y)
    proj_x, proj_c = z_swap(proj_y), c_swap(proj_y)
    attended = attend_forward(flags, queries, key_rows, value_rows, pairs, pairs, attended)
    attended, log_sums, mix_x, proj_x, cot_other = meet(*attended, mix_x, proj_x, cot_other)
    mix_others = (mix_y, mix_c, mix_x, c_swap(mix_x))
    proj_others = (proj_y, proj_c, proj_x, c_swap(proj_x))

    (normed_two, active, hidden_grad, out_mine, *out_send, middle_grad, branch_grad, attended_grad,
     middle_sums, own_sums, other_sums) = middle_stage(
        place, attended, res_own, res_other, cot_own, cot_other, gains[1:2], end_biases, fc_full,
        (out_own, fc_weight, proj_own, mix_others, proj_others))
    backward = functools.partial(attend_backward, flags, queries, key_rows, value_rows)
    restore = functools.partial(pack_rows, place)

    def small_outputs(small):
        part, first = hid // n_dp, half // n_dp
        return (jnp.concatenate([small[0:1, :D], small[0:1, D : 2 * D]], 0),
                lax.dynamic_slice(small, (0, 2 * D + hid + dp_at * first), (2, first)),
                lax.dynamic_slice(small, (0, 2 * D + dp_at * part), (1, part)).reshape(part),
                small[1:3, D : 2 * D - 1])

    if n_dp == 4 and n_group == 4:
        out_got = [y_swap(value) for value in out_send]
        proj_k, proj_s = proj_grad(after(place, middle_sums), active, cot_own, cot_other, attended, branch_grad)
        proj_k, proj_s, out_got[0] = meet(proj_k, proj_s, out_got[0])
        proj_c = c_swap(proj_s)
        fc_k, fc_s = fc_grad(after(place, proj_k), normed_two, hidden_grad)
        fc_k, fc_s, proj_k, proj_c, *out_got = meet(fc_k, fc_s, proj_k, proj_c, *out_got)
        fc_c = c_swap(fc_s)
        proj_fo = add_low(proj_k[1, 1], proj_c[1, 1])
        proj_xo = x_swap(proj_fo)
        proj_fm = add_low(proj_k[1, 0], after(proj_c, proj_fo)[1, 0])
        proj_xm = x_swap(proj_fm)
        fc_k, fc_c, proj_fo, proj_fm = meet(fc_k, fc_c, proj_fo, proj_fm)
        fc_away = add_low(fc_k[1], fc_c[1])
        fc_y = y_swap(fc_away)
        first, first_sums = backward(after(attended_grad, fc_away), log_sums, pairs, pairs)
        first, first_sums, proj_k, proj_c, proj_xo = meet(first, first_sums, proj_k, proj_c, proj_xo)
        proj_r = add_low(proj_k[0, 1], proj_c[0, 1], proj_xo)
        proj_y = y_swap(proj_r)
        qo_k, qo_s, qo_sum = qkv_grad(after(place, proj_r), normed_one, [first], qkv_others)
        qo_k, qo_s, fc_k, fc_c, fc_y = meet(qo_k, qo_s, fc_k, fc_c, fc_y)
        qo_c = c_swap(qo_s)
        fc_far = add_low(fc_k[0, 1], fc_c[0, 1], fc_y[1])
        fc_x = x_swap(fc_far)
        own_a, sums_a = backward(after(attended_grad, fc_far), log_sums, 0, pairs - 1)
        own_a, sums_a, proj_y, proj_xm, proj_k, proj_c = meet(own_a, sums_a, proj_y, proj_xm, proj_k, proj_c)
        proj_shard = add_low(proj_k[0, 0], proj_c[0, 0], proj_xm, proj_y)
        proj_z = chain_in(proj_shard)
        proj_shard, fc_x, qo_k, qo_c = meet(proj_shard, fc_x, qo_k, qo_c)
        fc_shard = add_low(fc_k[0, 0], fc_c[0, 0], fc_y[0], fc_x)
        fc_z = chain_in(fc_shard)
        qo_f = add_low(qo_k[1], qo_c[1])
        qo_x = x_swap(qo_f)
        own_b, sums_b = backward(after(attended_grad, qo_f, proj_shard, fc_shard), log_sums, pairs - 1, 1)
        qm_k, qm_s, qm_sum = qkv_grad(after(place, own_b), normed_one, [own_a, own_b], [qkv_weight])
        qm_k, qm_s, qm_sum, qo_k, qo_c, qo_x = meet(qm_k, qm_s, qm_sum, qo_k, qo_c, qo_x)
        qm_c = c_swap(qm_s)
        in_sums = (qm_sum + qo_sum) / gains[0:1]
        small = jnp.concatenate(
            [value[:4] for value in (in_sums, middle_sums, own_sums, other_sums, sums_a, sums_b, first_sums)], 1)
        small_c = c_swap(small)
        qo_r = add_low(qo_k[0], qo_c[0], qo_x)
        qo_y = y_swap(qo_r)
        qm_k, qm_c, qo_r, small, small_c = meet(qm_k, qm_c, qo_r, small, small_c)
        small = small + small_c
        small_x = x_swap(small)
        qm_f = add_low(after(qm_k, small)[1], qm_c[1])
        qm_x = x_swap(qm_f)
        qm_f, proj_shard, proj_z = meet(qm_f, proj_shard, proj_z)
        proj_shard = add_low(proj_shard, proj_z)
        proj_z = chain_across(proj_shard)
        block_out = restore(after(out_mine, proj_shard), *out_got)
        block_out, small, small_x = meet(block_out, small, small_x)
        small = small + small_x
        split = 2 * D + hid
        mine = jnp.concatenate([small[:, :split], small[:, split + hid : split + hid + half]], 1)
        other = jnp.concatenate([small[:, : 2 * D], small[:, split : split + hid], small[:, split + hid + half :]], 1)
        small_y = y_swap(other)
        qm_k, qm_c, qm_x, qo_y, mine, small_y = meet(qm_k, qm_c, qm_x, qo_y, mine, small_y)
        last = add_low(qm_k[0], qm_c[0], qm_x, qo_y)
        last_z = chain_in(last)
        small = mine + small_y
        small_z = chain_in(small)
        fc_shard, fc_z, proj_shard, proj_z, last, small = meet(fc_shard, fc_z, proj_shard, proj_z, last, small)
        fc_shard = add_low(fc_shard, fc_z)
        fc_z = chain_across(fc_shard)
        proj_shard = add_low(proj_shard, proj_z)
        proj_z = chain_out(proj_shard)
        in_mine, in_send = input_grad(
            after(place, last, proj_shard, fc_shard, small), [own_a, own_b], [first], res_own, res_other, middle_grad,
            gains[0:1], qkv_weight, qkv_others)
        in_mine, in_send, last, last_z, fc_shard, fc_z, small, small_z = meet(
            in_mine, in_send, last, last_z, fc_shard, fc_z, small, small_z)
        last = add_low(last, last_z)
        last_z = chain_across(last)
        small = small + small_z
        small_z = chain_across(small)
        fc_shard = add_low(after(fc_shard, last, small), fc_z)
        fc_z = chain_out(fc_shard)
        in_got = y_swap(in_send)
        middle_one = (group_at == 1) | (group_at == 2)
        small, last, fc_shard, proj_shard, proj_z = meet(small, last, fc_shard, proj_shard, proj_z)
        proj_shard = jnp.where(middle_one, proj_shard, proj_z)
        out_shard = proj_shard[hid // 4 :, : D - 1].astype(F32)
        proj_shard = proj_shard[: hid // 4, : D - 1].astype(F32)
        small, small_z, last, last_z, proj_shard, out_shard = meet(
            small, small_z, last, last_z, proj_shard, out_shard)
        last = add_low(last, last_z)
        last_z = chain_out(last)
        small = small + small_z
        small_z = chain_out(small)
        in_mine, in_got, last, small = meet(in_mine, in_got, last, small)
        in_out = restore(in_mine, in_got, in_got)
        in_out, fc_shard, fc_z = meet(in_out, fc_shard, fc_z)
        fc_shard = jnp.where(middle_one, fc_shard, fc_z).astype(F32)
        fc_shard, small, small_z = meet(fc_shard, small, small_z)
        small = small_outputs(jnp.where(middle_one, small, small_z))
        last, last_z, in_out, proj_shard, out_shard, fc_shard, *small = meet(
            last, last_z, in_out, proj_shard, out_shard, fc_shard, *small)
        qkv_shard = jnp.where(middle_one, last, last_z)
    else:
        first, first_sums = backward(attended_grad, log_sums, pairs, pairs)
        own, second_sums = backward(attended_grad, log_sums, 0, pairs)
        in_mine, in_send = input_grad(
            place, [own], [first], res_own, res_other, middle_grad, gains[0:1], qkv_weight, qkv_others)
        in_got = y_swap(in_send)
        in_out = restore(in_mine, in_got, in_got)
        block_out = restore(out_mine, *[y_swap(value) for value in out_send])
        qo_sum = qkv_grad(place, normed_one, [first], qkv_others)[2]
        qm_sum = qkv_grad(place, normed_one, [own], [qkv_weight])[2]

        def scatter(own, other):
            total = [lax.psum_scatter(value.astype(BF16), "dp", scatter_dimension=0, tiled=True)
                     for value in (own, other)]
            return lax.psum(add_low(total[0], y_swap(total[1])), "group")

        cot_rows = jnp.where(tensor_at == 0, jnp.concatenate([cot_own, cot_other]),
                             jnp.concatenate([cot_other, cot_own]))
        proj_shard = scatter(dot_tn(active[:, :hid], cot_rows), dot_tn(active[:, hid:], cot_rows))
        fc_shard = scatter(dot_tn(normed_two, hidden_grad[:, :hid]), dot_tn(normed_two, hidden_grad[:, hid:]))
        out_shard = scatter(dot_tn(attended[:, :half], branch_grad), dot_tn(attended[:, half:], branch_grad))
        proj_shard, out_shard = proj_shard[:, : D - 1].astype(F32), out_shard[:, : D - 1].astype(F32)
        fc_shard = fc_shard.astype(F32)
        qkv_shard = jnp.swapaxes(scatter(
            *[jnp.stack([dot_tn(normed_one, part[c]) for c in range(3)], 1) for part in (own, first)]), 0, 1)
        in_sums = (qm_sum + qo_sum) / gains[0:1]
        small = jnp.concatenate([in_sums, middle_sums, own_sums, second_sums], 1)
        small = small + y_swap(jnp.concatenate([in_sums, middle_sums, other_sums, first_sums], 1))
        small = small_outputs(lax.psum(small, ("dp", "group")))

    grad_gains, grad_qv_bias, grad_fc_bias, grad_out_biases = small
    return (
        block_out,
        in_out,
        grad_gains,
        qkv_shard.astype(F32),
        grad_qv_bias,
        out_shard,
        fc_shard,
        grad_fc_bias,
        proj_shard,
        grad_out_biases,
    )


def solution(mesh):
    sizes = dict(mesh.shape)
    in_specs = (
        P(("dp", "group"), "tensor", None),
        P(("dp", "group"), None),
        P(),
        P(None, None, "tensor"),
        P(None, "tensor"),
        P("tensor", None),
        P(None, "tensor"),
        P("tensor"),
        P("tensor", None),
        P(),
        P(("dp", "group"), "tensor", None),
    )
    out_specs = (
        P(("dp", "group"), "tensor", None),
        P(("dp", "group"), "tensor", None),
        P(),
        P(None, "dp", "tensor"),
        P(None, ("tensor", "dp")),
        P(("tensor", "dp"), None),
        P("dp", "tensor"),
        P(("tensor", "dp")),
        P(("tensor", "dp"), None),
        P(),
    )
    return jax.shard_map(
        functools.partial(on_device, sizes), mesh=mesh, in_specs=in_specs, out_specs=out_specs,
        check_vma=False)
```
